256 devices in a mesh: ref: 64 (over z, x, core), voc: 4 (over y).
Axes of the slice: x: 4, y: 4, z: 8, core: 2. Of those that a mesh axis runs over, the one named last changes fastest.
Arguments:
- private_logits: bfloat16 [768, 4, 128256], P('ref', None, 'voc'), may hold values from -16 to 16
- public_logits: bfloat16 [4, 4, 128256], P(None, None, ('voc', 'ref')), may hold values from -250 to 250
- noise: bfloat16 [4, 4, 128256], P(None, None, ('voc', 'ref')), may hold values from -6 to 6
- owner: int32 [768], P('ref'), may hold values from 0 to 3, as said below
- counts: int32 [4], replicated, may hold values from 1 to 192, as said below
- tokens: int32 [4, 4], replicated, may hold values from 0 to 128255
Outputs:
- logprobs: float32 [4, 4, 128256], P(None, None, ('voc', 'ref'))
- target: float32 [4, 4], replicated
The draws below stay inside these ranges and needn't reach their ends.
Inputs may be any that keep to these rules, and one draw needn't show every extreme that they name: `owner`: each of the 4 texts owns exactly 192 rows. `counts`: the count of a text is at least half of the rows that it owns, rounded up, and at most all of them; some text keeps all of its rows.
All inputs are finite; a program needn't handle non-finite values.
Results may differ from the reference program's by a relative error of at most 0.0003.
Values may be sent and summed in bfloat16 or wider, within the bound.
No kernel may reach another device: no remote copies, remote signals or barrier semaphores. Data moves between devices by JAX's collectives and lax.ppermute only.
A program may use at most 64 MiB of HBM per device.

```python
import jax
import jax.numpy as jnp
from jax import lax

V = 128256
TEXTS = 4
POS = 4
REF_DEV = 12
REFS = 768
N_REF = 64


def draw_public_logits(key, part):
    values = 3.0 * jax.random.normal(jax.random.fold_in(key, 21), (TEXTS, POS, V), jnp.float32)
    values = jnp.clip(values, -18.0, 18.0)
    return values.astype(jnp.bfloat16)


def split_rows(key):
    row_index = jnp.arange(REFS, dtype=jnp.int32)
    owner_rows = jax.random.permutation(jax.random.fold_in(key, 31), (row_index % TEXTS).astype(jnp.int32)).astype(jnp.int32)
    owned = jnp.full((TEXTS,), REFS // TEXTS, dtype=jnp.int32)
    removed = jax.random.randint(jax.random.fold_in(key, 32), (TEXTS,), 0, owned // 2 + 1, dtype=jnp.int32)
    keeper = jax.random.randint(jax.random.fold_in(key, 33), (), 0, TEXTS, dtype=jnp.int32)
    removed = jnp.where(jnp.arange(TEXTS, dtype=jnp.int32) == keeper, 0, removed).astype(jnp.int32)
    return (owner_rows, (owned - removed).astype(jnp.int32))


def draw_owner(key, part):
    return split_rows(key)[0]


def draw_counts(key, part):
    return split_rows(key)[1]


def plant(values, key, smallest, largest):
    index_at = [jax.random.randint(jax.random.fold_in(key, axis), (), 0, length) for axis, length in enumerate(values.shape)]
    main_axis = values.shape.index(max(values.shape))
    beside = index_at[:main_axis] + [(index_at[main_axis] + 1) % values.shape[main_axis]] + index_at[main_axis + 1:]
    return values.at[tuple(index_at)].set(smallest).at[tuple(beside)].set(largest)


def shard_levels(own_key, shape, cuts, low, high):
    level = 1.0
    for axis_at, shards_of in cuts:
        steps = jax.random.uniform(jax.random.fold_in(jax.random.fold_in(own_key, 6), axis_at), (shards_of,), jnp.float32, low / len(cuts), high / len(cuts))
        level = level * jnp.repeat(jnp.exp(steps), shape[axis_at] // shards_of).reshape((-1,) + (1,) * (len(shape) - 1 - axis_at))
    return level


def bell_draw(stream_key, dims, width, limit, cuts=(), held_as=jnp.bfloat16):
    entries = width * jax.random.normal(stream_key, dims, jnp.float32)
    if cuts:
        entries = entries * shard_levels(stream_key, dims, cuts, -0.22, 0.18)
    return jnp.clip(entries, -limit, limit).astype(held_as)


def setup_inputs(seed: int = 0) -> dict:
    key_list = jax.random.split(jax.random.key(seed), 7)
    return {
        "private_logits": bell_draw(key_list[0], (REFS, POS, V), 3.0, 16.0, ((0, 64), (2, 4))),
        "public_logits": draw_public_logits(jax.random.fold_in(key_list[6], 71), 0),
        "noise": bell_draw(key_list[2], (TEXTS, POS, V), 1.0, 6.0, ((2, 256),)),
        "owner": draw_owner(jax.random.fold_in(key_list[6], 71), 0),
        "counts": draw_counts(jax.random.fold_in(key_list[6], 71), 0),
        "tokens": plant(jax.random.randint(key_list[5], (TEXTS, POS), 0, V), jax.random.fold_in(key_list[5], 1), 0, V - 1).astype(jnp.int32),
    }


clip_bound = 2.0

def reference(private_logits, public_logits, noise, owner, counts, tokens):
    text_count = counts.shape[0]
    labels = jnp.arange(text_count, dtype=jnp.int32)
    chosen = (owner[:, None] == labels[None, :]).astype(jnp.int32)
    before = (jnp.cumsum(chosen, 0) - chosen).astype(jnp.int32)
    row_rank = lax.optimization_barrier(jnp.sum(before * chosen, 1)).astype(jnp.int32)
    row_limit = lax.optimization_barrier(jnp.sum(chosen * counts[None, :], 1)).astype(jnp.int32)
    select = chosen.astype(jnp.float32)
    weight = select * (row_rank < row_limit).astype(jnp.float32)[:, None]
    public_wide = public_logits.astype(jnp.float32)

    def accumulate(summed, pieces):
        private_piece, select_piece, weight_piece = pieces
        matched = jnp.einsum('rt,tpv->rpv', select_piece, public_wide, precision=lax.Precision.HIGHEST)
        clipped = jnp.clip(private_piece.astype(jnp.float32) - matched, -clip_bound, clip_bound)
        return (summed + jnp.einsum('rt,rpv->tpv', weight_piece, clipped, precision=lax.Precision.HIGHEST), None)
    grouped = (private_logits.reshape(N_REF, REF_DEV, POS, V), select.reshape(N_REF, REF_DEV, text_count), weight.reshape(N_REF, REF_DEV, text_count))
    summed, unused = lax.scan(accumulate, jnp.zeros((text_count, POS, V), jnp.float32), grouped)
    text_scale = 1.0 / (clip_bound * jnp.sqrt(counts.astype(jnp.float32)))
    combined = public_wide + summed * text_scale[:, None, None] + noise.astype(jnp.float32)
    row_peak = lax.optimization_barrier(jnp.max(combined, axis=2))
    lse = row_peak + jnp.log(lax.optimization_barrier(jnp.sum(jnp.exp(combined - row_peak[:, :, None]), axis=2)))
    logprobs = combined - lse[:, :, None]
    target = jnp.take_along_axis(logprobs, tokens[:, :, None], axis=2)[:, :, 0]
    return (logprobs, target)
```

```python
import jax
import jax.numpy as jnp
from jax import lax
from jax.experimental import pallas as pl
from jax.experimental.pallas import tpu as pltpu
from jax.sharding import Mesh
from jax.sharding import PartitionSpec as P

REF_VOC = ("ref_0", "ref_1", "ref_2", "voc")
REF = ("ref_0", "ref_1", "ref_2")
CHIP = ("ref_0", "ref_1")
CORE = "ref_2"
VOC_REF = ("voc", "ref_0", "ref_1", "ref_2")

clip_bound = 2.0

LANES = 128
WIDE = 512


def partial_sums_kernel(piece, scale):
    def kernel(owner, counts, ids, priv, own, other, keep, send, peak, pub, acc, left):
        rows, positions, columns = priv.shape
        texts = pub.shape[0]
        chips = own.shape[0]
        flat = texts * positions
        chip, core = ids[0], ids[1]
        lane = lax.broadcasted_iota(jnp.int32, (flat, LANES), 1)
        row = lax.broadcasted_iota(jnp.int32, (flat, LANES), 0)
        tail = piece // LANES * LANES
        used = piece - tail

        index = lax.broadcasted_iota(jnp.int32, (chips, flat, LANES), 0)
        near = own[:, :, tail:WIDE].astype(jnp.float32)
        far = other[:, :, tail:WIDE].astype(jnp.float32)
        earlier = jnp.sum(
            jnp.where(index < chip, near, 0.0) + jnp.where(index < chip + core, far, 0.0), axis=0
        )
        for t in range(texts):
            here = jnp.where((lane == used) & (row == t * positions), earlier, 0.0)
            left[t] = counts[t] - jnp.sum(here).astype(jnp.int32)

        def place(q, value):
            start = q * piece
            base = pl.multiple_of(start // LANES * LANES, LANES)
            shift = start - base
            turned = [
                pltpu.roll(value[:, k * LANES : (k + 1) * LANES], shift, 1)
                for k in range(WIDE // LANES)
            ]
            first = lane >= shift
            for t in range(texts):
                part = slice(t * positions, (t + 1) * positions)
                held = pub[t, :, pl.ds(base, LANES)]
                pub[t, :, pl.ds(base, LANES)] = jnp.where(first[part], turned[0][part], held)
            for k in range(1, WIDE // LANES + 1):
                if k < WIDE // LANES:
                    tile = jnp.where(first, turned[k], turned[k - 1])
                else:
                    tile = turned[k - 1]
                for t in range(texts):
                    part = slice(t * positions, (t + 1) * positions)
                    pub[t, :, pl.ds(base + k * LANES, LANES)] = tile[part]

        def join(j, top):
            a = own[j].astype(jnp.float32)
            b = other[j].astype(jnp.float32)
            place(2 * j, jnp.where(core == 0, a, b))
            place(2 * j + 1, jnp.where(core == 0, b, a))
            both = jnp.maximum(a, b)
            for k in range(WIDE // LANES):
                tile = both[:, k * LANES : (k + 1) * LANES]
                if k * LANES == tail:
                    tile = jnp.where(lane < used, tile, top)
                top = jnp.maximum(top, tile)
            return top

        lowest = jnp.full((flat, LANES), -jnp.inf, jnp.float32)
        top = lax.fori_loop(0, chips, join, lowest)
        peak[...] = jnp.broadcast_to(jnp.max(top, axis=1, keepdims=True), (flat, LANES))

        slots = []
        for r in range(rows):
            text = owner[r]
            still = left[text]
            left[text] = still - 1
            slots.append((text, jnp.where(still > 0, text, texts)))

        def accumulate(start, width):
            for t in range(texts):
                acc[t, :, pl.ds(start, width)] = jnp.zeros((positions, width), jnp.float32)
            for r, (text, slot) in enumerate(slots):
                value = priv[r, :, pl.ds(start, width)].astype(jnp.float32)
                value = value - pub[text, :, pl.ds(start, width)]
                value = jnp.clip(value, -clip_bound, clip_bound)
                acc[slot, :, pl.ds(start, width)] = acc[slot, :, pl.ds(start, width)] + value

        step = 2048
        acc[texts] = jnp.zeros(acc.shape[1:], jnp.float32)

        def chunk(i, carry):
            accumulate(pl.multiple_of(i * step, step), step)
            return carry

        lax.fori_loop(0, columns // step, chunk, 0)
        accumulate(columns // step * step, columns % step)

        def cut(q, out, j):
            start = q * piece
            base = pl.multiple_of(start // LANES * LANES, LANES)
            back = LANES - (start - base)
            turned = []
            for k in range(WIDE // LANES + 1):
                tile = jnp.concatenate(
                    [acc[t, :, pl.ds(base + k * LANES, LANES)] for t in range(texts)], axis=0
                )
                turned.append(pltpu.roll(tile, back, 1))
            for k in range(WIDE // LANES):
                tile = jnp.where(lane < back, turned[k], turned[k + 1])
                tile = jnp.round(tile * scale).astype(jnp.int32).astype(jnp.int16)
                out[j, :, k * LANES : (k + 1) * LANES] = tile

        def part_out(j, carry):
            cut(2 * j + core, keep, j)
            cut(2 * j + 1 - core, send, j)
            return carry

        lax.fori_loop(0, chips, part_out, 0)

    return kernel


def partial_sums(private_logits, own, other, owner, counts, ids, piece, scale):
    rows, positions, columns = private_logits.shape
    texts = counts.shape[0]
    chips, flat, wide = own.shape
    padded = -(-columns // LANES) * LANES
    smem = pl.BlockSpec(memory_space=pltpu.SMEM)
    vmem = pl.BlockSpec(memory_space=pltpu.VMEM)
    half = jax.ShapeDtypeStruct((chips, flat, wide), jnp.int16)
    return pl.pallas_call(
        partial_sums_kernel(piece, scale),
        out_shape=(half, half, jax.ShapeDtypeStruct((flat, LANES), jnp.float32)),
        in_specs=[smem, smem, smem, vmem, vmem, vmem],
        out_specs=(vmem, vmem, vmem),
        scratch_shapes=[
            pltpu.VMEM((texts, positions, padded), jnp.float32),
            pltpu.VMEM((texts + 1, positions, padded), jnp.float32),
            pltpu.SMEM((texts,), jnp.int32),
        ],
        name="partial_sums",
    )(owner, counts, ids, private_logits, own, other)


def body(private_logits, public_logits, noise, owner, counts, tokens):
    texts, positions, piece = public_logits.shape
    rows = owner.shape[0]
    flat = texts * positions
    chips = lax.axis_size(CHIP)
    chip, core = lax.axis_index(CHIP), lax.axis_index(CORE)
    swap = [(0, 1), (1, 0)]
    scale = float(32767 // (2 * rows * int(clip_bound)))

    labels = jnp.arange(texts, dtype=jnp.int32)
    held = jnp.sum((owner[:, None] == labels[None, :]).astype(jnp.int32), 0)
    public_rows = public_logits.reshape(flat, piece)
    count_column = jnp.repeat(held, positions).astype(jnp.bfloat16)[:, None]
    packed = jnp.concatenate([public_rows, count_column], axis=1)
    packed = jnp.pad(packed, ((0, 0), (0, WIDE - piece - 1)))
    own = lax.all_to_all(
        jnp.broadcast_to(packed, (chips, flat, WIDE)), CHIP, split_axis=0, concat_axis=0, tiled=True
    )
    other = lax.ppermute(own, CORE, swap)

    ids = jnp.stack([chip, core]).astype(jnp.int32)
    keep, send, peak = partial_sums(
        private_logits, own, other, owner, counts, ids, piece, scale
    )
    both = keep + lax.ppermute(send, CORE, swap)
    parts = lax.all_to_all(both, CHIP, split_axis=0, concat_axis=0, tiled=True)

    text_scale = 1.0 / (clip_bound * jnp.sqrt(counts.astype(jnp.float32)))
    summed = jnp.sum(parts.astype(jnp.float32), axis=0)
    row_scale = jnp.repeat(text_scale, positions)[:, None] * (1.0 / scale)
    noise_rows = jnp.pad(noise.reshape(flat, piece), ((0, 0), (0, WIDE - piece)))
    combined = packed.astype(jnp.float32) + summed * row_scale + noise_rows.astype(jnp.float32)
    at = jnp.arange(WIDE, dtype=jnp.int32)
    first_column = (lax.axis_index("voc") * lax.axis_size(REF) + lax.axis_index(REF)) * piece
    token_rows = tokens.reshape(flat)[:, None] - first_column
    level = peak[:, 0]
    inside = (at < piece)[None, :]
    terms = jnp.where(inside, jnp.exp(combined - level[:, None]), 0.0)
    row_total = jnp.sum(terms, axis=1)
    picked = jnp.sum(jnp.where((at[None, :] == token_rows) & inside, combined, 0.0), axis=1)

    stats = jnp.concatenate([row_total, picked, level])
    stats = jnp.pad(stats, (0, LANES - 3 * flat))
    devices = lax.axis_size(REF_VOC)
    everyone = lax.all_to_all(
        jnp.broadcast_to(stats, (devices, 1, LANES)), REF_VOC, split_axis=0, concat_axis=0, tiled=True
    ).reshape(devices, LANES)
    levels = everyone[:, 2 * flat : 3 * flat]
    row_peak = jnp.max(levels, axis=0)
    total = jnp.sum(everyone[:, :flat] * jnp.exp(levels - row_peak), axis=0)
    target = jnp.sum(everyone[:, flat : 2 * flat], axis=0)
    lse = row_peak + jnp.log(total)
    logprobs = (combined - lse[:, None])[:, :piece].reshape(texts, positions, piece)
    return (logprobs, (target - lse).reshape(texts, positions))


def solution(mesh):
    finer = Mesh(
        mesh.devices.reshape(8, 4, 2, mesh.shape["voc"]), ("ref_0", "ref_1", "ref_2", "voc")
    )
    placed = (P(REF, None, "voc"), P(None, None, VOC_REF), P(None, None, VOC_REF), P(REF), P(), P())
    return jax.shard_map(
        body, mesh=finer, in_specs=placed, out_specs=(P(None, None, VOC_REF), P()), check_vma=False
    )
```

```python
import jax
import jax.numpy as jnp
from jax import lax
from jax.experimental import pallas as pl
from jax.experimental.pallas import tpu as pltpu
from jax.sharding import Mesh
from jax.sharding import PartitionSpec as P

REF_VOC = ("ref_0", "ref_1", "ref_2", "voc")
REF = ("ref_0", "ref_1", "ref_2")
CHIP = ("ref_0", "ref_1")
CORE = "ref_2"
VOC_REF = ("voc", "ref_0", "ref_1", "ref_2")

clip_bound = 2.0

LANES = 128
WIDE = 512
TILES = WIDE // LANES
WINDOW = WIDE + LANES
GROUP = 4

PARAMS = pltpu.CompilerParams(vmem_limit_bytes=16 << 20)
SMEM = pl.BlockSpec(memory_space=pltpu.SMEM)
VMEM = pl.BlockSpec(memory_space=pltpu.VMEM)


def tile_of(x, k):
    return x[:, k * LANES : (k + 1) * LANES]


def turned(tiles, shift, lane):
    spun = [pltpu.roll(tile, shift, 1) for tile in tiles]
    return [jnp.where(lane >= shift, spun[k], spun[k - 1]) for k in range(TILES)]


def turned_back(tiles, shift, lane):
    back = LANES - shift
    spun = [pltpu.roll(tile, back, 1) for tile in tiles]
    return [jnp.where(lane < back, spun[k], spun[(k + 1) % TILES]) for k in range(TILES)]


def lanes_of(shape):
    return lax.broadcasted_iota(jnp.int32, shape, len(shape) - 1)


def pack_kernel(public, near, far, ids, out, flat_rows):
    texts, positions, piece = public.shape
    flat = texts * positions
    for t in range(texts):
        flat_rows[t * positions : (t + 1) * positions, :piece] = public[t].astype(jnp.float32)
    row = lax.broadcasted_iota(jnp.int32, (flat, LANES), 0)
    lane = lanes_of((flat, LANES))
    number = jnp.zeros((flat, LANES), jnp.float32)
    for t in range(texts):
        held = jnp.int32(0)
        for r in range(near.shape[0]):
            held += jnp.where(near[r] == t, 1, 0) + jnp.where(far[r] == t, 1, 0)
        inside = (row >= t * positions) & (row < (t + 1) * positions)
        number = jnp.where(inside, held.astype(jnp.float32), number)
    values = flat_rows[...]
    tiles = [
        jnp.where(lane + k * LANES < piece, tile_of(values, k), number) for k in range(TILES)
    ]
    tiles = [tile.astype(out.dtype) for tile in turned(tiles, ids[2], lane)]
    for j in range(out.shape[0]):
        for k in range(TILES):
            out[j, :, k * LANES : (k + 1) * LANES] = tiles[k]


def sums_kernel(piece, scale):
    def kernel(owner, partner, counts, ids, priv, swapped, own, out, pub, acc, left):
        rows, positions, columns = priv.shape
        texts = counts.shape[0]
        chips, flat, _ = own.shape
        chip, core = ids[0], ids[1]
        lane = lanes_of((flat, LANES))
        row = lax.broadcasted_iota(jnp.int32, (flat, LANES), 0)
        last = columns // LANES * LANES

        def begins(j):
            start = (2 * j + core) * piece
            base = start // LANES * LANES
            return pl.multiple_of(base, LANES), start - base

        def widen(j, earlier):
            value = own[j].astype(jnp.float32)
            for t in range(texts):
                part = value[t * positions : (t + 1) * positions]
                pub[t, :, pl.ds(pl.multiple_of(j * WINDOW, LANES), WIDE)] = part
                pub[t, :, pl.ds(pl.multiple_of(j * WINDOW + WIDE, LANES), LANES)] = part[:, :LANES]
            shift = begins(j)[1]
            free = jnp.where(shift == 0, LANES - 1, shift - 1)
            tile = jnp.where(shift == 0, tile_of(value, TILES - 1), tile_of(value, 0))
            free = jnp.where(j < chip, free, LANES)
            return earlier + jnp.where(lane == free, tile, 0.0)

        earlier = lax.fori_loop(0, chips, widen, jnp.zeros((flat, LANES), jnp.float32))
        for t in range(texts):
            here = jnp.where(row == t * positions, earlier, 0.0)
            left[t] = counts[t] - jnp.sum(here).astype(jnp.int32)

        slots = [[None] * rows, [None] * rows]
        for c in range(2):
            for r in range(rows):
                text = jnp.where(core == c, owner[r], partner[r])
                still = left[text]
                left[text] = still - 1
                slots[c][r] = jnp.where(still > 0, text, texts)
        acc[texts] = jnp.zeros(acc.shape[1:], jnp.float32)

        def accumulate(first, many, size):
            places = [first + g for g in range(many)]
            bases = [begins(j)[0] for j in places]
            for t in range(texts):
                for g in range(many):
                    acc[t, :, g * WINDOW : g * WINDOW + size[g]] = jnp.zeros(
                        (positions, size[g]), jnp.float32
                    )
            for r in range(rows):
                for held, text, c in ((priv, owner, core), (swapped, partner, 1 - core)):
                    slot = jnp.where(c == 0, slots[0][r], slots[1][r])
                    for g, j in enumerate(places):
                        at = pl.multiple_of(j * WINDOW, LANES)
                        value = held[r, :, pl.ds(bases[g], size[g])].astype(jnp.float32)
                        value = value - pub[text[r], :, pl.ds(at, size[g])]
                        value = jnp.clip(value, -clip_bound, clip_bound)
                        where = slice(g * WINDOW, g * WINDOW + size[g])
                        acc[slot, :, where] = acc[slot, :, where] + value
            for g, j in enumerate(places):
                shift = begins(j)[1]
                tiles = [
                    jnp.concatenate(
                        [
                            acc[t, :, g * WINDOW + k * LANES : g * WINDOW + (k + 1) * LANES]
                            for t in range(texts)
                        ],
                        axis=0,
                    )
                    for k in range(TILES + 1)
                ]
                tiles[0] = jnp.where(lane >= shift, tiles[0], tiles[TILES])
                for k in range(TILES):
                    fixed = jnp.round(tiles[k] * scale).astype(jnp.int32).astype(jnp.int16)
                    out[j, :, k * LANES : (k + 1) * LANES] = fixed

        def some(i, carry):
            accumulate(i * GROUP, GROUP, [WINDOW] * GROUP)
            return carry

        lax.fori_loop(0, chips // GROUP - 1, some, 0)
        accumulate(chips - GROUP, GROUP - 1, [WINDOW] * (GROUP - 1))
        for c in range(2):
            start = (2 * chips - 2 + c) * piece // LANES * LANES

            @pl.when(core == c)
            def _():
                accumulate(jnp.int32(chips - 1), 1, [min(WINDOW, columns - start)])

    return kernel


def chip_sums(private_logits, swapped, own, owner, partner, counts, ids, piece, scale):
    rows, positions, columns = private_logits.shape
    texts = counts.shape[0]
    chips, flat, wide = own.shape
    return pl.pallas_call(
        sums_kernel(piece, scale),
        out_shape=pltpu.VMEM((chips, flat, wide), jnp.int16),
        in_specs=[SMEM, SMEM, SMEM, SMEM, VMEM, VMEM, VMEM],
        out_specs=VMEM,
        scratch_shapes=[
            pltpu.VMEM((texts, positions, chips * WINDOW), jnp.float32),
            pltpu.VMEM((texts + 1, positions, GROUP * WINDOW), jnp.float32),
            pltpu.SMEM((texts,), jnp.int32),
        ],
        compiler_params=PARAMS,
        name="chip_sums",
    )(owner, partner, counts, ids, private_logits, swapped, own)


def finish_kernel(inverse):
    def kernel(counts, tokens, ids, parts, public, noise, combined, stats, base):
        texts, positions, piece = public.shape
        flat = texts * positions
        lane = lanes_of((flat, LANES))
        row = lax.broadcasted_iota(jnp.int32, (flat, LANES), 0)
        base[...] = jnp.full(base.shape, -jnp.inf, jnp.float32)
        for t in range(texts):
            part = slice(t * positions, (t + 1) * positions)
            base[0, part, :piece] = public[t].astype(jnp.float32)
            base[1, part, :piece] = noise[t].astype(jnp.float32)
        scale = jnp.zeros((flat, LANES), jnp.float32)
        token = jnp.zeros((flat, LANES), jnp.int32)
        for t in range(texts):
            inside = (row >= t * positions) & (row < (t + 1) * positions)
            number = jnp.where(inside, counts[t].astype(jnp.float32), 1.0)
            scale = jnp.where(inside, inverse / (clip_bound * jnp.sqrt(number)), scale)
            for p in range(positions):
                token = jnp.where(row == t * positions + p, tokens[t, p], token)
        token = token - ids[3]
        total = []
        for k in range(TILES):
            tile = parts[0, :, k * LANES : (k + 1) * LANES].astype(jnp.int32)
            for j in range(1, parts.shape[0]):
                tile = tile + parts[j, :, k * LANES : (k + 1) * LANES].astype(jnp.int32)
            total.append(tile.astype(jnp.float32))
        total = turned_back(total, ids[2], lane)
        public_tiles = [base[0, :, k * LANES : (k + 1) * LANES] for k in range(TILES)]
        level = public_tiles[0]
        for k in range(1, TILES):
            level = jnp.maximum(level, public_tiles[k])
        level = jnp.max(level, axis=1, keepdims=True)
        terms = jnp.zeros((flat, LANES), jnp.float32)
        picked = jnp.zeros((flat, LANES), jnp.float32)
        for k in range(TILES):
            tile = public_tiles[k] + total[k] * scale + base[1, :, k * LANES : (k + 1) * LANES]
            inside = lane + k * LANES < piece
            combined[:, k * LANES : (k + 1) * LANES] = tile
            terms = terms + jnp.where(inside, jnp.exp(tile - level), 0.0)
            picked = picked + jnp.where((lane + k * LANES == token) & inside, tile, 0.0)
        terms = jnp.sum(terms, axis=1, keepdims=True)
        picked = jnp.sum(picked, axis=1, keepdims=True)
        spread = jnp.where(lane == row, terms, 0.0)
        spread = spread + jnp.where(lane == row + flat, picked, 0.0)
        spread = spread + jnp.where(lane == row + 2 * flat, level, 0.0)
        stats[...] = jnp.sum(spread, axis=0, keepdims=True)

    return kernel


def body(private_logits, public_logits, noise, owner, counts, tokens):
    texts, positions, piece = public_logits.shape
    rows = owner.shape[0]
    flat = texts * positions
    chips = lax.axis_size(CHIP)
    chip, core = lax.axis_index(CHIP), lax.axis_index(CORE)
    swap = [(0, 1), (1, 0)]
    scale = float(32767 // (2 * rows * int(clip_bound)))
    place = lax.axis_index(REF)
    first_column = (lax.axis_index("voc") * lax.axis_size(REF) + place) * piece
    ids = jnp.stack([chip, core, place * piece % LANES, first_column]).astype(jnp.int32)

    partner = lax.ppermute(owner, CORE, swap)
    swapped = lax.ppermute(private_logits, CORE, swap)
    packed = pl.pallas_call(
        pack_kernel,
        out_shape=pltpu.VMEM((chips, flat, WIDE), jnp.bfloat16),
        in_specs=[VMEM, SMEM, SMEM, SMEM],
        out_specs=VMEM,
        scratch_shapes=[pltpu.VMEM((flat, WIDE), jnp.float32)],
        compiler_params=PARAMS,
        name="pack",
    )(public_logits, owner, partner, ids)
    own = lax.all_to_all(packed, CHIP, split_axis=0, concat_axis=0, tiled=True)
    private_logits, swapped, own = (
        pltpu.with_memory_space_constraint(x, pltpu.VMEM) for x in (private_logits, swapped, own)
    )
    sums = chip_sums(private_logits, swapped, own, owner, partner, counts, ids, piece, scale)
    parts = lax.all_to_all(sums, CHIP, split_axis=0, concat_axis=0, tiled=True)

    parts = pltpu.with_memory_space_constraint(parts, pltpu.VMEM)
    combined, stats = pl.pallas_call(
        finish_kernel(1.0 / scale),
        out_shape=(
            pltpu.VMEM((flat, WIDE), jnp.float32),
            pltpu.VMEM((1, LANES), jnp.float32),
        ),
        in_specs=[SMEM, SMEM, SMEM, VMEM, VMEM, VMEM],
        out_specs=(VMEM, VMEM),
        scratch_shapes=[pltpu.VMEM((2, flat, WIDE), jnp.float32)],
        compiler_params=PARAMS,
        name="finish",
    )(counts, tokens, ids, parts, public_logits, noise)

    devices = lax.axis_size(REF_VOC)
    everyone = lax.all_to_all(
        jnp.broadcast_to(stats, (devices, 1, LANES)), REF_VOC, split_axis=0, concat_axis=0, tiled=True
    ).reshape(devices, LANES)
    levels = everyone[:, 2 * flat : 3 * flat]
    row_peak = jnp.max(levels, axis=0)
    total = jnp.sum(everyone[:, :flat] * jnp.exp(levels - row_peak), axis=0)
    target = jnp.sum(everyone[:, flat : 2 * flat], axis=0)
    lse = row_peak + jnp.log(total)
    logprobs = (combined - lse[:, None])[:, :piece].reshape(texts, positions, piece)
    return (logprobs, (target - lse).reshape(texts, positions))


def solution(mesh):
    finer = Mesh(
        mesh.devices.reshape(8, 4, 2, mesh.shape["voc"]), ("ref_0", "ref_1", "ref_2", "voc")
    )
    placed = (P(REF, None, "voc"), P(None, None, VOC_REF), P(None, None, VOC_REF), P(REF), P(), P())
    return jax.shard_map(
        body, mesh=finer, in_specs=placed, out_specs=(P(None, None, VOC_REF), P()), check_vma=False
    )
```

```python
import jax
import jax.numpy as jnp
from jax import lax
from jax.experimental import pallas as pl
from jax.experimental.pallas import tpu as pltpu
from jax.sharding import Mesh
from jax.sharding import PartitionSpec as P

REF_VOC = ("ref_0", "ref_1", "ref_2", "voc")
REF = ("ref_0", "ref_1", "ref_2")
CHIP = ("ref_0", "ref_1")
CORE = "ref_2"
VOC_REF = ("voc", "ref_0", "ref_1", "ref_2")

clip_bound = 2.0

LANES = 128
WIDE = 512
TILES = WIDE // LANES
WINDOW = WIDE + LANES
GROUP = 4
LEAD = LANES

CHIP_AT, CORE_AT, SHIFT, FIRST, COUNTS, TOKENS, OWNER = 0, 1, 2, 3, 4, 8, 24

PARAMS = pltpu.CompilerParams(vmem_limit_bytes=16 << 20)
SMEM = pl.BlockSpec(memory_space=pltpu.SMEM)
VMEM = pl.BlockSpec(memory_space=pltpu.VMEM)
HBM = pl.BlockSpec(memory_space=pltpu.HBM)


def tile_of(x, k):
    return x[:, k * LANES : (k + 1) * LANES]


def turned(tiles, shift, lane):
    spun = [pltpu.roll(tile, shift, 1) for tile in tiles]
    return [jnp.where(lane >= shift, spun[k], spun[k - 1]) for k in range(TILES)]


def turned_back(tiles, shift, lane):
    back = LANES - shift
    spun = [pltpu.roll(tile, back, 1) for tile in tiles]
    return [jnp.where(lane < back, spun[k], spun[(k + 1) % TILES]) for k in range(TILES)]


def lanes_of(shape):
    return lax.broadcasted_iota(jnp.int32, shape, len(shape) - 1)


def pack_kernel(public, table, far, out, flat_rows):
    texts, positions, piece = public.shape
    flat = texts * positions
    for t in range(texts):
        flat_rows[t * positions : (t + 1) * positions, :piece] = public[t].astype(jnp.float32)
    row = lax.broadcasted_iota(jnp.int32, (flat, LANES), 0)
    lane = lanes_of((flat, LANES))
    number = jnp.zeros((flat, LANES), jnp.float32)
    for t in range(texts):
        held = jnp.int32(0)
        for r in range(far.shape[0]):
            held += jnp.where(table[OWNER + r] == t, 1, 0) + jnp.where(far[r] == t, 1, 0)
        inside = (row >= t * positions) & (row < (t + 1) * positions)
        number = jnp.where(inside, held.astype(jnp.float32), number)
    values = flat_rows[...]
    tiles = [
        jnp.where(lane + k * LANES < piece, tile_of(values, k), number) for k in range(TILES)
    ]
    tiles = [tile.astype(out.dtype) for tile in turned(tiles, table[SHIFT], lane)]
    for j in range(out.shape[0]):
        for k in range(TILES):
            out[j, :, k * LANES : (k + 1) * LANES] = tiles[k]


def sums_kernel(piece, scale):
    def kernel(table, partner, source, swapped, own, out, priv, pub, acc, left, arrived):
        rows, positions, columns = priv.shape
        texts = pub.shape[0]
        chips, flat, _ = own.shape
        groups = chips // GROUP
        chip, core = table[CHIP_AT], table[CORE_AT]

        stride = 2 * GROUP * piece
        stride = -(-stride // LANES) * LANES

        def copy_of(i, start, width):
            return pltpu.make_async_copy(
                source.at[:, :, pl.ds(start, width)],
                priv.at[:, :, pl.ds(start, width)],
                arrived.at[i],
            )

        first_chunk = (0, 0, stride + LEAD)
        last_start = LEAD + (groups - 1) * stride
        last_chunk = (groups - 1, last_start, columns - last_start)
        copy_of(*first_chunk).start()
        for i in range(1, groups - 1):
            copy_of(i, LEAD + i * stride, stride).start()
        copy_of(*last_chunk).start()

        lane = lanes_of((flat, LANES))
        row = lax.broadcasted_iota(jnp.int32, (flat, LANES), 0)
        last = columns // LANES * LANES

        def begins(j):
            start = (2 * j + core) * piece
            base = start // LANES * LANES
            return pl.multiple_of(base, LANES), start - base

        def widen(j, earlier):
            value = own[j].astype(jnp.float32)
            for t in range(texts):
                part = value[t * positions : (t + 1) * positions]
                pub[t, :, pl.ds(pl.multiple_of(j * WINDOW, LANES), WIDE)] = part
                pub[t, :, pl.ds(pl.multiple_of(j * WINDOW + WIDE, LANES), LANES)] = part[:, :LANES]
            shift = begins(j)[1]
            free = jnp.where(shift == 0, LANES - 1, shift - 1)
            tile = jnp.where(shift == 0, tile_of(value, TILES - 1), tile_of(value, 0))
            free = jnp.where(j < chip, free, LANES)
            return earlier + jnp.where(lane == free, tile, 0.0)

        earlier = lax.fori_loop(0, chips, widen, jnp.zeros((flat, LANES), jnp.float32))
        for t in range(texts):
            here = jnp.where(row == t * positions, earlier, 0.0)
            left[t] = table[COUNTS + t] - jnp.sum(here).astype(jnp.int32)

        slots = [[None] * rows, [None] * rows]
        for c in range(2):
            for r in range(rows):
                text = jnp.where(core == c, table[OWNER + r], partner[r])
                still = left[text]
                left[text] = still - 1
                slots[c][r] = jnp.where(still > 0, text, texts)
        acc[texts] = jnp.zeros(acc.shape[1:], jnp.float32)

        def accumulate(first, many, size):
            places = [first + g for g in range(many)]
            bases = [begins(j)[0] for j in places]
            for t in range(texts):
                for g in range(many):
                    acc[t, :, g * WINDOW : g * WINDOW + size[g]] = jnp.zeros(
                        (positions, size[g]), jnp.float32
                    )
            for r in range(rows):
                for held, text, c in (
                    (priv, table[OWNER + r], core),
                    (swapped, partner[r], 1 - core),
                ):
                    slot = jnp.where(c == 0, slots[0][r], slots[1][r])
                    for g, j in enumerate(places):
                        at = pl.multiple_of(j * WINDOW, LANES)
                        value = held[r, :, pl.ds(bases[g], size[g])].astype(jnp.float32)
                        value = value - pub[text, :, pl.ds(at, size[g])]
                        value = jnp.clip(value, -clip_bound, clip_bound)
                        where = slice(g * WINDOW, g * WINDOW + size[g])
                        acc[slot, :, where] = acc[slot, :, where] + value
            for g, j in enumerate(places):
                shift = begins(j)[1]
                tiles = [
                    jnp.concatenate(
                        [
                            acc[t, :, g * WINDOW + k * LANES : g * WINDOW + (k + 1) * LANES]
                            for t in range(texts)
                        ],
                        axis=0,
                    )
                    for k in range(TILES + 1)
                ]
                tiles[0] = jnp.where(lane >= shift, tiles[0], tiles[TILES])
                for k in range(TILES):
                    fixed = jnp.round(tiles[k] * scale).astype(jnp.int32).astype(jnp.int16)
                    out[j, :, k * LANES : (k + 1) * LANES] = fixed

        def some(i, carry):
            copy_of(i, pl.multiple_of(LEAD + i * stride, LANES), stride).wait()
            accumulate(i * GROUP, GROUP, [WINDOW] * GROUP)
            return carry

        copy_of(*first_chunk).wait()
        accumulate(jnp.int32(0), GROUP, [WINDOW] * GROUP)
        lax.fori_loop(1, groups - 1, some, 0)
        copy_of(*last_chunk).wait()
        accumulate(chips - GROUP, GROUP - 1, [WINDOW] * (GROUP - 1))
        for c in range(2):
            start = (2 * chips - 2 + c) * piece // LANES * LANES

            @pl.when(core == c)
            def _():
                accumulate(jnp.int32(chips - 1), 1, [min(WINDOW, columns - start)])

    return kernel


def chip_sums(private_logits, swapped, own, table, partner, texts, piece, scale):
    rows, positions, columns = private_logits.shape
    chips, flat, wide = own.shape
    return pl.pallas_call(
        sums_kernel(piece, scale),
        out_shape=pltpu.VMEM((chips, flat, wide), jnp.int16),
        in_specs=[SMEM, SMEM, HBM, VMEM, VMEM],
        out_specs=VMEM,
        scratch_shapes=[
            pltpu.VMEM(private_logits.shape, private_logits.dtype),
            pltpu.VMEM((texts, positions, chips * WINDOW), jnp.float32),
            pltpu.VMEM((texts + 1, positions, GROUP * WINDOW), jnp.float32),
            pltpu.SMEM((texts,), jnp.int32),
            pltpu.SemaphoreType.DMA((chips // GROUP,)),
        ],
        compiler_params=PARAMS,
        name="chip_sums",
    )(table, partner, private_logits, swapped, own)


def finish_kernel(inverse):
    def kernel(table, parts, public, noise, combined, stats, base):
        texts, positions, piece = public.shape
        flat = texts * positions
        lane = lanes_of((flat, LANES))
        row = lax.broadcasted_iota(jnp.int32, (flat, LANES), 0)
        base[...] = jnp.full(base.shape, -jnp.inf, jnp.float32)
        for t in range(texts):
            part = slice(t * positions, (t + 1) * positions)
            base[0, part, :piece] = public[t].astype(jnp.float32)
            base[1, part, :piece] = noise[t].astype(jnp.float32)
        scale = jnp.zeros((flat, LANES), jnp.float32)
        token = jnp.zeros((flat, LANES), jnp.int32)
        for t in range(texts):
            inside = (row >= t * positions) & (row < (t + 1) * positions)
            number = jnp.where(inside, table[COUNTS + t].astype(jnp.float32), 1.0)
            scale = jnp.where(inside, inverse / (clip_bound * jnp.sqrt(number)), scale)
            for p in range(positions):
                at = t * positions + p
                token = jnp.where(row == at, table[TOKENS + at], token)
        token = token - table[FIRST]
        total = []
        for k in range(TILES):
            tile = parts[0, :, k * LANES : (k + 1) * LANES].astype(jnp.int32)
            for j in range(1, parts.shape[0]):
                tile = tile + parts[j, :, k * LANES : (k + 1) * LANES].astype(jnp.int32)
            total.append(tile.astype(jnp.float32))
        total = turned_back(total, table[SHIFT], lane)
        public_tiles = [base[0, :, k * LANES : (k + 1) * LANES] for k in range(TILES)]
        level = public_tiles[0]
        for k in range(1, TILES):
            level = jnp.maximum(level, public_tiles[k])
        level = jnp.max(level, axis=1, keepdims=True)
        terms = jnp.zeros((flat, LANES), jnp.float32)
        picked = jnp.zeros((flat, LANES), jnp.float32)
        for k in range(TILES):
            tile = public_tiles[k] + total[k] * scale + base[1, :, k * LANES : (k + 1) * LANES]
            inside = lane + k * LANES < piece
            combined[:, k * LANES : (k + 1) * LANES] = tile
            terms = terms + jnp.where(inside, jnp.exp(tile - level), 0.0)
            picked = picked + jnp.where((lane + k * LANES == token) & inside, tile, 0.0)
        terms = jnp.sum(terms, axis=1, keepdims=True)
        picked = jnp.sum(picked, axis=1, keepdims=True)
        spread = jnp.where(lane == row, terms, 0.0)
        spread = spread + jnp.where(lane == row + flat, picked, 0.0)
        spread = spread + jnp.where(lane == row + 2 * flat, level, 0.0)
        stats[...] = jnp.sum(spread, axis=0, keepdims=True)

    return kernel


def last_kernel(everyone, combined, logprobs, target):
    texts, positions, piece = logprobs.shape
    flat = texts * positions
    values = everyone[...]
    lane = lanes_of((1, LANES))
    level = jnp.max(values, axis=0, keepdims=True)
    weight = pltpu.roll(jnp.exp(values - level), LANES - 2 * flat, 1)
    total = jnp.sum(values * weight, axis=0, keepdims=True)
    picked = pltpu.roll(jnp.sum(values, axis=0, keepdims=True), LANES - flat, 1)
    level = pltpu.roll(level, LANES - 2 * flat, 1)
    own = lane < flat
    lse = jnp.where(own, level + jnp.log(jnp.where(own, total, 1.0)), 0.0)
    picked = picked - lse
    square = (flat, LANES)
    mine = lanes_of(square) == lax.broadcasted_iota(jnp.int32, square, 0)
    column = jnp.sum(jnp.where(mine, jnp.broadcast_to(lse, square), 0.0), axis=1, keepdims=True)
    shifted = combined[:, :piece] - column
    for t in range(texts):
        logprobs[t] = shifted[t * positions : (t + 1) * positions]
    for t in range(texts):
        turn = picked if t == 0 else pltpu.roll(picked, LANES - t * positions, 1)
        target[t : t + 1, :] = turn[:, :positions]


def body(private_logits, public_logits, noise, owner, counts, tokens):
    texts, positions, piece = public_logits.shape
    rows = owner.shape[0]
    flat = texts * positions
    chips = lax.axis_size(CHIP)
    chip, core = lax.axis_index(CHIP), lax.axis_index(CORE)
    swap = [(0, 1), (1, 0)]
    scale = float(32767 // (2 * rows * int(clip_bound)))
    place = lax.axis_index(REF)
    first_column = (lax.axis_index("voc") * lax.axis_size(REF) + place) * piece
    table = jnp.concatenate(
        [
            jnp.stack([chip, core, place * piece % LANES, first_column]).astype(jnp.int32),
            counts,
            tokens.reshape(-1),
            owner,
        ]
    )

    partner = lax.ppermute(owner, CORE, swap)
    partner, private_later = lax.optimization_barrier((partner, private_logits))
    swapped = lax.ppermute(private_later, CORE, swap)
    packed = pl.pallas_call(
        pack_kernel,
        out_shape=pltpu.VMEM((chips, flat, WIDE), jnp.bfloat16),
        in_specs=[VMEM, SMEM, SMEM],
        out_specs=VMEM,
        scratch_shapes=[pltpu.VMEM((flat, WIDE), jnp.float32)],
        compiler_params=PARAMS,
        name="pack",
    )(pltpu.with_memory_space_constraint(public_logits, pltpu.HBM), table, partner)
    own = lax.all_to_all(packed, CHIP, split_axis=0, concat_axis=0, tiled=True)
    swapped, own = (pltpu.with_memory_space_constraint(x, pltpu.VMEM) for x in (swapped, own))
    source = pltpu.with_memory_space_constraint(private_logits, pltpu.HBM)
    sums = chip_sums(source, swapped, own, table, partner, texts, piece, scale)
    parts = lax.all_to_all(sums, CHIP, split_axis=0, concat_axis=0, tiled=True)

    parts = pltpu.with_memory_space_constraint(parts, pltpu.VMEM)
    combined, stats = pl.pallas_call(
        finish_kernel(1.0 / scale),
        out_shape=(
            pltpu.VMEM((flat, WIDE), jnp.float32),
            pltpu.VMEM((1, LANES), jnp.float32),
        ),
        in_specs=[SMEM, VMEM, VMEM, VMEM],
        out_specs=(VMEM, VMEM),
        scratch_shapes=[pltpu.VMEM((2, flat, WIDE), jnp.float32)],
        compiler_params=PARAMS,
        name="finish",
    )(table, parts, public_logits, noise)

    devices = lax.axis_size(REF_VOC)
    everyone = lax.all_to_all(
        jnp.broadcast_to(stats, (devices, 1, LANES)), REF_VOC, split_axis=0, concat_axis=0, tiled=True
    ).reshape(devices, LANES)
    return pl.pallas_call(
        last_kernel,
        out_shape=(
            jax.ShapeDtypeStruct(public_logits.shape, jnp.float32),
            jax.ShapeDtypeStruct((texts, positions), jnp.float32),
        ),
        in_specs=[VMEM, VMEM],
        out_specs=(VMEM, VMEM),
        compiler_params=PARAMS,
        name="last",
    )(pltpu.with_memory_space_constraint(everyone, pltpu.VMEM), combined)


def solution(mesh):
    finer = Mesh(
        mesh.devices.reshape(8, 4, 2, mesh.shape["voc"]), ("ref_0", "ref_1", "ref_2", "voc")
    )
    placed = (P(REF, None, "voc"), P(None, None, VOC_REF), P(None, None, VOC_REF), P(REF), P(), P())
    return jax.shard_map(
        body, mesh=finer, in_specs=placed, out_specs=(P(None, None, VOC_REF), P()), check_vma=False
    )
```

```python
import jax
import jax.numpy as jnp
from jax import lax
from jax.experimental import pallas as pl
from jax.experimental.pallas import tpu as pltpu
from jax.sharding import Mesh
from jax.sharding import PartitionSpec as P

REF_VOC = ("ref_0", "ref_1", "ref_2", "voc")
REF = ("ref_0", "ref_1", "ref_2")
CHIP = ("ref_0", "ref_1")
CORE = "ref_2"
VOC_REF = ("voc", "ref_0", "ref_1", "ref_2")

clip_bound = 2.0

LANES = 128
WIDE = 512
TILES = WIDE // LANES
WINDOW = WIDE + LANES
GROUP = 4
LEAD = LANES

CHIP_AT, CORE_AT, SHIFT, FIRST = range(4)

PARAMS = pltpu.CompilerParams(vmem_limit_bytes=16 << 20)
SMEM = pl.BlockSpec(memory_space=pltpu.SMEM)
VMEM = pl.BlockSpec(memory_space=pltpu.VMEM)
HBM = pl.BlockSpec(memory_space=pltpu.HBM)


def tile_of(x, k):
    return x[:, k * LANES : (k + 1) * LANES]


def turned(tiles, shift, lane):
    spun = [pltpu.roll(tile, shift, 1) for tile in tiles]
    return [jnp.where(lane >= shift, spun[k], spun[k - 1]) for k in range(TILES)]


def turned_back(tiles, shift, lane):
    back = LANES - shift
    spun = [pltpu.roll(tile, back, 1) for tile in tiles]
    return [jnp.where(lane < back, spun[k], spun[(k + 1) % TILES]) for k in range(TILES)]


def lanes_of(shape):
    return lax.broadcasted_iota(jnp.int32, shape, len(shape) - 1)


def rows_of(array, scratch):
    texts, positions, piece = array.shape
    for t in range(texts):
        part = slice(t * positions, (t + 1) * positions)
        scratch[part, :piece] = array[t].astype(jnp.float32)
    values = scratch[...]
    lane = lanes_of((texts * positions, LANES))
    return [
        jnp.where(lane + k * LANES < piece, tile_of(values, k), 0.0) for k in range(TILES)
    ]


def column_of(lane, k, shift):
    return (lane + k * LANES - shift) & (WIDE - 1)


def turn_kernel(public, ids, out, scratch):
    lane = lanes_of((out.shape[0], LANES))
    for k, tile in enumerate(turned(rows_of(public, scratch), ids[SHIFT], lane)):
        out[:, k * LANES : (k + 1) * LANES] = tile


def mark_kernel(piece, positions):
    def kernel(one, near, far, ids, out):
        flat = one.shape[0]
        row = lax.broadcasted_iota(jnp.int32, (flat, LANES), 0)
        lane = lanes_of((flat, LANES))
        number = jnp.zeros((flat, LANES), jnp.float32)
        for t in range(flat // positions):
            held = jnp.int32(0)
            for r in range(near.shape[0]):
                held += jnp.where(near[r] == t, 1, 0) + jnp.where(far[r] == t, 1, 0)
            inside = (row >= t * positions) & (row < (t + 1) * positions)
            number = jnp.where(inside, held.astype(jnp.float32), number)
        for k in range(TILES):
            tile = one[:, k * LANES : (k + 1) * LANES]
            tile = jnp.where(column_of(lane, k, ids[SHIFT]) < piece, tile, number)
            tile = tile.astype(out.dtype)
            for j in range(out.shape[0]):
                out[j, :, k * LANES : (k + 1) * LANES] = tile

    return kernel


def sums_kernel(piece, scale):
    def kernel(owner, partner, counts, ids, source, swapped, own, out, priv, pub, acc, left, arrived):
        rows, positions, columns = priv.shape
        texts = pub.shape[0]
        chips, flat, _ = own.shape
        groups = chips // GROUP
        chip, core = ids[CHIP_AT], ids[CORE_AT]

        stride = 2 * GROUP * piece
        stride = -(-stride // LANES) * LANES

        def copy_of(i, start, width):
            return pltpu.make_async_copy(
                source.at[:, :, pl.ds(start, width)],
                priv.at[:, :, pl.ds(start, width)],
                arrived.at[i],
            )

        first_chunk = (0, 0, stride + LEAD)
        last_start = LEAD + (groups - 1) * stride
        last_chunk = (groups - 1, last_start, columns - last_start)
        copy_of(*first_chunk).start()
        for i in range(1, groups - 1):
            copy_of(i, LEAD + i * stride, stride).start()
        copy_of(*last_chunk).start()

        lane = lanes_of((flat, LANES))
        row = lax.broadcasted_iota(jnp.int32, (flat, LANES), 0)
        last = columns // LANES * LANES

        def begins(j):
            start = (2 * j + core) * piece
            base = start // LANES * LANES
            return pl.multiple_of(base, LANES), start - base

        def widen(j, earlier):
            value = own[j].astype(jnp.float32)
            for t in range(texts):
                part = value[t * positions : (t + 1) * positions]
                pub[t, :, pl.ds(pl.multiple_of(j * WINDOW, LANES), WIDE)] = part
                pub[t, :, pl.ds(pl.multiple_of(j * WINDOW + WIDE, LANES), LANES)] = part[:, :LANES]
            shift = begins(j)[1]
            free = jnp.where(shift == 0, LANES - 1, shift - 1)
            tile = jnp.where(shift == 0, tile_of(value, TILES - 1), tile_of(value, 0))
            free = jnp.where(j < chip, free, LANES)
            return earlier + jnp.where(lane == free, tile, 0.0)

        earlier = lax.fori_loop(
            0, chips, widen, jnp.zeros((flat, LANES), jnp.float32), unroll=4
        )
        for t in range(texts):
            here = jnp.where(row == t * positions, earlier, 0.0)
            left[t] = counts[t] - jnp.sum(here).astype(jnp.int32)

        slots = [[None] * rows, [None] * rows]
        for c in range(2):
            for r in range(rows):
                text = jnp.where(core == c, owner[r], partner[r])
                still = left[text]
                left[text] = still - 1
                slots[c][r] = jnp.where(still > 0, text, texts)
        acc[texts] = jnp.zeros(acc.shape[1:], jnp.float32)

        def accumulate(first, many, size):
            places = [first + g for g in range(many)]
            bases = [begins(j)[0] for j in places]
            for t in range(texts):
                for g in range(many):
                    acc[t, :, g * WINDOW : g * WINDOW + size[g]] = jnp.zeros(
                        (positions, size[g]), jnp.float32
                    )
            for r in range(rows):
                for held, text, c in (
                    (priv, owner[r], core),
                    (swapped, partner[r], 1 - core),
                ):
                    slot = jnp.where(c == 0, slots[0][r], slots[1][r])
                    for g, j in enumerate(places):
                        at = pl.multiple_of(j * WINDOW, LANES)
                        value = held[r, :, pl.ds(bases[g], size[g])].astype(jnp.float32)
                        value = value - pub[text, :, pl.ds(at, size[g])]
                        value = jnp.clip(value, -clip_bound, clip_bound)
                        where = slice(g * WINDOW, g * WINDOW + size[g])
                        acc[slot, :, where] = acc[slot, :, where] + value
            for g, j in enumerate(places):
                shift = begins(j)[1]
                tiles = [
                    jnp.concatenate(
                        [
                            acc[t, :, g * WINDOW + k * LANES : g * WINDOW + (k + 1) * LANES]
                            for t in range(texts)
                        ],
                        axis=0,
                    )
                    for k in range(TILES + 1)
                ]
                tiles[0] = jnp.where(lane >= shift, tiles[0], tiles[TILES])
                for k in range(TILES):
                    fixed = jnp.round(tiles[k] * scale).astype(jnp.int32).astype(jnp.int16)
                    out[j, :, k * LANES : (k + 1) * LANES] = fixed

        def some(i, carry):
            copy_of(i, pl.multiple_of(LEAD + i * stride, LANES), stride).wait()
            accumulate(i * GROUP, GROUP, [WINDOW] * GROUP)
            return carry

        copy_of(*first_chunk).wait()
        accumulate(jnp.int32(0), GROUP, [WINDOW] * GROUP)
        lax.fori_loop(1, groups - 1, some, 0)
        copy_of(*last_chunk).wait()
        accumulate(chips - GROUP, GROUP - 1, [WINDOW] * (GROUP - 1))
        for c in range(2):
            start = (2 * chips - 2 + c) * piece // LANES * LANES

            @pl.when(core == c)
            def _():
                accumulate(jnp.int32(chips - 1), 1, [min(WINDOW, columns - start)])

    return kernel


def chip_sums(private_logits, swapped, own, owner, partner, counts, ids, piece, scale):
    rows, positions, columns = private_logits.shape
    texts = counts.shape[0]
    chips, flat, wide = own.shape
    return pl.pallas_call(
        sums_kernel(piece, scale),
        out_shape=pltpu.VMEM((chips, flat, wide), jnp.int16),
        in_specs=[SMEM, SMEM, SMEM, SMEM, HBM, VMEM, VMEM],
        out_specs=VMEM,
        scratch_shapes=[
            pltpu.VMEM(private_logits.shape, private_logits.dtype),
            pltpu.VMEM((texts, positions, chips * WINDOW), jnp.float32),
            pltpu.VMEM((texts + 1, positions, GROUP * WINDOW), jnp.float32),
            pltpu.SMEM((texts,), jnp.int32),
            pltpu.SemaphoreType.DMA((chips // GROUP,)),
        ],
        compiler_params=PARAMS,
        name="chip_sums",
    )(owner, partner, counts, ids, private_logits, swapped, own)


def prepare_kernel(inverse):
    def kernel(public, noise, counts, tokens, ids, base, chosen, level, scale, scratch):
        texts, positions, piece = public.shape
        flat = texts * positions
        square = (flat, LANES)
        lane = lanes_of(square)
        row = lax.broadcasted_iota(jnp.int32, square, 0)
        factor = jnp.zeros(square, jnp.float32)
        token = jnp.zeros(square, jnp.int32)
        for t in range(texts):
            inside = (row >= t * positions) & (row < (t + 1) * positions)
            number = jnp.where(inside, counts[t].astype(jnp.float32), 1.0)
            factor = jnp.where(inside, inverse / (clip_bound * jnp.sqrt(number)), factor)
            for p in range(positions):
                token = jnp.where(row == t * positions + p, tokens[t, p], token)
        scale[...] = factor
        token = token - ids[FIRST]
        public_tiles = turned(rows_of(public, scratch.at[0]), ids[SHIFT], lane)
        noise_tiles = turned(rows_of(noise, scratch.at[1]), ids[SHIFT], lane)
        top = jnp.full(square, -jnp.inf, jnp.float32)
        for k in range(TILES):
            column = column_of(lane, k, ids[SHIFT])
            inside = column < piece
            part = slice(k * LANES, (k + 1) * LANES)
            top = jnp.maximum(top, jnp.where(inside, public_tiles[k], -jnp.inf))
            base[:, part] = jnp.where(inside, public_tiles[k] + noise_tiles[k], -jnp.inf)
            chosen[:, part] = jnp.where(inside & (column == token), 1.0, 0.0)
        level[...] = jnp.broadcast_to(jnp.max(top, axis=1, keepdims=True), square)

    return kernel


def finish_kernel(parts, base, chosen, level, scale, combined, stats):
    flat = base.shape[0]
    square = (flat, LANES)
    lane = lanes_of(square)
    row = lax.broadcasted_iota(jnp.int32, square, 0)
    terms = jnp.zeros(square, jnp.float32)
    picked = jnp.zeros(square, jnp.float32)
    for k in range(TILES):
        part = slice(k * LANES, (k + 1) * LANES)
        total = parts[0, :, part].astype(jnp.int32)
        for j in range(1, parts.shape[0]):
            total = total + parts[j, :, part].astype(jnp.int32)
        tile = base[:, part] + total.astype(jnp.float32) * scale[...]
        combined[:, part] = tile
        terms = terms + jnp.exp(tile - level[...])
        picked = picked + jnp.where(chosen[:, part] > 0.0, tile, 0.0)
    terms = jnp.sum(terms, axis=1, keepdims=True)
    picked = jnp.sum(picked, axis=1, keepdims=True)
    spread = jnp.where(lane == row, terms, 0.0)
    spread = spread + jnp.where(lane == row + flat, picked, 0.0)
    spread = spread + jnp.where(lane == row + 2 * flat, level[...], 0.0)
    stats[...] = jnp.sum(spread, axis=0, keepdims=True)


def untwist_kernel(combined, ids, out):
    lane = lanes_of((combined.shape[0], LANES))
    values = combined[...]
    tiles = turned_back([tile_of(values, k) for k in range(TILES)], ids[SHIFT], lane)
    for k in range(TILES):
        out[:, k * LANES : (k + 1) * LANES] = tiles[k]


def last_kernel(everyone, combined, logprobs, target):
    texts, positions, piece = logprobs.shape
    flat = texts * positions
    values = everyone[...]
    lane = lanes_of((1, LANES))
    level = jnp.max(values, axis=0, keepdims=True)
    weight = pltpu.roll(jnp.exp(values - level), LANES - 2 * flat, 1)
    total = jnp.sum(values * weight, axis=0, keepdims=True)
    picked = pltpu.roll(jnp.sum(values, axis=0, keepdims=True), LANES - flat, 1)
    level = pltpu.roll(level, LANES - 2 * flat, 1)
    own = lane < flat
    lse = jnp.where(own, level + jnp.log(jnp.where(own, total, 1.0)), 0.0)
    picked = picked - lse
    square = (flat, LANES)
    mine = lanes_of(square) == lax.broadcasted_iota(jnp.int32, square, 0)
    column = jnp.sum(jnp.where(mine, jnp.broadcast_to(lse, square), 0.0), axis=1, keepdims=True)
    shifted = combined[:, :piece] - column
    for t in range(texts):
        logprobs[t] = shifted[t * positions : (t + 1) * positions]
    for t in range(texts):
        turn = picked if t == 0 else pltpu.roll(picked, LANES - t * positions, 1)
        target[t : t + 1, :] = turn[:, :positions]


def body(private_logits, public_logits, noise, owner, counts, tokens):
    texts, positions, piece = public_logits.shape
    rows = owner.shape[0]
    flat = texts * positions
    chips = lax.axis_size(CHIP)
    chip, core = lax.axis_index(CHIP), lax.axis_index(CORE)
    swap = [(0, 1), (1, 0)]
    scale = float(32767 // (2 * rows * int(clip_bound)))
    place = lax.axis_index(REF)
    first_column = (lax.axis_index("voc") * lax.axis_size(REF) + place) * piece
    ids = jnp.stack([chip, core, place * piece % LANES, first_column]).astype(jnp.int32)
    owner_there, counts_there, tokens_there, public_there = (
        pltpu.with_memory_space_constraint(x, pltpu.HBM)
        for x in (owner, counts, tokens, public_logits)
    )

    partner = lax.ppermute(owner, CORE, swap)
    one = pl.pallas_call(
        turn_kernel,
        out_shape=pltpu.VMEM((flat, WIDE), jnp.float32),
        in_specs=[VMEM, SMEM],
        out_specs=VMEM,
        scratch_shapes=[pltpu.VMEM((flat, WIDE), jnp.float32)],
        compiler_params=PARAMS,
        name="turn",
    )(public_there, ids)
    partner, private_later, one = lax.optimization_barrier((partner, private_logits, one))
    swapped = lax.ppermute(private_later, CORE, swap)
    packed = pl.pallas_call(
        mark_kernel(piece, positions),
        out_shape=pltpu.VMEM((chips, flat, WIDE), jnp.bfloat16),
        in_specs=[VMEM, SMEM, SMEM, SMEM],
        out_specs=VMEM,
        compiler_params=PARAMS,
        name="mark",
    )(one, owner_there, partner, ids)
    own = lax.all_to_all(packed, CHIP, split_axis=0, concat_axis=0, tiled=True)
    swapped, own = (pltpu.with_memory_space_constraint(x, pltpu.VMEM) for x in (swapped, own))
    source = pltpu.with_memory_space_constraint(private_logits, pltpu.HBM)
    sums = chip_sums(
        source, swapped, own, owner_there, partner, counts_there, ids, piece, scale
    )
    sums, public_later, noise_later = lax.optimization_barrier((sums, public_logits, noise))
    parts = lax.all_to_all(sums, CHIP, split_axis=0, concat_axis=0, tiled=True)
    public_later, noise_later = (
        pltpu.with_memory_space_constraint(x, pltpu.HBM) for x in (public_later, noise_later)
    )
    square = pltpu.VMEM((flat, LANES), jnp.float32)
    long = pltpu.VMEM((flat, WIDE), jnp.float32)
    base, chosen, level, factor = pl.pallas_call(
        prepare_kernel(1.0 / scale),
        out_shape=(long, long, square, square),
        in_specs=[VMEM, VMEM, SMEM, SMEM, SMEM],
        out_specs=(VMEM, VMEM, VMEM, VMEM),
        scratch_shapes=[pltpu.VMEM((2, flat, WIDE), jnp.float32)],
        compiler_params=PARAMS,
        name="prepare",
    )(public_later, noise_later, counts_there, tokens_there, ids)

    parts = pltpu.with_memory_space_constraint(parts, pltpu.VMEM)
    combined, stats = pl.pallas_call(
        finish_kernel,
        out_shape=(long, pltpu.VMEM((1, LANES), jnp.float32)),
        in_specs=[VMEM, VMEM, VMEM, VMEM, VMEM],
        out_specs=(VMEM, VMEM),
        compiler_params=PARAMS,
        name="finish",
    )(parts, base, chosen, level, factor)

    devices = lax.axis_size(REF_VOC)
    everyone = lax.all_to_all(
        jnp.broadcast_to(stats, (devices, 1, LANES)), REF_VOC, split_axis=0, concat_axis=0, tiled=True
    ).reshape(devices, LANES)
    combined = pl.pallas_call(
        untwist_kernel,
        out_shape=long,
        in_specs=[VMEM, SMEM],
        out_specs=VMEM,
        compiler_params=PARAMS,
        name="untwist",
    )(combined, ids)
    return pl.pallas_call(
        last_kernel,
        out_shape=(
            jax.ShapeDtypeStruct(public_logits.shape, jnp.float32),
            jax.ShapeDtypeStruct((texts, positions), jnp.float32),
        ),
        in_specs=[VMEM, VMEM],
        out_specs=(VMEM, VMEM),
        compiler_params=PARAMS,
        name="last",
    )(pltpu.with_memory_space_constraint(everyone, pltpu.VMEM), combined)


def solution(mesh):
    finer = Mesh(
        mesh.devices.reshape(8, 4, 2, mesh.shape["voc"]), ("ref_0", "ref_1", "ref_2", "voc")
    )
    placed = (P(REF, None, "voc"), P(None, None, VOC_REF), P(None, None, VOC_REF), P(REF), P(), P())
    return jax.shard_map(
        body, mesh=finer, in_specs=placed, out_specs=(P(None, None, VOC_REF), P()), check_vma=False
    )
```

```python
import jax
import jax.numpy as jnp
from jax import lax
from jax.experimental import pallas as pl
from jax.experimental.pallas import tpu as pltpu
from jax.sharding import Mesh
from jax.sharding import PartitionSpec as P

REF_VOC = ("ref_0", "ref_1", "ref_2", "voc")
REF = ("ref_0", "ref_1", "ref_2")
CHIP = ("ref_0", "ref_1")
CORE = "ref_2"
VOC_REF = ("voc", "ref_0", "ref_1", "ref_2")

clip_bound = 2.0

LANES = 128
WIDE = 512
TILES = WIDE // LANES
WINDOW = WIDE + LANES
GROUP = 4
LEAD = LANES

PARAMS = pltpu.CompilerParams(vmem_limit_bytes=16 << 20)
SMEM = pl.BlockSpec(memory_space=pltpu.SMEM)
VMEM = pl.BlockSpec(memory_space=pltpu.VMEM)
HBM = pl.BlockSpec(memory_space=pltpu.HBM)


def tile_of(x, k):
    return x[:, k * LANES : (k + 1) * LANES]


def turned(tiles, shift, lane):
    spun = [pltpu.roll(tile, shift, 1) for tile in tiles]
    return [jnp.where(lane >= shift, spun[k], spun[k - 1]) for k in range(TILES)]


def turned_back(tiles, shift, lane):
    back = LANES - shift
    spun = [pltpu.roll(tile, back, 1) for tile in tiles]
    return [jnp.where(lane < back, spun[k], spun[(k + 1) % TILES]) for k in range(TILES)]


def lanes_of(shape):
    return lax.broadcasted_iota(jnp.int32, shape, len(shape) - 1)


def rows_of(array, scratch):
    texts, positions, piece = array.shape
    for t in range(texts):
        part = slice(t * positions, (t + 1) * positions)
        scratch[part, :piece] = array[t].astype(jnp.float32)
    values = scratch[...]
    lane = lanes_of((texts * positions, LANES))
    return [
        jnp.where(lane + k * LANES < piece, tile_of(values, k), 0.0) for k in range(TILES)
    ]


def column_of(lane, k, shift):
    return (lane + k * LANES - shift) & (WIDE - 1)


def place_of(sizes):
    chip = lax.axis_index("ref_0") * sizes[1] + lax.axis_index("ref_1")
    return chip, lax.axis_index("ref_2")


def turn_of(sizes, piece):
    chip, core = place_of(sizes)
    return ((2 * chip + core) * piece) & (LANES - 1)


def inside_text(row, t, positions):
    return (row >= t * positions) & (row < (t + 1) * positions)


def turn_kernel(sizes):
    def kernel(public, near, out, number, scratch):
        texts, positions, piece = public.shape
        square = number.shape
        lane = lanes_of(square)
        row = lax.broadcasted_iota(jnp.int32, square, 0)
        shift = turn_of(sizes, piece)
        for k, tile in enumerate(turned(rows_of(public, scratch), shift, lane)):
            out[:, k * LANES : (k + 1) * LANES] = tile
        many = jnp.zeros(square, jnp.float32)
        for t in range(texts):
            held = jnp.int32(0)
            for r in range(near.shape[0]):
                held += jnp.where(near[r] == t, 1, 0)
            many = jnp.where(inside_text(row, t, positions), held.astype(jnp.float32), many)
        number[...] = many

    return kernel


def mark_kernel(sizes, piece, positions):
    def kernel(one, number, far, out):
        square = number.shape
        row = lax.broadcasted_iota(jnp.int32, square, 0)
        lane = lanes_of(square)
        shift = turn_of(sizes, piece)
        many = number[...]
        for t in range(square[0] // positions):
            held = jnp.sum(jnp.where(far[...] == t, 1.0, 0.0), axis=1, keepdims=True)
            held = jnp.broadcast_to(held, square)
            many = many + jnp.where(inside_text(row, t, positions), held, 0.0)
        for k in range(TILES):
            tile = one[:, k * LANES : (k + 1) * LANES]
            tile = jnp.where(column_of(lane, k, shift) < piece, tile, many)
            tile = tile.astype(out.dtype)
            for j in range(out.shape[0]):
                out[j, :, k * LANES : (k + 1) * LANES] = tile

    return kernel


def sums_kernel(sizes, scale):
    def kernel(
        owner_there, partner_there, counts_there, tokens_there, public_there, noise_there,
        source, swapped, own,
        out, base, chosen, level, factor,
        priv, pub, acc, public, noise, scratch, owner, partner, counts, tokens, left, arrived, small,
    ):
        piece = public.shape[2]
        rows, positions, columns = priv.shape
        texts = pub.shape[0]
        chips, flat, _ = own.shape
        groups = chips // GROUP
        chip, core = place_of(sizes)

        stride = 2 * GROUP * piece
        stride = -(-stride // LANES) * LANES

        def copy_of(i, start, width):
            return pltpu.make_async_copy(
                source.at[:, :, pl.ds(start, width)],
                priv.at[:, :, pl.ds(start, width)],
                arrived.at[i],
            )

        first_chunk = (0, 0, stride + LEAD)
        last_start = LEAD + (groups - 1) * stride
        last_chunk = (groups - 1, last_start, columns - last_start)
        pairs = (
            (owner_there, owner),
            (partner_there, partner),
            (counts_there, counts),
            (tokens_there, tokens),
            (public_there, public),
            (noise_there, noise),
        )
        little = [
            pltpu.make_async_copy(there, here, small.at[i]) for i, (there, here) in enumerate(pairs)
        ]
        for copy in little:
            copy.start()
        copy_of(*first_chunk).start()
        for i in range(1, groups - 1):
            copy_of(i, LEAD + i * stride, stride).start()
        copy_of(*last_chunk).start()

        lane = lanes_of((flat, LANES))
        row = lax.broadcasted_iota(jnp.int32, (flat, LANES), 0)
        last = columns // LANES * LANES

        def begins(j):
            start = (2 * j + core) * piece
            base = start // LANES * LANES
            return pl.multiple_of(base, LANES), start - base

        def widen(j, earlier):
            value = own[j].astype(jnp.float32)
            for t in range(texts):
                part = value[t * positions : (t + 1) * positions]
                pub[t, :, pl.ds(pl.multiple_of(j * WINDOW, LANES), WIDE)] = part
                pub[t, :, pl.ds(pl.multiple_of(j * WINDOW + WIDE, LANES), LANES)] = part[:, :LANES]
            shift = begins(j)[1]
            free = jnp.where(shift == 0, LANES - 1, shift - 1)
            tile = jnp.where(shift == 0, tile_of(value, TILES - 1), tile_of(value, 0))
            free = jnp.where(j < chip, free, LANES)
            return earlier + jnp.where(lane == free, tile, 0.0)

        earlier = lax.fori_loop(
            0, chips, widen, jnp.zeros((flat, LANES), jnp.float32), unroll=4
        )
        for copy in little:
            copy.wait()
        prepare(sizes, scale, public, noise, counts, tokens, scratch, base, chosen, level, factor)

        for t in range(texts):
            here = jnp.where(row == t * positions, earlier, 0.0)
            left[t] = counts[t] - jnp.sum(here).astype(jnp.int32)

        slots = [[None] * rows, [None] * rows]
        for c in range(2):
            for r in range(rows):
                text = jnp.where(core == c, owner[r], partner[r])
                still = left[text]
                left[text] = still - 1
                slots[c][r] = jnp.where(still > 0, text, texts)
        acc[texts] = jnp.zeros(acc.shape[1:], jnp.float32)

        def accumulate(first, many, size):
            places = [first + g for g in range(many)]
            bases = [begins(j)[0] for j in places]
            for t in range(texts):
                for g in range(many):
                    acc[t, :, g * WINDOW : g * WINDOW + size[g]] = jnp.zeros(
                        (positions, size[g]), jnp.float32
                    )
            for r in range(rows):
                for held, text, c in (
                    (priv, owner[r], core),
                    (swapped, partner[r], 1 - core),
                ):
                    slot = jnp.where(c == 0, slots[0][r], slots[1][r])
                    for g, j in enumerate(places):
                        at = pl.multiple_of(j * WINDOW, LANES)
                        value = held[r, :, pl.ds(bases[g], size[g])].astype(jnp.float32)
                        value = value - pub[text, :, pl.ds(at, size[g])]
                        value = jnp.clip(value, -clip_bound, clip_bound)
                        where = slice(g * WINDOW, g * WINDOW + size[g])
                        acc[slot, :, where] = acc[slot, :, where] + value
            for g, j in enumerate(places):
                shift = begins(j)[1]
                tiles = [
                    jnp.concatenate(
                        [
                            acc[t, :, g * WINDOW + k * LANES : g * WINDOW + (k + 1) * LANES]
                            for t in range(texts)
                        ],
                        axis=0,
                    )
                    for k in range(TILES + 1)
                ]
                tiles[0] = jnp.where(lane >= shift, tiles[0], tiles[TILES])
                for k in range(TILES):
                    fixed = jnp.round(tiles[k] * scale).astype(jnp.int32).astype(jnp.int16)
                    out[j, :, k * LANES : (k + 1) * LANES] = fixed

        def some(i, carry):
            copy_of(i, pl.multiple_of(LEAD + i * stride, LANES), stride).wait()
            accumulate(i * GROUP, GROUP, [WINDOW] * GROUP)
            return carry

        copy_of(*first_chunk).wait()
        accumulate(jnp.int32(0), GROUP, [WINDOW] * GROUP)
        lax.fori_loop(1, groups - 1, some, 0)
        copy_of(*last_chunk).wait()
        accumulate(chips - GROUP, GROUP - 1, [WINDOW] * (GROUP - 1))
        for c in range(2):
            start = (2 * chips - 2 + c) * piece // LANES * LANES

            @pl.when(core == c)
            def _():
                accumulate(jnp.int32(chips - 1), 1, [min(WINDOW, columns - start)])

    return kernel


def chip_sums(sizes, owner, partner, counts, tokens, public, noise, source, swapped, own, scale):
    rows, positions, columns = source.shape
    texts = counts.shape[0]
    chips, flat, wide = own.shape
    long = pltpu.VMEM((flat, wide), jnp.float32)
    square = pltpu.VMEM((flat, LANES), jnp.float32)
    return pl.pallas_call(
        sums_kernel(sizes, scale),
        out_shape=(pltpu.VMEM((chips, flat, wide), jnp.int16), long, long, square, square),
        in_specs=[HBM, VMEM, HBM, HBM, HBM, HBM, HBM, VMEM, VMEM],
        out_specs=(VMEM,) * 5,
        scratch_shapes=[
            pltpu.VMEM(source.shape, source.dtype),
            pltpu.VMEM((texts, positions, chips * WINDOW), jnp.float32),
            pltpu.VMEM((texts + 1, positions, GROUP * WINDOW), jnp.float32),
            pltpu.VMEM(public.shape, public.dtype),
            pltpu.VMEM(noise.shape, noise.dtype),
            pltpu.VMEM((2, flat, wide), jnp.float32),
            pltpu.SMEM((rows,), jnp.int32),
            pltpu.SMEM((rows,), jnp.int32),
            pltpu.SMEM((texts,), jnp.int32),
            pltpu.SMEM((texts, positions), jnp.int32),
            pltpu.SMEM((texts,), jnp.int32),
            pltpu.SemaphoreType.DMA((chips // GROUP,)),
            pltpu.SemaphoreType.DMA((6,)),
        ],
        compiler_params=PARAMS,
        name="chip_sums",
    )(owner, partner, counts, tokens, public, noise, source, swapped, own)


def prepare(sizes, scale_of, public, noise, counts, tokens, scratch, base, chosen, level, factor):
    texts, positions, piece = public.shape
    square = (texts * positions, LANES)
    lane = lanes_of(square)
    row = lax.broadcasted_iota(jnp.int32, square, 0)
    shift = turn_of(sizes, piece)
    chip, core = place_of(sizes)
    chips = sizes[0] * sizes[1]
    first = (lax.axis_index("voc") * 2 * chips + 2 * chip + core) * piece
    number = jnp.ones(square, jnp.float32)
    token = jnp.zeros(square, jnp.int32)
    for t in range(texts):
        number = jnp.where(inside_text(row, t, positions), counts[t].astype(jnp.float32), number)
        for p in range(positions):
            token = jnp.where(row == t * positions + p, tokens[t, p] - first, token)
    factor[...] = (1.0 / scale_of) / (clip_bound * jnp.sqrt(number))
    public_tiles = turned(rows_of(public, scratch.at[0]), shift, lane)
    noise_tiles = turned(rows_of(noise, scratch.at[1]), shift, lane)
    top = jnp.full(square, -jnp.inf, jnp.float32)
    for k in range(TILES):
        column = column_of(lane, k, shift)
        inside = column < piece
        part = slice(k * LANES, (k + 1) * LANES)
        top = jnp.maximum(top, jnp.where(inside, public_tiles[k], -jnp.inf))
        base[:, part] = jnp.where(inside, public_tiles[k] + noise_tiles[k], -jnp.inf)
        chosen[:, part] = jnp.where(inside & (column == token), 1.0, 0.0)
    level[...] = jnp.broadcast_to(jnp.max(top, axis=1, keepdims=True), square)


def finish_kernel(parts, base, chosen, level, scale, combined, stats):
    flat = base.shape[0]
    square = (flat, LANES)
    lane = lanes_of(square)
    row = lax.broadcasted_iota(jnp.int32, square, 0)
    terms = jnp.zeros(square, jnp.float32)
    picked = jnp.zeros(square, jnp.float32)
    for k in range(TILES):
        part = slice(k * LANES, (k + 1) * LANES)
        total = parts[0, :, part].astype(jnp.int32)
        for j in range(1, parts.shape[0]):
            total = total + parts[j, :, part].astype(jnp.int32)
        tile = base[:, part] + total.astype(jnp.float32) * scale[...]
        combined[:, part] = tile
        terms = terms + jnp.exp(tile - level[...])
        picked = picked + jnp.where(chosen[:, part] > 0.0, tile, 0.0)
    terms = jnp.sum(terms, axis=1, keepdims=True)
    picked = jnp.sum(picked, axis=1, keepdims=True)
    spread = jnp.where(lane == row, terms, 0.0)
    spread = spread + jnp.where(lane == row + flat, picked, 0.0)
    spread = spread + jnp.where(lane == row + 2 * flat, level[...], 0.0)
    stats[...] = jnp.sum(spread, axis=0, keepdims=True)


def last_kernel(sizes):
    def kernel(everyone, combined, logprobs, target, natural):
        texts, positions, piece = logprobs.shape
        flat = texts * positions
        values = everyone[...]
        lane = lanes_of((1, LANES))
        level = jnp.max(values, axis=0, keepdims=True)
        weight = pltpu.roll(jnp.exp(values - level), LANES - 2 * flat, 1)
        total = jnp.sum(values * weight, axis=0, keepdims=True)
        picked = pltpu.roll(jnp.sum(values, axis=0, keepdims=True), LANES - flat, 1)
        level = pltpu.roll(level, LANES - 2 * flat, 1)
        own = lane < flat
        lse = jnp.where(own, level + jnp.log(jnp.where(own, total, 1.0)), 0.0)
        picked = picked - lse
        square = (flat, LANES)
        mine = lanes_of(square) == lax.broadcasted_iota(jnp.int32, square, 0)
        column = jnp.sum(jnp.where(mine, jnp.broadcast_to(lse, square), 0.0), axis=1, keepdims=True)
        tiles = [combined[:, k * LANES : (k + 1) * LANES] - column for k in range(TILES)]
        for k, tile in enumerate(turned_back(tiles, turn_of(sizes, piece), lanes_of(square))):
            natural[:, k * LANES : (k + 1) * LANES] = tile
        shifted = natural[:, :piece]
        for t in range(texts):
            logprobs[t] = shifted[t * positions : (t + 1) * positions]
        for t in range(texts):
            turn = picked if t == 0 else pltpu.roll(picked, LANES - t * positions, 1)
            target[t : t + 1, :] = turn[:, :positions]

    return kernel


def body(private_logits, public_logits, noise, owner, counts, tokens):
    texts, positions, piece = public_logits.shape
    rows = owner.shape[0]
    flat = texts * positions
    sizes = (lax.axis_size("ref_0"), lax.axis_size("ref_1"))
    chips = sizes[0] * sizes[1]
    swap = [(0, 1), (1, 0)]
    scale = float(32767 // (2 * rows * int(clip_bound)))
    square = pltpu.VMEM((flat, LANES), jnp.float32)
    long = pltpu.VMEM((flat, WIDE), jnp.float32)
    owner_there, counts_there, tokens_there, public_there, noise_there, private_there = (
        pltpu.with_memory_space_constraint(x, pltpu.HBM)
        for x in (owner, counts, tokens, public_logits, noise, private_logits)
    )

    partner = lax.ppermute(owner, CORE, swap)
    one, number = pl.pallas_call(
        turn_kernel(sizes),
        out_shape=(long, square),
        in_specs=[VMEM, SMEM],
        out_specs=(VMEM, VMEM),
        scratch_shapes=[pltpu.VMEM((flat, WIDE), jnp.float32)],
        compiler_params=PARAMS,
        name="turn",
    )(public_there, owner_there)
    partner, private_later, one = lax.optimization_barrier((partner, private_logits, one))
    swapped = lax.ppermute(private_later, CORE, swap)
    packed = pl.pallas_call(
        mark_kernel(sizes, piece, positions),
        out_shape=pltpu.VMEM((chips, flat, WIDE), jnp.bfloat16),
        in_specs=[VMEM, VMEM, VMEM],
        out_specs=VMEM,
        compiler_params=PARAMS,
        name="mark",
    )(one, number, partner.reshape(1, rows))
    own = lax.all_to_all(packed, CHIP, split_axis=0, concat_axis=0, tiled=True)
    swapped, own, partner = (
        pltpu.with_memory_space_constraint(x, pltpu.VMEM) for x in (swapped, own, partner)
    )
    sums, base, chosen, level, factor = chip_sums(
        sizes, owner_there, partner, counts_there, tokens_there, public_there, noise_there,
        private_there, swapped, own, scale,
    )
    parts = lax.all_to_all(sums, CHIP, split_axis=0, concat_axis=0, tiled=True)
    parts = pltpu.with_memory_space_constraint(parts, pltpu.VMEM)
    combined, stats = pl.pallas_call(
        finish_kernel,
        out_shape=(long, pltpu.VMEM((1, LANES), jnp.float32)),
        in_specs=[VMEM] * 5,
        out_specs=(VMEM, VMEM),
        compiler_params=PARAMS,
        name="finish",
    )(parts, base, chosen, level, factor)

    devices = lax.axis_size(REF_VOC)
    everyone = lax.all_to_all(
        jnp.broadcast_to(stats, (devices, 1, LANES)), REF_VOC, split_axis=0, concat_axis=0, tiled=True
    ).reshape(devices, LANES)
    return pl.pallas_call(
        last_kernel(sizes),
        out_shape=(
            jax.ShapeDtypeStruct(public_logits.shape, jnp.float32),
            jax.ShapeDtypeStruct((texts, positions), jnp.float32),
        ),
        in_specs=[VMEM, VMEM],
        out_specs=(VMEM, VMEM),
        scratch_shapes=[pltpu.VMEM((flat, WIDE), jnp.float32)],
        compiler_params=PARAMS,
        name="last",
    )(pltpu.with_memory_space_constraint(everyone, pltpu.VMEM), combined)


def solution(mesh):
    finer = Mesh(
        mesh.devices.reshape(8, 4, 2, mesh.shape["voc"]), ("ref_0", "ref_1", "ref_2", "voc")
    )
    placed = (P(REF, None, "voc"), P(None, None, VOC_REF), P(None, None, VOC_REF), P(REF), P(), P())
    return jax.shard_map(
        body, mesh=finer, in_specs=placed, out_specs=(P(None, None, VOC_REF), P()), check_vma=False
    )
```

```python
import jax
import jax.numpy as jnp
from jax import lax
from jax.experimental import pallas as pl
from jax.experimental.pallas import tpu as pltpu
from jax.sharding import Mesh
from jax.sharding import PartitionSpec as P

REF_VOC = ("ref_0", "ref_1", "ref_2", "voc")
REF = ("ref_0", "ref_1", "ref_2")
CHIP = ("ref_0", "ref_1")
CORE = "ref_2"
VOC_REF = ("voc", "ref_0", "ref_1", "ref_2")

clip_bound = 2.0

LANES = 128
WIDE = 512
TILES = WIDE // LANES
WINDOW = WIDE + LANES
GROUP = 4
AROUND = (2, 1, 3, 0)
LEAD = LANES

PARAMS = pltpu.CompilerParams(vmem_limit_bytes=16 << 20)
SMEM = pl.BlockSpec(memory_space=pltpu.SMEM)
VMEM = pl.BlockSpec(memory_space=pltpu.VMEM)
HBM = pl.BlockSpec(memory_space=pltpu.HBM)


def tile_of(x, k):
    return x[:, k * LANES : (k + 1) * LANES]


def turned(tiles, shift, lane):
    spun = [pltpu.roll(tile, shift, 1) for tile in tiles]
    return [jnp.where(lane >= shift, spun[k], spun[k - 1]) for k in range(TILES)]


def turned_back(tiles, shift, lane):
    back = LANES - shift
    spun = [pltpu.roll(tile, back, 1) for tile in tiles]
    return [jnp.where(lane < back, spun[k], spun[(k + 1) % TILES]) for k in range(TILES)]


def lanes_of(shape):
    return lax.broadcasted_iota(jnp.int32, shape, len(shape) - 1)


def rows_of(array, scratch):
    texts, positions, piece = array.shape
    for t in range(texts):
        part = slice(t * positions, (t + 1) * positions)
        scratch[part, :piece] = array[t].astype(jnp.float32)
    values = scratch[...]
    lane = lanes_of((texts * positions, LANES))
    return [
        jnp.where(lane + k * LANES < piece, tile_of(values, k), 0.0) for k in range(TILES)
    ]


def column_of(lane, k, shift):
    return (lane + k * LANES - shift) & (WIDE - 1)


def place_of(sizes):
    chip = lax.axis_index("ref_0") * sizes[1] + lax.axis_index("ref_1")
    return chip, lax.axis_index("ref_2")


def turn_of(sizes, piece):
    chip, core = place_of(sizes)
    return ((2 * chip + core) * piece) & (LANES - 1)


def inside_text(row, t, positions):
    return (row >= t * positions) & (row < (t + 1) * positions)


def turn_kernel(sizes):
    def kernel(public, near, out, number, scratch):
        texts, positions, piece = public.shape
        square = number.shape
        lane = lanes_of(square)
        row = lax.broadcasted_iota(jnp.int32, square, 0)
        shift = turn_of(sizes, piece)
        for k, tile in enumerate(turned(rows_of(public, scratch), shift, lane)):
            out[:, k * LANES : (k + 1) * LANES] = tile
        many = jnp.zeros(square, jnp.float32)
        for t in range(texts):
            held = jnp.int32(0)
            for r in range(near.shape[0]):
                held += jnp.where(near[r] == t, 1, 0)
            many = jnp.where(inside_text(row, t, positions), held.astype(jnp.float32), many)
        number[...] = many

    return kernel


def mark_kernel(sizes, piece, positions):
    def kernel(one, number, far, out):
        square = number.shape
        row = lax.broadcasted_iota(jnp.int32, square, 0)
        lane = lanes_of(square)
        shift = turn_of(sizes, piece)
        many = number[...]
        for t in range(square[0] // positions):
            held = jnp.sum(jnp.where(far[...] == t, 1.0, 0.0), axis=1, keepdims=True)
            held = jnp.broadcast_to(held, square)
            many = many + jnp.where(inside_text(row, t, positions), held, 0.0)
        for k in range(TILES):
            tile = one[:, k * LANES : (k + 1) * LANES]
            tile = jnp.where(column_of(lane, k, shift) < piece, tile, many)
            tile = tile.astype(out.dtype)
            for j in range(out.shape[0]):
                out[j, :, k * LANES : (k + 1) * LANES] = tile

    return kernel


class Rows:
    def __init__(self, plan, priv, swapped):
        rows, self.positions, self.columns = priv.shape
        self.entries = []
        for h, held in enumerate((priv, swapped)):
            for r in range(rows):
                at = h * rows + r
                self.entries.append((held, r, plan[at], plan[2 * rows + at]))

    def clipped(self, entry, start, pub, at, width):
        held, r, text, _ = entry
        value = held[r, :, pl.ds(start, width)].astype(jnp.float32)
        value = value - pub[text, :, pl.ds(at, width)]
        return jnp.clip(value, -clip_bound, clip_bound)


def begins(j, core, piece):
    start = (2 * j + core) * piece
    base = start // LANES * LANES
    return pl.multiple_of(base, LANES), start - base


def widen_into(pub, place, value, positions):
    for t in range(pub.shape[0]):
        part = value[t * positions : (t + 1) * positions]
        pub[t, :, pl.ds(pl.multiple_of(place * WINDOW, LANES), WIDE)] = part
        pub[t, :, pl.ds(pl.multiple_of(place * WINDOW + WIDE, LANES), LANES)] = part[:, :LANES]


def sum_windows(rows, pub, acc, core, piece, scale, windows, may_end=None):
    texts = pub.shape[0]
    sizes = [WIDE if may_end is not None and g in may_end else WINDOW for g in range(len(windows))]
    bases = [begins(j, core, piece)[0] for j, _, _ in windows]
    at = [pl.multiple_of(place * WINDOW, LANES) for _, place, _ in windows]
    for t in range(texts):
        for g, size in enumerate(sizes):
            acc[t, :, g * WINDOW : g * WINDOW + size] = jnp.zeros((rows.positions, size), jnp.float32)
    for entry in rows.entries:
        slot = entry[3]
        for g, size in enumerate(sizes):
            value = rows.clipped(entry, bases[g], pub, at[g], size)
            where = slice(g * WINDOW, g * WINDOW + size)
            acc[slot, :, where] = acc[slot, :, where] + value

    def edge(g, width):
        sums = [jnp.zeros((rows.positions, width), jnp.float32) for _ in range(texts)]
        start = pl.multiple_of(bases[g] + WIDE, LANES)
        for entry in rows.entries:
            value = rows.clipped(entry, start, pub, pl.multiple_of(at[g] + WIDE, LANES), width)
            for t in range(texts):
                sums[t] = sums[t] + jnp.where(entry[3] == t, value, 0.0)
        for t in range(texts):
            acc[t, :, g * WINDOW + WIDE : g * WINDOW + WIDE + width] = sums[t]

    for g in may_end or ():
        rest = rows.columns % LANES
        ends = bases[g] + WINDOW > rows.columns

        @pl.when(ends)
        def _():
            edge(g, rest)

        @pl.when(jnp.logical_not(ends))
        def _():
            edge(g, LANES)

    lane = lanes_of((texts * rows.positions, LANES))
    for g, (j, _, store) in enumerate(windows):
        shift = begins(j, core, piece)[1]
        tiles = [
            jnp.concatenate(
                [acc[t, :, g * WINDOW + k * LANES : g * WINDOW + (k + 1) * LANES] for t in range(texts)],
                axis=0,
            )
            for k in range(TILES + 1)
        ]
        tiles[0] = jnp.where(lane >= shift, tiles[0], tiles[TILES])
        for k in range(TILES):
            fixed = jnp.round(tiles[k] * scale).astype(jnp.int32).astype(jnp.int16)
            store(slice(k * LANES, (k + 1) * LANES), fixed)


def storing(out, index):
    def store(part, value):
        out[index, :, part] = value

    return store


def away_kernel(sizes, scale, piece):
    def kernel(
        owner_there, partner_there, counts_there, source, swapped, own,
        away_0, away_1, away_2, priv, plan,
        pub, acc, owner, partner, counts, left, arrived, small,
    ):
        rows, positions, columns = priv.shape
        texts = pub.shape[0]
        chips, flat, _ = own.shape
        lines, beside = sizes
        chip, core = place_of(sizes)
        mine = lax.axis_index("ref_1")
        lane = lanes_of((flat, LANES))
        row = lax.broadcasted_iota(jnp.int32, (flat, LANES), 0)

        stride = 2 * beside * piece
        stride = -(-stride // LANES) * LANES

        def copy_of(i, start, width):
            return pltpu.make_async_copy(
                source.at[:, :, pl.ds(start, width)],
                priv.at[:, :, pl.ds(start, width)],
                arrived.at[i],
            )

        first_chunk = (0, 0, stride + LEAD)
        last_start = LEAD + (lines - 1) * stride
        last_chunk = (lines - 1, last_start, columns - last_start)
        pairs = ((owner_there, owner), (partner_there, partner), (counts_there, counts))
        little = [
            pltpu.make_async_copy(there, here, small.at[i]) for i, (there, here) in enumerate(pairs)
        ]
        for copy in little:
            copy.start()
        copy_of(*first_chunk).start()
        for i in range(1, lines - 1):
            copy_of(i, LEAD + i * stride, stride).start()
        copy_of(*last_chunk).start()

        def widen(i, earlier):
            for n in range(beside):
                j = beside * i + (mine ^ AROUND[n])
                value = own[j].astype(jnp.float32)
                if n < beside - 1:
                    widen_into(pub, i * (beside - 1) + n, value, positions)
                shift = begins(j, core, piece)[1]
                free = jnp.where(shift == 0, LANES - 1, shift - 1)
                tile = jnp.where(shift == 0, tile_of(value, TILES - 1), tile_of(value, 0))
                free = jnp.where(j < chip, free, LANES)
                earlier = earlier + jnp.where(lane == free, tile, 0.0)
            return earlier

        earlier = lax.fori_loop(0, lines, widen, jnp.zeros((flat, LANES), jnp.float32))
        for copy in little:
            copy.wait()
        for t in range(texts):
            here = jnp.where(row == t * positions, earlier, 0.0)
            left[t] = counts[t] - jnp.sum(here).astype(jnp.int32)

        for c in range(2):
            for r in range(rows):
                text = jnp.where(core == c, owner[r], partner[r])
                still = left[text]
                left[text] = still - 1
                at = jnp.where(core == c, r, rows + r)
                plan[at] = text
                plan[2 * rows + at] = jnp.where(still > 0, text, texts)
        acc[texts] = jnp.zeros(acc.shape[1:], jnp.float32)
        held = Rows(plan, priv, swapped)
        outs = (away_0, away_1, away_2)

        def line(i, may_end=None):
            windows = [
                (beside * i + (mine ^ AROUND[n]), i * (beside - 1) + n, storing(outs[n], i))
                for n in range(beside - 1)
            ]
            sum_windows(held, pub, acc, core, piece, scale, windows, may_end)

        def some(i, carry):
            copy_of(i, pl.multiple_of(LEAD + i * stride, LANES), stride).wait()
            line(i)
            return carry

        copy_of(*first_chunk).wait()
        line(jnp.int32(0))
        lax.fori_loop(1, lines - 1, some, 0)
        copy_of(*last_chunk).wait()
        line(jnp.int32(lines - 1), range(beside - 1))

    return kernel


def own_kernel(sizes, scale, piece):
    def kernel(
        public, noise, counts, tokens, plan, priv, swapped, own,
        out, base, chosen, level, factor,
        pub, acc, scratch,
    ):
        texts = pub.shape[0]
        lines, beside = sizes
        chip, core = place_of(sizes)
        mine = lax.axis_index("ref_1")
        held = Rows(plan, priv, swapped)
        for i in range(lines):
            widen_into(pub, i, own[beside * i + mine].astype(jnp.float32), held.positions)
        acc[texts] = jnp.zeros(acc.shape[1:], jnp.float32)
        for first in range(0, lines, GROUP):
            windows = [(beside * i + mine, i, storing(out, i)) for i in range(first, first + GROUP)]
            may_end = (GROUP - 1,) if first + GROUP == lines else None
            sum_windows(held, pub, acc, core, piece, scale, windows, may_end)
        prepare(sizes, scale / beside, public, noise, counts, tokens, scratch, base, chosen, level, factor)

    return kernel


def join_kernel(a, b, c, d, out):
    for i in range(out.shape[0]):
        total = (a[i].astype(jnp.int32) + b[i].astype(jnp.int32)) + (
            c[i].astype(jnp.int32) + d[i].astype(jnp.int32)
        )
        total = jnp.round(total.astype(jnp.float32) * 0.25)
        out[i] = total.astype(jnp.int32).astype(jnp.int16)


def prepare(sizes, scale_of, public, noise, counts, tokens, scratch, base, chosen, level, factor):
    texts, positions, piece = public.shape
    square = (texts * positions, LANES)
    lane = lanes_of(square)
    row = lax.broadcasted_iota(jnp.int32, square, 0)
    shift = turn_of(sizes, piece)
    chip, core = place_of(sizes)
    chips = sizes[0] * sizes[1]
    first = (lax.axis_index("voc") * 2 * chips + 2 * chip + core) * piece
    number = jnp.ones(square, jnp.float32)
    token = jnp.zeros(square, jnp.int32)
    for t in range(texts):
        number = jnp.where(inside_text(row, t, positions), counts[t].astype(jnp.float32), number)
        for p in range(positions):
            token = jnp.where(row == t * positions + p, tokens[t, p] - first, token)
    factor[...] = (1.0 / scale_of) / (clip_bound * jnp.sqrt(number))
    public_tiles = turned(rows_of(public, scratch.at[0]), shift, lane)
    noise_tiles = turned(rows_of(noise, scratch.at[1]), shift, lane)
    top = jnp.full(square, -jnp.inf, jnp.float32)
    for k in range(TILES):
        column = column_of(lane, k, shift)
        inside = column < piece
        part = slice(k * LANES, (k + 1) * LANES)
        top = jnp.maximum(top, jnp.where(inside, public_tiles[k], -jnp.inf))
        base[:, part] = jnp.where(inside, public_tiles[k] + noise_tiles[k], -jnp.inf)
        chosen[:, part] = jnp.where(inside & (column == token), 1.0, 0.0)
    level[...] = jnp.broadcast_to(jnp.max(top, axis=1, keepdims=True), square)


def finish_kernel(parts, base, chosen, level, scale, combined, stats):
    flat = base.shape[0]
    square = (flat, LANES)
    lane = lanes_of(square)
    row = lax.broadcasted_iota(jnp.int32, square, 0)
    terms = jnp.zeros(square, jnp.float32)
    picked = jnp.zeros(square, jnp.float32)
    for k in range(TILES):
        part = slice(k * LANES, (k + 1) * LANES)
        total = parts[0, :, part].astype(jnp.int32)
        for j in range(1, parts.shape[0]):
            total = total + parts[j, :, part].astype(jnp.int32)
        tile = base[:, part] + total.astype(jnp.float32) * scale[...]
        combined[:, part] = tile
        terms = terms + jnp.exp(tile - level[...])
        picked = picked + jnp.where(chosen[:, part] > 0.0, tile, 0.0)
    terms = jnp.sum(terms, axis=1, keepdims=True)
    picked = jnp.sum(picked, axis=1, keepdims=True)
    spread = jnp.where(lane == row, terms, 0.0)
    spread = spread + jnp.where(lane == row + flat, picked, 0.0)
    spread = spread + jnp.where(lane == row + 2 * flat, level[...], 0.0)
    stats[...] = jnp.sum(spread, axis=0, keepdims=True)


def last_kernel(sizes):
    def kernel(everyone, combined, logprobs, target, natural):
        texts, positions, piece = logprobs.shape
        flat = texts * positions
        values = everyone[...]
        lane = lanes_of((1, LANES))
        level = jnp.max(values, axis=0, keepdims=True)
        weight = pltpu.roll(jnp.exp(values - level), LANES - 2 * flat, 1)
        total = jnp.sum(values * weight, axis=0, keepdims=True)
        picked = pltpu.roll(jnp.sum(values, axis=0, keepdims=True), LANES - flat, 1)
        level = pltpu.roll(level, LANES - 2 * flat, 1)
        own = lane < flat
        lse = jnp.where(own, level + jnp.log(jnp.where(own, total, 1.0)), 0.0)
        picked = picked - lse
        square = (flat, LANES)
        mine = lanes_of(square) == lax.broadcasted_iota(jnp.int32, square, 0)
        column = jnp.sum(jnp.where(mine, jnp.broadcast_to(lse, square), 0.0), axis=1, keepdims=True)
        tiles = [combined[:, k * LANES : (k + 1) * LANES] - column for k in range(TILES)]
        for k, tile in enumerate(turned_back(tiles, turn_of(sizes, piece), lanes_of(square))):
            natural[:, k * LANES : (k + 1) * LANES] = tile
        shifted = natural[:, :piece]
        for t in range(texts):
            logprobs[t] = shifted[t * positions : (t + 1) * positions]
        for t in range(texts):
            turn = picked if t == 0 else pltpu.roll(picked, LANES - t * positions, 1)
            target[t : t + 1, :] = turn[:, :positions]

    return kernel


def body(private_logits, public_logits, noise, owner, counts, tokens):
    texts, positions, piece = public_logits.shape
    rows = owner.shape[0]
    flat = texts * positions
    sizes = (lax.axis_size("ref_0"), lax.axis_size("ref_1"))
    chips = sizes[0] * sizes[1]
    swap = [(0, 1), (1, 0)]
    scale = float(32767 // (2 * rows * int(clip_bound)))
    square = pltpu.VMEM((flat, LANES), jnp.float32)
    long = pltpu.VMEM((flat, WIDE), jnp.float32)
    owner_there, counts_there, tokens_there, public_there, noise_there, private_there = (
        pltpu.with_memory_space_constraint(x, pltpu.HBM)
        for x in (owner, counts, tokens, public_logits, noise, private_logits)
    )

    partner = lax.ppermute(owner, CORE, swap)
    one, number = pl.pallas_call(
        turn_kernel(sizes),
        out_shape=(long, square),
        in_specs=[VMEM, SMEM],
        out_specs=(VMEM, VMEM),
        scratch_shapes=[pltpu.VMEM((flat, WIDE), jnp.float32)],
        compiler_params=PARAMS,
        name="turn",
    )(public_there, owner_there)
    partner, private_later, one = lax.optimization_barrier((partner, private_logits, one))
    swapped = lax.ppermute(private_later, CORE, swap)
    packed = pl.pallas_call(
        mark_kernel(sizes, piece, positions),
        out_shape=pltpu.VMEM((chips, flat, WIDE), jnp.bfloat16),
        in_specs=[VMEM, VMEM, VMEM],
        out_specs=VMEM,
        compiler_params=PARAMS,
        name="mark",
    )(one, number, partner.reshape(1, rows))
    own = lax.all_to_all(packed, CHIP, split_axis=0, concat_axis=0, tiled=True)
    swapped, own, partner = (
        pltpu.with_memory_space_constraint(x, pltpu.VMEM) for x in (swapped, own, partner)
    )
    lines, beside = sizes
    line_sums = pltpu.VMEM((lines, flat, WIDE), jnp.int16)
    windows = lines * WINDOW
    *away, private_here, plan = pl.pallas_call(
        away_kernel(sizes, scale, piece),
        out_shape=(
            *[line_sums] * (beside - 1),
            pltpu.VMEM(private_logits.shape, private_logits.dtype),
            jax.ShapeDtypeStruct((4 * rows,), jnp.int32),
        ),
        in_specs=[HBM, VMEM, HBM, HBM, VMEM, VMEM],
        out_specs=(VMEM,) * beside + (SMEM,),
        scratch_shapes=[
            pltpu.VMEM((texts, positions, (beside - 1) * windows), jnp.float32),
            pltpu.VMEM((texts + 1, positions, (beside - 1) * WINDOW), jnp.float32),
            pltpu.SMEM((rows,), jnp.int32),
            pltpu.SMEM((rows,), jnp.int32),
            pltpu.SMEM((texts,), jnp.int32),
            pltpu.SMEM((texts,), jnp.int32),
            pltpu.SemaphoreType.DMA((lines,)),
            pltpu.SemaphoreType.DMA((3,)),
        ],
        compiler_params=PARAMS,
        name="away_sums",
    )(owner_there, partner, counts_there, private_there, swapped, own)
    got = [
        lax.ppermute(x, "ref_1", [(k, k ^ m) for k in range(beside)])
        for x, m in zip(away, AROUND)
    ]
    line, base, chosen, level, factor = pl.pallas_call(
        own_kernel(sizes, scale, piece),
        out_shape=(line_sums, long, long, square, square),
        in_specs=[VMEM, VMEM, SMEM, SMEM, SMEM, VMEM, VMEM, VMEM],
        out_specs=(VMEM,) * 5,
        scratch_shapes=[
            pltpu.VMEM((texts, positions, windows), jnp.float32),
            pltpu.VMEM((texts + 1, positions, GROUP * WINDOW), jnp.float32),
            pltpu.VMEM((2, flat, WIDE), jnp.float32),
        ],
        compiler_params=PARAMS,
        name="own_sums",
    )(public_there, noise_there, counts_there, tokens_there, plan, private_here, swapped, own)
    joined = pl.pallas_call(
        join_kernel,
        out_shape=line_sums,
        in_specs=[VMEM] * 4,
        out_specs=VMEM,
        compiler_params=PARAMS,
        name="join",
    )(line, *[pltpu.with_memory_space_constraint(x, pltpu.VMEM) for x in got])
    parts = lax.all_to_all(joined, "ref_0", split_axis=0, concat_axis=0, tiled=True)
    parts = pltpu.with_memory_space_constraint(parts, pltpu.VMEM)
    combined, stats = pl.pallas_call(
        finish_kernel,
        out_shape=(long, pltpu.VMEM((1, LANES), jnp.float32)),
        in_specs=[VMEM] * 5,
        out_specs=(VMEM, VMEM),
        compiler_params=PARAMS,
        name="finish",
    )(parts, base, chosen, level, factor)

    devices = lax.axis_size(REF_VOC)
    everyone = lax.all_to_all(
        jnp.broadcast_to(stats, (devices, 1, LANES)), REF_VOC, split_axis=0, concat_axis=0, tiled=True
    ).reshape(devices, LANES)
    return pl.pallas_call(
        last_kernel(sizes),
        out_shape=(
            jax.ShapeDtypeStruct(public_logits.shape, jnp.float32),
            jax.ShapeDtypeStruct((texts, positions), jnp.float32),
        ),
        in_specs=[VMEM, VMEM],
        out_specs=(VMEM, VMEM),
        scratch_shapes=[pltpu.VMEM((flat, WIDE), jnp.float32)],
        compiler_params=PARAMS,
        name="last",
    )(pltpu.with_memory_space_constraint(everyone, pltpu.VMEM), combined)


def solution(mesh):
    finer = Mesh(
        mesh.devices.reshape(8, 4, 2, mesh.shape["voc"]), ("ref_0", "ref_1", "ref_2", "voc")
    )
    placed = (P(REF, None, "voc"), P(None, None, VOC_REF), P(None, None, VOC_REF), P(REF), P(), P())
    return jax.shard_map(
        body, mesh=finer, in_specs=placed, out_specs=(P(None, None, VOC_REF), P()), check_vma=False
    )
```

```python
import jax
import jax.numpy as jnp
from jax import lax
from jax.experimental import pallas as pl
from jax.experimental.pallas import tpu as pltpu
from jax.sharding import Mesh
from jax.sharding import PartitionSpec as P

REF_VOC = ("ref_0", "ref_1", "ref_2", "voc")
REF = ("ref_0", "ref_1", "ref_2")
CHIP = ("ref_0", "ref_1")
CORE = "ref_2"
VOC_REF = ("voc", "ref_0", "ref_1", "ref_2")

clip_bound = 2.0

LANES = 128
WIDE = 512
TILES = WIDE // LANES
WINDOW = WIDE + LANES
GROUP = 4
AROUND = (2, 1, 3, 0)
LEAD = LANES

PARAMS = pltpu.CompilerParams(vmem_limit_bytes=16 << 20)
SMEM = pl.BlockSpec(memory_space=pltpu.SMEM)
VMEM = pl.BlockSpec(memory_space=pltpu.VMEM)
HBM = pl.BlockSpec(memory_space=pltpu.HBM)


def tile_of(x, k):
    return x[:, k * LANES : (k + 1) * LANES]


def turned(tiles, shift, lane):
    spun = [pltpu.roll(tile, shift, 1) for tile in tiles]
    return [jnp.where(lane >= shift, spun[k], spun[k - 1]) for k in range(TILES)]


def turned_back(tiles, shift, lane):
    back = LANES - shift
    spun = [pltpu.roll(tile, back, 1) for tile in tiles]
    return [jnp.where(lane < back, spun[k], spun[(k + 1) % TILES]) for k in range(TILES)]


def lanes_of(shape):
    return lax.broadcasted_iota(jnp.int32, shape, len(shape) - 1)


def rows_of(array, scratch):
    texts, positions, piece = array.shape
    for t in range(texts):
        part = slice(t * positions, (t + 1) * positions)
        scratch[part, :piece] = array[t].astype(jnp.float32)
    values = scratch[...]
    lane = lanes_of((texts * positions, LANES))
    return [
        jnp.where(lane + k * LANES < piece, tile_of(values, k), 0.0) for k in range(TILES)
    ]


def column_of(lane, k, shift):
    return (lane + k * LANES - shift) & (WIDE - 1)


def place_of(sizes):
    chip = lax.axis_index("ref_0") * sizes[1] + lax.axis_index("ref_1")
    return chip, lax.axis_index("ref_2")


def turn_of(sizes, piece):
    chip, core = place_of(sizes)
    return ((2 * chip + core) * piece) & (LANES - 1)


def inside_text(row, t, positions):
    return (row >= t * positions) & (row < (t + 1) * positions)


def turn_kernel(sizes):
    def kernel(public, near, out, number, scratch):
        texts, positions, piece = public.shape
        square = number.shape
        lane = lanes_of(square)
        row = lax.broadcasted_iota(jnp.int32, square, 0)
        shift = turn_of(sizes, piece)
        for k, tile in enumerate(turned(rows_of(public, scratch), shift, lane)):
            out[:, k * LANES : (k + 1) * LANES] = tile
        many = jnp.zeros(square, jnp.float32)
        for t in range(texts):
            held = jnp.int32(0)
            for r in range(near.shape[0]):
                held += jnp.where(near[r] == t, 1, 0)
            many = jnp.where(inside_text(row, t, positions), held.astype(jnp.float32), many)
        number[...] = many

    return kernel


def mark_kernel(sizes, piece, positions):
    def kernel(one, number, far, out):
        square = number.shape
        row = lax.broadcasted_iota(jnp.int32, square, 0)
        lane = lanes_of(square)
        shift = turn_of(sizes, piece)
        many = number[...]
        for t in range(square[0] // positions):
            held = jnp.sum(jnp.where(far[...] == t, 1.0, 0.0), axis=1, keepdims=True)
            held = jnp.broadcast_to(held, square)
            many = many + jnp.where(inside_text(row, t, positions), held, 0.0)
        for k in range(TILES):
            tile = one[:, k * LANES : (k + 1) * LANES]
            tile = jnp.where(column_of(lane, k, shift) < piece, tile, many)
            tile = tile.astype(out.dtype)
            for j in range(out.shape[0]):
                out[j, :, k * LANES : (k + 1) * LANES] = tile

    return kernel


class Rows:
    def __init__(self, plan, priv, swapped):
        rows, self.positions, self.columns = priv.shape
        self.entries = []
        for h, held in enumerate((priv, swapped)):
            for r in range(rows):
                at = h * rows + r
                self.entries.append((held, r, plan[at], plan[2 * rows + at]))


def begins(j, core, piece):
    start = (2 * j + core) * piece
    base = start // LANES * LANES
    return pl.multiple_of(base, LANES), start - base


def widen_into(pub, place, value, positions):
    for t in range(pub.shape[0]):
        part = value[t * positions : (t + 1) * positions]
        pub[t, :, pl.ds(pl.multiple_of(place * WINDOW, LANES), WIDE)] = part
        pub[t, :, pl.ds(pl.multiple_of(place * WINDOW + WIDE, LANES), LANES)] = part[:, :LANES]


def fill_strip(rows, strip):
    last = rows.columns // LANES * LANES
    strip[...] = jnp.zeros(strip.shape, strip.dtype)
    for e, (held, r, _, _) in enumerate(rows.entries):
        strip[e, :, : rows.columns - last] = held[r, :, last:]


def sum_windows(rows, pub, acc, core, piece, scale, windows, strip=None):
    texts = pub.shape[0]
    whole = rows.columns // LANES * LANES
    bases = [begins(j, core, piece)[0] for j, _, _ in windows]
    at = [pl.multiple_of(place * WINDOW, LANES) for _, place, _ in windows]
    acc[:texts, :, : len(windows) * WINDOW] = jnp.zeros(
        (texts, rows.positions, len(windows) * WINDOW), jnp.float32
    )
    if strip is not None:
        fill_strip(rows, strip)
        ends = [base + WINDOW > rows.columns for base in bases]
        edges = [pl.multiple_of(jnp.minimum(base + WIDE, whole - LANES), LANES) for base in bases]
    for e, (held, r, text, slot) in enumerate(rows.entries):
        for g in range(len(windows)):
            size = WINDOW if strip is None else WIDE
            parts = [(0, held[r, :, pl.ds(bases[g], size)])]
            if strip is not None:
                parts.append((WIDE, jnp.where(ends[g], strip[e], held[r, :, pl.ds(edges[g], LANES)])))
            for offset, value in parts:
                width = value.shape[1]
                beside = pub[text, :, pl.ds(pl.multiple_of(at[g] + offset, LANES), width)]
                value = jnp.clip(value.astype(jnp.float32) - beside, -clip_bound, clip_bound)
                where = slice(g * WINDOW + offset, g * WINDOW + offset + width)
                acc[slot, :, where] = acc[slot, :, where] + value
    lane = lanes_of((texts * rows.positions, LANES))
    for g, (j, _, store) in enumerate(windows):
        shift = begins(j, core, piece)[1]
        tiles = [
            jnp.concatenate(
                [acc[t, :, g * WINDOW + k * LANES : g * WINDOW + (k + 1) * LANES] for t in range(texts)],
                axis=0,
            )
            for k in range(TILES + 1)
        ]
        tiles[0] = jnp.where(lane >= shift, tiles[0], tiles[TILES])
        for k in range(TILES):
            fixed = jnp.round(tiles[k] * scale).astype(jnp.int32).astype(jnp.int16)
            store(slice(k * LANES, (k + 1) * LANES), fixed)


def storing(out, index):
    def store(part, value):
        out[index, :, part] = value

    return store


def far_kernel(sizes, scale, piece):
    def kernel(
        owner_there, partner_there, counts_there, source, swapped, own,
        out, priv, plan,
        pub, acc, strip, owner, partner, counts, left, arrived, small,
    ):
        rows, positions, columns = priv.shape
        texts = pub.shape[0]
        chips, flat, _ = own.shape
        lines, beside = sizes
        chip, core = place_of(sizes)
        mine = lax.axis_index("ref_1")
        lane = lanes_of((flat, LANES))
        row = lax.broadcasted_iota(jnp.int32, (flat, LANES), 0)

        stride = 2 * beside * piece
        stride = -(-stride // LANES) * LANES

        def copy_of(i, start, width):
            return pltpu.make_async_copy(
                source.at[:, :, pl.ds(start, width)],
                priv.at[:, :, pl.ds(start, width)],
                arrived.at[i],
            )

        first_chunk = (0, 0, stride + LEAD)
        last_start = LEAD + (lines - 1) * stride
        last_chunk = (lines - 1, last_start, columns - last_start)
        pairs = ((owner_there, owner), (partner_there, partner), (counts_there, counts))
        little = [
            pltpu.make_async_copy(there, here, small.at[i]) for i, (there, here) in enumerate(pairs)
        ]
        for copy in little:
            copy.start()
        copy_of(*first_chunk).start()
        for i in range(1, lines - 1):
            copy_of(i, LEAD + i * stride, stride).start()
        copy_of(*last_chunk).start()

        def widen(i, earlier):
            for n in range(beside):
                j = beside * i + (mine ^ AROUND[n])
                value = own[j].astype(jnp.float32)
                if n == 0:
                    widen_into(pub, i, value, positions)
                shift = begins(j, core, piece)[1]
                free = jnp.where(shift == 0, LANES - 1, shift - 1)
                tile = jnp.where(shift == 0, tile_of(value, TILES - 1), tile_of(value, 0))
                free = jnp.where(j < chip, free, LANES)
                earlier = earlier + jnp.where(lane == free, tile, 0.0)
            return earlier

        earlier = lax.fori_loop(0, lines, widen, jnp.zeros((flat, LANES), jnp.float32))
        for copy in little:
            copy.wait()
        for t in range(texts):
            here = jnp.where(row == t * positions, earlier, 0.0)
            left[t] = counts[t] - jnp.sum(here).astype(jnp.int32)

        for c in range(2):
            for r in range(rows):
                text = jnp.where(core == c, owner[r], partner[r])
                still = left[text]
                left[text] = still - 1
                at = jnp.where(core == c, r, rows + r)
                plan[at] = text
                plan[2 * rows + at] = jnp.where(still > 0, text, texts)
        acc[texts] = jnp.zeros(acc.shape[1:], jnp.float32)
        held = Rows(plan, priv, swapped)
        for i in range(lines):
            copies = {0: first_chunk, lines - 1: last_chunk}
            copy_of(*copies.get(i, (i, LEAD + i * stride, stride))).wait()
            if i % GROUP == GROUP - 1:
                windows = [
                    (beside * k + (mine ^ AROUND[0]), k, storing(out, k))
                    for k in range(i + 1 - GROUP, i + 1)
                ]
                last = i == lines - 1
                sum_windows(held, pub, acc, core, piece, scale, windows, strip if last else None)

    return kernel


def near_kernel(sizes, scale, piece):
    def kernel(plan, priv, swapped, own, out_1, out_2, pub, acc, strip):
        texts = pub.shape[0]
        lines, beside = sizes
        chip, core = place_of(sizes)
        mine = lax.axis_index("ref_1")
        held = Rows(plan, priv, swapped)
        acc[texts] = jnp.zeros(acc.shape[1:], jnp.float32)
        step = GROUP // 2

        def some(first, strip=None):
            windows = []
            for k in range(step):
                i = first + k
                for n, out in ((1, out_1), (2, out_2)):
                    j = beside * i + (mine ^ AROUND[n])
                    place = 2 * k + n - 1
                    widen_into(pub, place, own[j].astype(jnp.float32), held.positions)
                    windows.append((j, place, storing(out, i)))
            sum_windows(held, pub, acc, core, piece, scale, windows, strip)

        def looped(b, carry):
            some(b * step)
            return carry

        lax.fori_loop(0, lines // step - 1, looped, 0)
        some(lines - step, strip)

    return kernel


def own_kernel(sizes, scale, piece):
    def kernel(
        public, noise, counts, tokens, plan, priv, swapped, own,
        out, base, chosen, level, factor,
        pub, acc, strip, scratch,
    ):
        texts = pub.shape[0]
        lines, beside = sizes
        chip, core = place_of(sizes)
        mine = lax.axis_index("ref_1")
        held = Rows(plan, priv, swapped)
        for i in range(lines):
            widen_into(pub, i, own[beside * i + mine].astype(jnp.float32), held.positions)
        acc[texts] = jnp.zeros(acc.shape[1:], jnp.float32)
        for first in range(0, lines, GROUP):
            windows = [(beside * i + mine, i, storing(out, i)) for i in range(first, first + GROUP)]
            last = first + GROUP == lines
            sum_windows(held, pub, acc, core, piece, scale, windows, strip if last else None)
        prepare(sizes, scale / beside, public, noise, counts, tokens, scratch, base, chosen, level, factor)

    return kernel


def join_kernel(a, b, c, d, out):
    for i in range(out.shape[0]):
        total = (a[i].astype(jnp.int32) + b[i].astype(jnp.int32)) + (
            c[i].astype(jnp.int32) + d[i].astype(jnp.int32)
        )
        total = jnp.round(total.astype(jnp.float32) * 0.25)
        out[i] = total.astype(jnp.int32).astype(jnp.int16)


def prepare(sizes, scale_of, public, noise, counts, tokens, scratch, base, chosen, level, factor):
    texts, positions, piece = public.shape
    square = (texts * positions, LANES)
    lane = lanes_of(square)
    row = lax.broadcasted_iota(jnp.int32, square, 0)
    shift = turn_of(sizes, piece)
    chip, core = place_of(sizes)
    chips = sizes[0] * sizes[1]
    first = (lax.axis_index("voc") * 2 * chips + 2 * chip + core) * piece
    number = jnp.ones(square, jnp.float32)
    token = jnp.zeros(square, jnp.int32)
    for t in range(texts):
        number = jnp.where(inside_text(row, t, positions), counts[t].astype(jnp.float32), number)
        for p in range(positions):
            token = jnp.where(row == t * positions + p, tokens[t, p] - first, token)
    factor[...] = (1.0 / scale_of) / (clip_bound * jnp.sqrt(number))
    public_tiles = turned(rows_of(public, scratch.at[0]), shift, lane)
    noise_tiles = turned(rows_of(noise, scratch.at[1]), shift, lane)
    top = jnp.full(square, -jnp.inf, jnp.float32)
    for k in range(TILES):
        column = column_of(lane, k, shift)
        inside = column < piece
        part = slice(k * LANES, (k + 1) * LANES)
        top = jnp.maximum(top, jnp.where(inside, public_tiles[k], -jnp.inf))
        base[:, part] = jnp.where(inside, public_tiles[k] + noise_tiles[k], -jnp.inf)
        chosen[:, part] = jnp.where(inside & (column == token), 1.0, 0.0)
    level[...] = jnp.broadcast_to(jnp.max(top, axis=1, keepdims=True), square)


def finish_kernel(parts, base, chosen, level, scale, combined, stats):
    flat = base.shape[0]
    square = (flat, LANES)
    lane = lanes_of(square)
    row = lax.broadcasted_iota(jnp.int32, square, 0)
    terms = jnp.zeros(square, jnp.float32)
    picked = jnp.zeros(square, jnp.float32)
    for k in range(TILES):
        part = slice(k * LANES, (k + 1) * LANES)
        total = parts[0, :, part].astype(jnp.int32)
        for j in range(1, parts.shape[0]):
            total = total + parts[j, :, part].astype(jnp.int32)
        tile = base[:, part] + total.astype(jnp.float32) * scale[...]
        combined[:, part] = tile
        terms = terms + jnp.exp(tile - level[...])
        picked = picked + jnp.where(chosen[:, part] > 0.0, tile, 0.0)
    terms = jnp.sum(terms, axis=1, keepdims=True)
    picked = jnp.sum(picked, axis=1, keepdims=True)
    spread = jnp.where(lane == row, terms, 0.0)
    spread = spread + jnp.where(lane == row + flat, picked, 0.0)
    spread = spread + jnp.where(lane == row + 2 * flat, level[...], 0.0)
    stats[...] = jnp.sum(spread, axis=0, keepdims=True)


def last_kernel(sizes):
    def kernel(everyone, combined, logprobs, target, natural):
        texts, positions, piece = logprobs.shape
        flat = texts * positions
        values = everyone[...]
        lane = lanes_of((1, LANES))
        level = jnp.max(values, axis=0, keepdims=True)
        weight = pltpu.roll(jnp.exp(values - level), LANES - 2 * flat, 1)
        total = jnp.sum(values * weight, axis=0, keepdims=True)
        picked = pltpu.roll(jnp.sum(values, axis=0, keepdims=True), LANES - flat, 1)
        level = pltpu.roll(level, LANES - 2 * flat, 1)
        own = lane < flat
        lse = jnp.where(own, level + jnp.log(jnp.where(own, total, 1.0)), 0.0)
        picked = picked - lse
        square = (flat, LANES)
        mine = lanes_of(square) == lax.broadcasted_iota(jnp.int32, square, 0)
        column = jnp.sum(jnp.where(mine, jnp.broadcast_to(lse, square), 0.0), axis=1, keepdims=True)
        tiles = [combined[:, k * LANES : (k + 1) * LANES] - column for k in range(TILES)]
        for k, tile in enumerate(turned_back(tiles, turn_of(sizes, piece), lanes_of(square))):
            natural[:, k * LANES : (k + 1) * LANES] = tile
        shifted = natural[:, :piece]
        for t in range(texts):
            logprobs[t] = shifted[t * positions : (t + 1) * positions]
        for t in range(texts):
            turn = picked if t == 0 else pltpu.roll(picked, LANES - t * positions, 1)
            target[t : t + 1, :] = turn[:, :positions]

    return kernel


def body(private_logits, public_logits, noise, owner, counts, tokens):
    texts, positions, piece = public_logits.shape
    rows = owner.shape[0]
    flat = texts * positions
    sizes = (lax.axis_size("ref_0"), lax.axis_size("ref_1"))
    chips = sizes[0] * sizes[1]
    swap = [(0, 1), (1, 0)]
    scale = float(32767 // (2 * rows * int(clip_bound)))
    square = pltpu.VMEM((flat, LANES), jnp.float32)
    long = pltpu.VMEM((flat, WIDE), jnp.float32)
    owner_there, counts_there, tokens_there, public_there, noise_there, private_there = (
        pltpu.with_memory_space_constraint(x, pltpu.HBM)
        for x in (owner, counts, tokens, public_logits, noise, private_logits)
    )

    partner = lax.ppermute(owner, CORE, swap)
    one, number = pl.pallas_call(
        turn_kernel(sizes),
        out_shape=(long, square),
        in_specs=[VMEM, SMEM],
        out_specs=(VMEM, VMEM),
        scratch_shapes=[pltpu.VMEM((flat, WIDE), jnp.float32)],
        compiler_params=PARAMS,
        name="turn",
    )(public_there, owner_there)
    partner, private_later, one = lax.optimization_barrier((partner, private_logits, one))
    swapped = lax.ppermute(private_later, CORE, swap)
    packed = pl.pallas_call(
        mark_kernel(sizes, piece, positions),
        out_shape=pltpu.VMEM((chips, flat, WIDE), jnp.bfloat16),
        in_specs=[VMEM, VMEM, VMEM],
        out_specs=VMEM,
        compiler_params=PARAMS,
        name="mark",
    )(one, number, partner.reshape(1, rows))
    own = lax.all_to_all(packed, CHIP, split_axis=0, concat_axis=0, tiled=True)
    swapped, own, partner = (
        pltpu.with_memory_space_constraint(x, pltpu.VMEM) for x in (swapped, own, partner)
    )
    lines, beside = sizes
    line_sums = pltpu.VMEM((lines, flat, WIDE), jnp.int16)
    windows = lines * WINDOW
    sums_scratch = pltpu.VMEM((texts + 1, positions, GROUP * WINDOW), jnp.float32)
    strip = pltpu.VMEM((2 * rows, positions, LANES), private_logits.dtype)

    def beyond(x, m):
        return lax.ppermute(x, "ref_1", [(k, k ^ m) for k in range(beside)])

    far, private_here, plan = pl.pallas_call(
        far_kernel(sizes, scale, piece),
        out_shape=(
            line_sums,
            pltpu.VMEM(private_logits.shape, private_logits.dtype),
            jax.ShapeDtypeStruct((4 * rows,), jnp.int32),
        ),
        in_specs=[HBM, VMEM, HBM, HBM, VMEM, VMEM],
        out_specs=(VMEM, VMEM, SMEM),
        scratch_shapes=[
            pltpu.VMEM((texts, positions, windows), jnp.float32),
            sums_scratch,
            strip,
            pltpu.SMEM((rows,), jnp.int32),
            pltpu.SMEM((rows,), jnp.int32),
            pltpu.SMEM((texts,), jnp.int32),
            pltpu.SMEM((texts,), jnp.int32),
            pltpu.SemaphoreType.DMA((lines,)),
            pltpu.SemaphoreType.DMA((3,)),
        ],
        compiler_params=PARAMS,
        name="far_sums",
    )(owner_there, partner, counts_there, private_there, swapped, own)
    got = [beyond(far, AROUND[0])]
    near = pl.pallas_call(
        near_kernel(sizes, scale, piece),
        out_shape=(line_sums, line_sums),
        in_specs=[SMEM, VMEM, VMEM, VMEM],
        out_specs=(VMEM, VMEM),
        scratch_shapes=[
            pltpu.VMEM((texts, positions, GROUP * WINDOW), jnp.float32),
            sums_scratch,
            strip,
        ],
        compiler_params=PARAMS,
        name="near_sums",
    )(plan, private_here, swapped, own)
    got += [beyond(x, m) for x, m in zip(near, AROUND[1:])]
    near_done, own_later = lax.optimization_barrier((near[0], own))
    line, base, chosen, level, factor = pl.pallas_call(
        own_kernel(sizes, scale, piece),
        out_shape=(line_sums, long, long, square, square),
        in_specs=[VMEM, VMEM, SMEM, SMEM, SMEM, VMEM, VMEM, VMEM],
        out_specs=(VMEM,) * 5,
        scratch_shapes=[
            pltpu.VMEM((texts, positions, windows), jnp.float32),
            sums_scratch,
            strip,
            pltpu.VMEM((2, flat, WIDE), jnp.float32),
        ],
        compiler_params=PARAMS,
        name="own_sums",
    )(public_there, noise_there, counts_there, tokens_there, plan, private_here, swapped, own_later)
    joined = pl.pallas_call(
        join_kernel,
        out_shape=line_sums,
        in_specs=[VMEM] * 4,
        out_specs=VMEM,
        compiler_params=PARAMS,
        name="join",
    )(line, *[pltpu.with_memory_space_constraint(x, pltpu.VMEM) for x in got])
    parts = lax.all_to_all(joined, "ref_0", split_axis=0, concat_axis=0, tiled=True)
    parts = pltpu.with_memory_space_constraint(parts, pltpu.VMEM)
    combined, stats = pl.pallas_call(
        finish_kernel,
        out_shape=(long, pltpu.VMEM((1, LANES), jnp.float32)),
        in_specs=[VMEM] * 5,
        out_specs=(VMEM, VMEM),
        compiler_params=PARAMS,
        name="finish",
    )(parts, base, chosen, level, factor)

    devices = lax.axis_size(REF_VOC)
    everyone = lax.all_to_all(
        jnp.broadcast_to(stats, (devices, 1, LANES)), REF_VOC, split_axis=0, concat_axis=0, tiled=True
    ).reshape(devices, LANES)
    return pl.pallas_call(
        last_kernel(sizes),
        out_shape=(
            jax.ShapeDtypeStruct(public_logits.shape, jnp.float32),
            jax.ShapeDtypeStruct((texts, positions), jnp.float32),
        ),
        in_specs=[VMEM, VMEM],
        out_specs=(VMEM, VMEM),
        scratch_shapes=[pltpu.VMEM((flat, WIDE), jnp.float32)],
        compiler_params=PARAMS,
        name="last",
    )(pltpu.with_memory_space_constraint(everyone, pltpu.VMEM), combined)


def solution(mesh):
    finer = Mesh(
        mesh.devices.reshape(8, 4, 2, mesh.shape["voc"]), ("ref_0", "ref_1", "ref_2", "voc")
    )
    placed = (P(REF, None, "voc"), P(None, None, VOC_REF), P(None, None, VOC_REF), P(REF), P(), P())
    return jax.shard_map(
        body, mesh=finer, in_specs=placed, out_specs=(P(None, None, VOC_REF), P()), check_vma=False
    )
```

```python
import jax
import jax.numpy as jnp
from jax import lax
from jax.experimental import pallas as pl
from jax.experimental.pallas import tpu as pltpu
from jax.sharding import Mesh
from jax.sharding import PartitionSpec as P

REF_VOC = ("ref_0", "ref_1", "ref_2", "voc")
REF = ("ref_0", "ref_1", "ref_2")
CHIP = ("ref_0", "ref_1")
CORE = "ref_2"
VOC_REF = ("voc", "ref_0", "ref_1", "ref_2")

clip_bound = 2.0

LANES = 128
WIDE = 512
TILES = WIDE // LANES
WINDOW = WIDE + LANES
GROUP = 4
AROUND = (2, 1, 3, 0)

PARAMS = pltpu.CompilerParams(vmem_limit_bytes=16 << 20)
SMEM = pl.BlockSpec(memory_space=pltpu.SMEM)
VMEM = pl.BlockSpec(memory_space=pltpu.VMEM)
HBM = pl.BlockSpec(memory_space=pltpu.HBM)


def tile_of(x, k):
    return x[:, k * LANES : (k + 1) * LANES]


def turned(tiles, shift, lane):
    spun = [pltpu.roll(tile, shift, 1) for tile in tiles]
    return [jnp.where(lane >= shift, spun[k], spun[k - 1]) for k in range(TILES)]


def turned_back(tiles, shift, lane):
    back = LANES - shift
    spun = [pltpu.roll(tile, back, 1) for tile in tiles]
    return [jnp.where(lane < back, spun[k], spun[(k + 1) % TILES]) for k in range(TILES)]


def lanes_of(shape):
    return lax.broadcasted_iota(jnp.int32, shape, len(shape) - 1)


def rows_of(array, scratch):
    texts, positions, piece = array.shape
    for t in range(texts):
        part = slice(t * positions, (t + 1) * positions)
        scratch[part, :piece] = array[t].astype(jnp.float32)
    values = scratch[...]
    lane = lanes_of((texts * positions, LANES))
    return [
        jnp.where(lane + k * LANES < piece, tile_of(values, k), 0.0) for k in range(TILES)
    ]


def column_of(lane, k, shift):
    return (lane + k * LANES - shift) & (WIDE - 1)


def place_of(sizes):
    chip = lax.axis_index("ref_0") * sizes[1] + lax.axis_index("ref_1")
    return chip, lax.axis_index("ref_2")


def turn_of(sizes, piece):
    chip, core = place_of(sizes)
    return ((2 * chip + core) * piece) & (LANES - 1)


def inside_text(row, t, positions):
    return (row >= t * positions) & (row < (t + 1) * positions)


def turn_kernel(sizes):
    def kernel(public, near, out, number, scratch):
        texts, positions, piece = public.shape
        square = number.shape
        lane = lanes_of(square)
        row = lax.broadcasted_iota(jnp.int32, square, 0)
        shift = turn_of(sizes, piece)
        for k, tile in enumerate(turned(rows_of(public, scratch), shift, lane)):
            out[:, k * LANES : (k + 1) * LANES] = tile
        many = jnp.zeros(square, jnp.float32)
        for t in range(texts):
            held = jnp.int32(0)
            for r in range(near.shape[0]):
                held += jnp.where(near[r] == t, 1, 0)
            many = jnp.where(inside_text(row, t, positions), held.astype(jnp.float32), many)
        number[...] = many

    return kernel


def mark_kernel(sizes, piece, positions):
    def kernel(one, number, far, out):
        square = number.shape
        row = lax.broadcasted_iota(jnp.int32, square, 0)
        lane = lanes_of(square)
        shift = turn_of(sizes, piece)
        many = number[...]
        for t in range(square[0] // positions):
            held = jnp.sum(jnp.where(far[...] == t, 1.0, 0.0), axis=1, keepdims=True)
            held = jnp.broadcast_to(held, square)
            many = many + jnp.where(inside_text(row, t, positions), held, 0.0)
        for k in range(TILES):
            tile = one[:, k * LANES : (k + 1) * LANES]
            tile = jnp.where(column_of(lane, k, shift) < piece, tile, many)
            tile = tile.astype(out.dtype)
            for j in range(out.shape[0]):
                out[j, :, k * LANES : (k + 1) * LANES] = tile

    return kernel


class Rows:
    def __init__(self, plan, priv, swapped):
        rows, self.positions, self.columns = priv.shape
        self.entries = []
        for h, held in enumerate((priv, swapped)):
            for r in range(rows):
                at = h * rows + r
                self.entries.append((held, r, plan[at], plan[2 * rows + at]))


def begins(j, core, piece):
    start = (2 * j + core) * piece
    base = start // LANES * LANES
    return pl.multiple_of(base, LANES), start - base


def widen_into(pub, place, value, positions):
    for t in range(pub.shape[0]):
        part = value[t * positions : (t + 1) * positions]
        pub[t, :, pl.ds(pl.multiple_of(place * WINDOW, LANES), WIDE)] = part
        pub[t, :, pl.ds(pl.multiple_of(place * WINDOW + WIDE, LANES), LANES)] = part[:, :LANES]


def fill_strip(rows, strip):
    last = rows.columns // LANES * LANES
    strip[...] = jnp.zeros(strip.shape, strip.dtype)
    for e, (held, r, _, _) in enumerate(rows.entries):
        strip[e, :, : rows.columns - last] = held[r, :, last:]


def sum_windows(rows, pub, acc, core, piece, scale, windows, strip=None):
    texts = pub.shape[0]
    whole = rows.columns // LANES * LANES
    bases = [begins(j, core, piece)[0] for j, _, _ in windows]
    at = [pl.multiple_of(place * WINDOW, LANES) for _, place, _ in windows]
    acc[:texts, :, : len(windows) * WINDOW] = jnp.zeros(
        (texts, rows.positions, len(windows) * WINDOW), jnp.float32
    )
    if strip is not None:
        fill_strip(rows, strip)
        ends = [base + WINDOW > rows.columns for base in bases]
        edges = [pl.multiple_of(jnp.minimum(base + WIDE, whole - LANES), LANES) for base in bases]
    for e, (held, r, text, slot) in enumerate(rows.entries):
        for g in range(len(windows)):
            size = WINDOW if strip is None else WIDE
            parts = [(0, held[r, :, pl.ds(bases[g], size)])]
            if strip is not None:
                parts.append((WIDE, jnp.where(ends[g], strip[e], held[r, :, pl.ds(edges[g], LANES)])))
            for offset, value in parts:
                width = value.shape[1]
                beside = pub[text, :, pl.ds(pl.multiple_of(at[g] + offset, LANES), width)]
                value = jnp.clip(value.astype(jnp.float32) - beside, -clip_bound, clip_bound)
                where = slice(g * WINDOW + offset, g * WINDOW + offset + width)
                acc[slot, :, where] = acc[slot, :, where] + value
    lane = lanes_of((texts * rows.positions, LANES))
    for g, (j, _, store) in enumerate(windows):
        shift = begins(j, core, piece)[1]
        tiles = [
            jnp.concatenate(
                [acc[t, :, g * WINDOW + k * LANES : g * WINDOW + (k + 1) * LANES] for t in range(texts)],
                axis=0,
            )
            for k in range(TILES + 1)
        ]
        tiles[0] = jnp.where(lane >= shift, tiles[0], tiles[TILES])
        for k in range(TILES):
            fixed = jnp.round(tiles[k] * scale).astype(jnp.int32).astype(jnp.int16)
            store(slice(k * LANES, (k + 1) * LANES), fixed)


def storing(out, index):
    def store(part, value):
        out[index, :, part] = value

    return store


def far_kernel(sizes, scale, piece):
    def kernel(
        owner_there, partner_there, counts_there, priv, swapped, own,
        out, plan,
        pub, acc, strip, owner, partner, counts, left, small,
    ):
        rows, positions, columns = priv.shape
        texts = pub.shape[0]
        chips, flat, _ = own.shape
        lines, beside = sizes
        chip, core = place_of(sizes)
        mine = lax.axis_index("ref_1")
        lane = lanes_of((flat, LANES))
        row = lax.broadcasted_iota(jnp.int32, (flat, LANES), 0)

        pairs = ((owner_there, owner), (partner_there, partner), (counts_there, counts))
        little = [
            pltpu.make_async_copy(there, here, small.at[i]) for i, (there, here) in enumerate(pairs)
        ]
        for copy in little:
            copy.start()

        def widen(i, earlier):
            for n in range(beside):
                j = beside * i + (mine ^ AROUND[n])
                value = own[j].astype(jnp.float32)
                if n == 0:
                    widen_into(pub, i, value, positions)
                shift = begins(j, core, piece)[1]
                free = jnp.where(shift == 0, LANES - 1, shift - 1)
                tile = jnp.where(shift == 0, tile_of(value, TILES - 1), tile_of(value, 0))
                free = jnp.where(j < chip, free, LANES)
                earlier = earlier + jnp.where(lane == free, tile, 0.0)
            return earlier

        earlier = lax.fori_loop(0, lines, widen, jnp.zeros((flat, LANES), jnp.float32))
        for copy in little:
            copy.wait()
        for t in range(texts):
            here = jnp.where(row == t * positions, earlier, 0.0)
            left[t] = counts[t] - jnp.sum(here).astype(jnp.int32)

        for c in range(2):
            for r in range(rows):
                text = jnp.where(core == c, owner[r], partner[r])
                still = left[text]
                left[text] = still - 1
                at = jnp.where(core == c, r, rows + r)
                plan[at] = text
                plan[2 * rows + at] = jnp.where(still > 0, text, texts)
        acc[texts] = jnp.zeros(acc.shape[1:], jnp.float32)
        held = Rows(plan, priv, swapped)
        for i in range(lines):
            if i % GROUP == GROUP - 1:
                windows = [
                    (beside * k + (mine ^ AROUND[0]), k, storing(out, k))
                    for k in range(i + 1 - GROUP, i + 1)
                ]
                last = i == lines - 1
                sum_windows(held, pub, acc, core, piece, scale, windows, strip if last else None)

    return kernel


def near_kernel(sizes, scale, piece):
    def kernel(plan, priv, swapped, own, out_1, out_2, pub, acc, strip):
        texts = pub.shape[0]
        lines, beside = sizes
        chip, core = place_of(sizes)
        mine = lax.axis_index("ref_1")
        held = Rows(plan, priv, swapped)
        acc[texts] = jnp.zeros(acc.shape[1:], jnp.float32)
        step = GROUP // 2

        def some(first, strip=None):
            windows = []
            for k in range(step):
                i = first + k
                for n, out in ((1, out_1), (2, out_2)):
                    j = beside * i + (mine ^ AROUND[n])
                    place = 2 * k + n - 1
                    widen_into(pub, place, own[j].astype(jnp.float32), held.positions)
                    windows.append((j, place, storing(out, i)))
            sum_windows(held, pub, acc, core, piece, scale, windows, strip)

        def looped(b, carry):
            some(b * step)
            return carry

        lax.fori_loop(0, lines // step - 1, looped, 0)
        some(lines - step, strip)

    return kernel


def own_kernel(sizes, scale, piece):
    def kernel(
        public, noise, counts, tokens, plan, priv, swapped, own,
        out, base, chosen, level, factor,
        pub, acc, strip, scratch,
    ):
        texts = pub.shape[0]
        lines, beside = sizes
        chip, core = place_of(sizes)
        mine = lax.axis_index("ref_1")
        held = Rows(plan, priv, swapped)
        for i in range(lines):
            widen_into(pub, i, own[beside * i + mine].astype(jnp.float32), held.positions)
        acc[texts] = jnp.zeros(acc.shape[1:], jnp.float32)
        for first in range(0, lines, GROUP):
            windows = [(beside * i + mine, i, storing(out, i)) for i in range(first, first + GROUP)]
            last = first + GROUP == lines
            sum_windows(held, pub, acc, core, piece, scale, windows, strip if last else None)
        prepare(sizes, scale / beside, public, noise, counts, tokens, scratch, base, chosen, level, factor)

    return kernel


def join_kernel(a, b, c, d, out):
    for i in range(out.shape[0]):
        total = (a[i].astype(jnp.int32) + b[i].astype(jnp.int32)) + (
            c[i].astype(jnp.int32) + d[i].astype(jnp.int32)
        )
        total = jnp.round(total.astype(jnp.float32) * 0.25)
        out[i] = total.astype(jnp.int32).astype(jnp.int16)


def prepare(sizes, scale_of, public, noise, counts, tokens, scratch, base, chosen, level, factor):
    texts, positions, piece = public.shape
    square = (texts * positions, LANES)
    lane = lanes_of(square)
    row = lax.broadcasted_iota(jnp.int32, square, 0)
    shift = turn_of(sizes, piece)
    chip, core = place_of(sizes)
    chips = sizes[0] * sizes[1]
    first = (lax.axis_index("voc") * 2 * chips + 2 * chip + core) * piece
    number = jnp.ones(square, jnp.float32)
    token = jnp.zeros(square, jnp.int32)
    for t in range(texts):
        number = jnp.where(inside_text(row, t, positions), counts[t].astype(jnp.float32), number)
        for p in range(positions):
            token = jnp.where(row == t * positions + p, tokens[t, p] - first, token)
    factor[...] = (1.0 / scale_of) / (clip_bound * jnp.sqrt(number))
    public_tiles = turned(rows_of(public, scratch.at[0]), shift, lane)
    noise_tiles = turned(rows_of(noise, scratch.at[1]), shift, lane)
    top = jnp.full(square, -jnp.inf, jnp.float32)
    for k in range(TILES):
        column = column_of(lane, k, shift)
        inside = column < piece
        part = slice(k * LANES, (k + 1) * LANES)
        top = jnp.maximum(top, jnp.where(inside, public_tiles[k], -jnp.inf))
        base[:, part] = jnp.where(inside, public_tiles[k] + noise_tiles[k], -jnp.inf)
        chosen[:, part] = jnp.where(inside & (column == token), 1.0, 0.0)
    level[...] = jnp.broadcast_to(jnp.max(top, axis=1, keepdims=True), square)


def finish_kernel(parts, base, chosen, level, scale, combined, stats):
    flat = base.shape[0]
    square = (flat, LANES)
    lane = lanes_of(square)
    row = lax.broadcasted_iota(jnp.int32, square, 0)
    terms = jnp.zeros(square, jnp.float32)
    picked = jnp.zeros(square, jnp.float32)
    for k in range(TILES):
        part = slice(k * LANES, (k + 1) * LANES)
        total = parts[0, :, part].astype(jnp.int32)
        for j in range(1, parts.shape[0]):
            total = total + parts[j, :, part].astype(jnp.int32)
        tile = base[:, part] + total.astype(jnp.float32) * scale[...]
        combined[:, part] = tile
        terms = terms + jnp.exp(tile - level[...])
        picked = picked + jnp.where(chosen[:, part] > 0.0, tile, 0.0)
    terms = jnp.sum(terms, axis=1, keepdims=True)
    picked = jnp.sum(picked, axis=1, keepdims=True)
    spread = jnp.where(lane == row, terms, 0.0)
    spread = spread + jnp.where(lane == row + flat, picked, 0.0)
    spread = spread + jnp.where(lane == row + 2 * flat, level[...], 0.0)
    stats[...] = jnp.sum(spread, axis=0, keepdims=True)


def last_kernel(sizes):
    def kernel(everyone, combined, logprobs, target, natural):
        texts, positions, piece = logprobs.shape
        flat = texts * positions
        values = everyone[...]
        lane = lanes_of((1, LANES))
        level = jnp.max(values, axis=0, keepdims=True)
        weight = pltpu.roll(jnp.exp(values - level), LANES - 2 * flat, 1)
        total = jnp.sum(values * weight, axis=0, keepdims=True)
        picked = pltpu.roll(jnp.sum(values, axis=0, keepdims=True), LANES - flat, 1)
        level = pltpu.roll(level, LANES - 2 * flat, 1)
        own = lane < flat
        lse = jnp.where(own, level + jnp.log(jnp.where(own, total, 1.0)), 0.0)
        picked = picked - lse
        square = (flat, LANES)
        mine = lanes_of(square) == lax.broadcasted_iota(jnp.int32, square, 0)
        column = jnp.sum(jnp.where(mine, jnp.broadcast_to(lse, square), 0.0), axis=1, keepdims=True)
        tiles = [combined[:, k * LANES : (k + 1) * LANES] - column for k in range(TILES)]
        for k, tile in enumerate(turned_back(tiles, turn_of(sizes, piece), lanes_of(square))):
            natural[:, k * LANES : (k + 1) * LANES] = tile
        shifted = natural[:, :piece]
        for t in range(texts):
            logprobs[t] = shifted[t * positions : (t + 1) * positions]
        for t in range(texts):
            turn = picked if t == 0 else pltpu.roll(picked, LANES - t * positions, 1)
            target[t : t + 1, :] = turn[:, :positions]

    return kernel


def body(private_logits, public_logits, noise, owner, counts, tokens):
    texts, positions, piece = public_logits.shape
    rows = owner.shape[0]
    flat = texts * positions
    sizes = (lax.axis_size("ref_0"), lax.axis_size("ref_1"))
    chips = sizes[0] * sizes[1]
    swap = [(0, 1), (1, 0)]
    scale = float(32767 // (2 * rows * int(clip_bound)))
    square = pltpu.VMEM((flat, LANES), jnp.float32)
    long = pltpu.VMEM((flat, WIDE), jnp.float32)
    owner_there, counts_there, tokens_there, public_there, noise_there = (
        pltpu.with_memory_space_constraint(x, pltpu.HBM)
        for x in (owner, counts, tokens, public_logits, noise)
    )

    partner = lax.ppermute(owner, CORE, swap)
    one, number = pl.pallas_call(
        turn_kernel(sizes),
        out_shape=(long, square),
        in_specs=[VMEM, SMEM],
        out_specs=(VMEM, VMEM),
        scratch_shapes=[pltpu.VMEM((flat, WIDE), jnp.float32)],
        compiler_params=PARAMS,
        name="turn",
    )(public_there, owner_there)
    partner, private_later, one = lax.optimization_barrier((partner, private_logits, one))
    swapped = lax.ppermute(private_later, CORE, swap)
    private_here = lax.ppermute(private_later, CORE, [(0, 0), (1, 1)])
    packed = pl.pallas_call(
        mark_kernel(sizes, piece, positions),
        out_shape=pltpu.VMEM((chips, flat, WIDE), jnp.bfloat16),
        in_specs=[VMEM, VMEM, VMEM],
        out_specs=VMEM,
        compiler_params=PARAMS,
        name="mark",
    )(one, number, partner.reshape(1, rows))
    own = lax.all_to_all(packed, CHIP, split_axis=0, concat_axis=0, tiled=True)
    swapped, own, partner, private_here = (
        pltpu.with_memory_space_constraint(x, pltpu.VMEM)
        for x in (swapped, own, partner, private_here)
    )
    lines, beside = sizes
    line_sums = pltpu.VMEM((lines, flat, WIDE), jnp.int16)
    windows = lines * WINDOW
    sums_scratch = pltpu.VMEM((texts + 1, positions, GROUP * WINDOW), jnp.float32)
    strip = pltpu.VMEM((2 * rows, positions, LANES), private_logits.dtype)

    def beyond(x, m):
        return lax.ppermute(x, "ref_1", [(k, k ^ m) for k in range(beside)])

    far, plan = pl.pallas_call(
        far_kernel(sizes, scale, piece),
        out_shape=(
            line_sums,
            jax.ShapeDtypeStruct((4 * rows,), jnp.int32),
        ),
        in_specs=[HBM, VMEM, HBM, VMEM, VMEM, VMEM],
        out_specs=(VMEM, SMEM),
        scratch_shapes=[
            pltpu.VMEM((texts, positions, windows), jnp.float32),
            sums_scratch,
            strip,
            pltpu.SMEM((rows,), jnp.int32),
            pltpu.SMEM((rows,), jnp.int32),
            pltpu.SMEM((texts,), jnp.int32),
            pltpu.SMEM((texts,), jnp.int32),
            pltpu.SemaphoreType.DMA((3,)),
        ],
        compiler_params=PARAMS,
        name="far_sums",
    )(owner_there, partner, counts_there, private_here, swapped, own)
    got = [beyond(far, AROUND[0])]
    near = pl.pallas_call(
        near_kernel(sizes, scale, piece),
        out_shape=(line_sums, line_sums),
        in_specs=[SMEM, VMEM, VMEM, VMEM],
        out_specs=(VMEM, VMEM),
        scratch_shapes=[
            pltpu.VMEM((texts, positions, GROUP * WINDOW), jnp.float32),
            sums_scratch,
            strip,
        ],
        compiler_params=PARAMS,
        name="near_sums",
    )(plan, private_here, swapped, own)
    got += [beyond(x, m) for x, m in zip(near, AROUND[1:])]
    near_done, own_later = lax.optimization_barrier((near[0], own))
    line, base, chosen, level, factor = pl.pallas_call(
        own_kernel(sizes, scale, piece),
        out_shape=(line_sums, long, long, square, square),
        in_specs=[VMEM, VMEM, SMEM, SMEM, SMEM, VMEM, VMEM, VMEM],
        out_specs=(VMEM,) * 5,
        scratch_shapes=[
            pltpu.VMEM((texts, positions, windows), jnp.float32),
            sums_scratch,
            strip,
            pltpu.VMEM((2, flat, WIDE), jnp.float32),
        ],
        compiler_params=PARAMS,
        name="own_sums",
    )(public_there, noise_there, counts_there, tokens_there, plan, private_here, swapped, own_later)
    joined = pl.pallas_call(
        join_kernel,
        out_shape=line_sums,
        in_specs=[VMEM] * 4,
        out_specs=VMEM,
        compiler_params=PARAMS,
        name="join",
    )(line, *[pltpu.with_memory_space_constraint(x, pltpu.VMEM) for x in got])
    parts = lax.all_to_all(joined, "ref_0", split_axis=0, concat_axis=0, tiled=True)
    parts = pltpu.with_memory_space_constraint(parts, pltpu.VMEM)
    combined, stats = pl.pallas_call(
        finish_kernel,
        out_shape=(long, pltpu.VMEM((1, LANES), jnp.float32)),
        in_specs=[VMEM] * 5,
        out_specs=(VMEM, VMEM),
        compiler_params=PARAMS,
        name="finish",
    )(parts, base, chosen, level, factor)

    devices = lax.axis_size(REF_VOC)
    everyone = lax.all_to_all(
        jnp.broadcast_to(stats, (devices, 1, LANES)), REF_VOC, split_axis=0, concat_axis=0, tiled=True
    ).reshape(devices, LANES)
    return pl.pallas_call(
        last_kernel(sizes),
        out_shape=(
            jax.ShapeDtypeStruct(public_logits.shape, jnp.float32),
            jax.ShapeDtypeStruct((texts, positions), jnp.float32),
        ),
        in_specs=[VMEM, VMEM],
        out_specs=(VMEM, VMEM),
        scratch_shapes=[pltpu.VMEM((flat, WIDE), jnp.float32)],
        compiler_params=PARAMS,
        name="last",
    )(pltpu.with_memory_space_constraint(everyone, pltpu.VMEM), combined)


def solution(mesh):
    finer = Mesh(
        mesh.devices.reshape(8, 4, 2, mesh.shape["voc"]), ("ref_0", "ref_1", "ref_2", "voc")
    )
    placed = (P(REF, None, "voc"), P(None, None, VOC_REF), P(None, None, VOC_REF), P(REF), P(), P())
    return jax.shard_map(
        body, mesh=finer, in_specs=placed, out_specs=(P(None, None, VOC_REF), P()), check_vma=False
    )
```

```python
import jax
import jax.numpy as jnp
from jax import lax
from jax.experimental import pallas as pl
from jax.experimental.pallas import tpu as pltpu
from jax.sharding import Mesh
from jax.sharding import PartitionSpec as P

REF_VOC = ("ref_0", "ref_1", "ref_2", "voc")
REF = ("ref_0", "ref_1", "ref_2")
CHIP = ("ref_0", "ref_1")
CORE = "ref_2"
VOC_REF = ("voc", "ref_0", "ref_1", "ref_2")

clip_bound = 2.0

LANES = 128
WIDE = 512
TILES = WIDE // LANES
WINDOW = WIDE + LANES
GROUP = 4
AROUND = (2, 1, 3, 0)
LEAD = LANES

PARAMS = pltpu.CompilerParams(vmem_limit_bytes=16 << 20)
SMEM = pl.BlockSpec(memory_space=pltpu.SMEM)
VMEM = pl.BlockSpec(memory_space=pltpu.VMEM)
HBM = pl.BlockSpec(memory_space=pltpu.HBM)


def tile_of(x, k):
    return x[:, k * LANES : (k + 1) * LANES]


def turned(tiles, shift, lane):
    spun = [pltpu.roll(tile, shift, 1) for tile in tiles]
    return [jnp.where(lane >= shift, spun[k], spun[k - 1]) for k in range(TILES)]


def turned_back(tiles, shift, lane):
    back = LANES - shift
    spun = [pltpu.roll(tile, back, 1) for tile in tiles]
    return [jnp.where(lane < back, spun[k], spun[(k + 1) % TILES]) for k in range(TILES)]


def lanes_of(shape):
    return lax.broadcasted_iota(jnp.int32, shape, len(shape) - 1)


def rows_of(array, scratch):
    texts, positions, piece = array.shape
    for t in range(texts):
        part = slice(t * positions, (t + 1) * positions)
        scratch[part, :piece] = array[t].astype(jnp.float32)
    values = scratch[...]
    lane = lanes_of((texts * positions, LANES))
    return [
        jnp.where(lane + k * LANES < piece, tile_of(values, k), 0.0) for k in range(TILES)
    ]


def column_of(lane, k, shift):
    return (lane + k * LANES - shift) & (WIDE - 1)


def place_of(sizes):
    chip = lax.axis_index("ref_0") * sizes[1] + lax.axis_index("ref_1")
    return chip, lax.axis_index("ref_2")


def turn_of(sizes, piece):
    chip, core = place_of(sizes)
    return ((2 * chip + core) * piece) & (LANES - 1)


def inside_text(row, t, positions):
    return (row >= t * positions) & (row < (t + 1) * positions)


def turn_kernel(sizes):
    def kernel(public, near, out, number, scratch):
        texts, positions, piece = public.shape
        square = number.shape
        lane = lanes_of(square)
        row = lax.broadcasted_iota(jnp.int32, square, 0)
        shift = turn_of(sizes, piece)
        for k, tile in enumerate(turned(rows_of(public, scratch), shift, lane)):
            out[:, k * LANES : (k + 1) * LANES] = tile
        many = jnp.zeros(square, jnp.float32)
        for t in range(texts):
            held = jnp.int32(0)
            for r in range(near.shape[0]):
                held += jnp.where(near[r] == t, 1, 0)
            many = jnp.where(inside_text(row, t, positions), held.astype(jnp.float32), many)
        number[...] = many

    return kernel


def mark_kernel(sizes, piece, positions):
    def kernel(one, number, far, out):
        square = number.shape
        row = lax.broadcasted_iota(jnp.int32, square, 0)
        lane = lanes_of(square)
        shift = turn_of(sizes, piece)
        many = number[...]
        for t in range(square[0] // positions):
            held = jnp.sum(jnp.where(far[...] == t, 1.0, 0.0), axis=1, keepdims=True)
            held = jnp.broadcast_to(held, square)
            many = many + jnp.where(inside_text(row, t, positions), held, 0.0)
        for k in range(TILES):
            tile = one[:, k * LANES : (k + 1) * LANES]
            tile = jnp.where(column_of(lane, k, shift) < piece, tile, many)
            tile = tile.astype(out.dtype)
            for j in range(out.shape[0]):
                out[j, :, k * LANES : (k + 1) * LANES] = tile

    return kernel


class Rows:
    def __init__(self, plan, priv, swapped):
        rows, self.positions, self.columns = priv.shape
        self.entries = []
        for h, held in enumerate((priv, swapped)):
            for r in range(rows):
                at = h * rows + r
                self.entries.append((held, r, plan[at], plan[2 * rows + at]))


def begins(j, core, piece):
    start = (2 * j + core) * piece
    base = start // LANES * LANES
    return pl.multiple_of(base, LANES), start - base


def widen_into(pub, place, value, positions):
    for t in range(pub.shape[0]):
        part = value[t * positions : (t + 1) * positions]
        pub[t, :, pl.ds(pl.multiple_of(place * WINDOW, LANES), WIDE)] = part
        pub[t, :, pl.ds(pl.multiple_of(place * WINDOW + WIDE, LANES), LANES)] = part[:, :LANES]


def fill_strip(rows, strip, entries):
    last = rows.columns // LANES * LANES
    for e in entries:
        held, r = rows.entries[e][:2]
        strip[e] = jnp.zeros(strip.shape[1:], strip.dtype)
        strip[e, :, : rows.columns - last] = held[r, :, last:]


def sum_windows(rows, pub, acc, core, piece, scale, windows, strip=None):
    clear(rows, acc, 0, len(windows))
    add_rows(rows, pub, acc, core, piece, windows, range(len(rows.entries)), 0, strip)
    store_sums(rows, acc, core, piece, scale, windows, 0)


def clear(rows, acc, first, many):
    texts = acc.shape[0] - 1
    acc[:texts, :, first * WINDOW : (first + many) * WINDOW] = jnp.zeros(
        (texts, rows.positions, many * WINDOW), jnp.float32
    )


def add_rows(rows, pub, acc, core, piece, windows, entries, first, strip=None):
    whole = rows.columns // LANES * LANES
    bases = [begins(j, core, piece)[0] for j, _, _ in windows]
    at = [pl.multiple_of(place * WINDOW, LANES) for _, place, _ in windows]
    if strip is not None:
        fill_strip(rows, strip, entries)
        ends = [base + WINDOW > rows.columns for base in bases]
        edges = [pl.multiple_of(jnp.minimum(base + WIDE, whole - LANES), LANES) for base in bases]
    for e in entries:
        held, r, text, slot = rows.entries[e]
        for g in range(len(windows)):
            size = WINDOW if strip is None else WIDE
            parts = [(0, held[r, :, pl.ds(bases[g], size)])]
            if strip is not None:
                parts.append((WIDE, jnp.where(ends[g], strip[e], held[r, :, pl.ds(edges[g], LANES)])))
            for offset, value in parts:
                width = value.shape[1]
                beside = pub[text, :, pl.ds(pl.multiple_of(at[g] + offset, LANES), width)]
                value = jnp.clip(value.astype(jnp.float32) - beside, -clip_bound, clip_bound)
                start = (first + g) * WINDOW + offset
                acc[slot, :, start : start + width] = acc[slot, :, start : start + width] + value


def store_sums(rows, acc, core, piece, scale, windows, first):
    texts = acc.shape[0] - 1
    lane = lanes_of((texts * rows.positions, LANES))
    for g, (j, _, store) in enumerate(windows):
        shift = begins(j, core, piece)[1]
        tiles = [
            jnp.concatenate(
                [tile_at(acc, t, (first + g) * WINDOW + k * LANES) for t in range(texts)],
                axis=0,
            )
            for k in range(TILES + 1)
        ]
        tiles[0] = jnp.where(lane >= shift, tiles[0], tiles[TILES])
        for k in range(TILES):
            fixed = jnp.round(tiles[k] * scale).astype(jnp.int32).astype(jnp.int16)
            store(slice(k * LANES, (k + 1) * LANES), fixed)


def tile_at(acc, t, start):
    return acc[t, :, start : start + LANES]


def storing(out, index):
    def store(part, value):
        out[index, :, part] = value

    return store


def far_kernel(sizes, scale, piece):
    def kernel(
        owner_there, partner_there, counts_there, source, swapped, own,
        out, priv, plan,
        pub, acc, strip, owner, partner, counts, left, arrived, small,
    ):
        rows, positions, columns = priv.shape
        texts = pub.shape[0]
        chips, flat, _ = own.shape
        lines, beside = sizes
        chip, core = place_of(sizes)
        mine = lax.axis_index("ref_1")
        lane = lanes_of((flat, LANES))
        row = lax.broadcasted_iota(jnp.int32, (flat, LANES), 0)

        stride = 2 * beside * piece
        stride = -(-stride // LANES) * LANES

        def copy_of(i, start, width):
            return pltpu.make_async_copy(
                source.at[:, :, pl.ds(start, width)],
                priv.at[:, :, pl.ds(start, width)],
                arrived.at[i],
            )

        first_chunk = (0, 0, stride + LEAD)
        last_start = LEAD + (lines - 1) * stride
        last_chunk = (lines - 1, last_start, columns - last_start)
        pairs = ((owner_there, owner), (partner_there, partner), (counts_there, counts))
        little = [
            pltpu.make_async_copy(there, here, small.at[i]) for i, (there, here) in enumerate(pairs)
        ]
        for copy in little:
            copy.start()
        copy_of(*first_chunk).start()
        for i in range(1, lines - 1):
            copy_of(i, LEAD + i * stride, stride).start()
        copy_of(*last_chunk).start()

        def widen(i, earlier):
            for n in range(beside):
                j = beside * i + (mine ^ AROUND[n])
                value = own[j].astype(jnp.float32)
                if n == 0:
                    widen_into(pub, i, value, positions)
                shift = begins(j, core, piece)[1]
                free = jnp.where(shift == 0, LANES - 1, shift - 1)
                tile = jnp.where(shift == 0, tile_of(value, TILES - 1), tile_of(value, 0))
                free = jnp.where(j < chip, free, LANES)
                earlier = earlier + jnp.where(lane == free, tile, 0.0)
            return earlier

        earlier = lax.fori_loop(0, lines, widen, jnp.zeros((flat, LANES), jnp.float32))
        for copy in little:
            copy.wait()
        for t in range(texts):
            here = jnp.where(row == t * positions, earlier, 0.0)
            left[t] = counts[t] - jnp.sum(here).astype(jnp.int32)

        for c in range(2):
            for r in range(rows):
                text = jnp.where(core == c, owner[r], partner[r])
                still = left[text]
                left[text] = still - 1
                at = jnp.where(core == c, r, rows + r)
                plan[at] = text
                plan[2 * rows + at] = jnp.where(still > 0, text, texts)
        acc[texts] = jnp.zeros(acc.shape[1:], jnp.float32)
        held = Rows(plan, priv, swapped)
        windows = [(beside * i + (mine ^ AROUND[0]), i, storing(out, i)) for i in range(lines)]
        clear(held, acc, 0, lines)

        def add(entries, first):
            batch = windows[first : first + GROUP]
            edge = strip if first + GROUP == lines else None
            add_rows(held, pub, acc, core, piece, batch, entries, first, edge)

        for first in range(0, lines, GROUP):
            add(range(rows, 2 * rows), first)
        copies = {0: first_chunk, lines - 1: last_chunk}
        for first in range(0, lines, GROUP):
            for i in range(first, first + GROUP):
                copy_of(*copies.get(i, (i, LEAD + i * stride, stride))).wait()
            add(range(rows), first)
            store_sums(held, acc, core, piece, scale, windows[first : first + GROUP], first)

    return kernel


def near_kernel(sizes, scale, piece):
    def kernel(plan, priv, swapped, own, out_1, out_2, pub, acc, strip):
        texts = pub.shape[0]
        lines, beside = sizes
        chip, core = place_of(sizes)
        mine = lax.axis_index("ref_1")
        held = Rows(plan, priv, swapped)
        acc[texts] = jnp.zeros(acc.shape[1:], jnp.float32)
        step = GROUP // 2

        def some(first, strip=None):
            windows = []
            for k in range(step):
                i = first + k
                for n, out in ((1, out_1), (2, out_2)):
                    j = beside * i + (mine ^ AROUND[n])
                    place = 2 * k + n - 1
                    widen_into(pub, place, own[j].astype(jnp.float32), held.positions)
                    windows.append((j, place, storing(out, i)))
            sum_windows(held, pub, acc, core, piece, scale, windows, strip)

        def looped(b, carry):
            some(b * step)
            return carry

        lax.fori_loop(0, lines // step - 1, looped, 0)
        some(lines - step, strip)

    return kernel


def own_kernel(sizes, scale, piece):
    def kernel(
        public, noise, counts, tokens, plan, priv, swapped, own,
        out, base, chosen, level, factor,
        pub, acc, strip, scratch,
    ):
        texts = pub.shape[0]
        lines, beside = sizes
        chip, core = place_of(sizes)
        mine = lax.axis_index("ref_1")
        held = Rows(plan, priv, swapped)
        for i in range(lines):
            widen_into(pub, i, own[beside * i + mine].astype(jnp.float32), held.positions)
        acc[texts] = jnp.zeros(acc.shape[1:], jnp.float32)
        for first in range(0, lines, GROUP):
            windows = [(beside * i + mine, i, storing(out, i)) for i in range(first, first + GROUP)]
            last = first + GROUP == lines
            sum_windows(held, pub, acc, core, piece, scale, windows, strip if last else None)
        prepare(sizes, scale / beside, public, noise, counts, tokens, scratch, base, chosen, level, factor)

    return kernel


def join_kernel(a, b, c, d, out):
    for i in range(out.shape[0]):
        total = (a[i].astype(jnp.int32) + b[i].astype(jnp.int32)) + (
            c[i].astype(jnp.int32) + d[i].astype(jnp.int32)
        )
        total = jnp.round(total.astype(jnp.float32) * 0.25)
        out[i] = total.astype(jnp.int32).astype(jnp.int16)


def prepare(sizes, scale_of, public, noise, counts, tokens, scratch, base, chosen, level, factor):
    texts, positions, piece = public.shape
    square = (texts * positions, LANES)
    lane = lanes_of(square)
    row = lax.broadcasted_iota(jnp.int32, square, 0)
    shift = turn_of(sizes, piece)
    chip, core = place_of(sizes)
    chips = sizes[0] * sizes[1]
    first = (lax.axis_index("voc") * 2 * chips + 2 * chip + core) * piece
    number = jnp.ones(square, jnp.float32)
    token = jnp.zeros(square, jnp.int32)
    for t in range(texts):
        number = jnp.where(inside_text(row, t, positions), counts[t].astype(jnp.float32), number)
        for p in range(positions):
            token = jnp.where(row == t * positions + p, tokens[t, p] - first, token)
    factor[...] = (1.0 / scale_of) / (clip_bound * jnp.sqrt(number))
    public_tiles = turned(rows_of(public, scratch.at[0]), shift, lane)
    noise_tiles = turned(rows_of(noise, scratch.at[1]), shift, lane)
    top = jnp.full(square, -jnp.inf, jnp.float32)
    for k in range(TILES):
        column = column_of(lane, k, shift)
        inside = column < piece
        part = slice(k * LANES, (k + 1) * LANES)
        top = jnp.maximum(top, jnp.where(inside, public_tiles[k], -jnp.inf))
        base[:, part] = jnp.where(inside, public_tiles[k] + noise_tiles[k], -jnp.inf)
        chosen[:, part] = jnp.where(inside & (column == token), 1.0, 0.0)
    level[...] = jnp.broadcast_to(jnp.max(top, axis=1, keepdims=True), square)


def finish_kernel(parts, base, chosen, level, scale, combined, stats):
    flat = base.shape[0]
    square = (flat, LANES)
    lane = lanes_of(square)
    row = lax.broadcasted_iota(jnp.int32, square, 0)
    terms = jnp.zeros(square, jnp.float32)
    picked = jnp.zeros(square, jnp.float32)
    for k in range(TILES):
        part = slice(k * LANES, (k + 1) * LANES)
        total = parts[0, :, part].astype(jnp.int32)
        for j in range(1, parts.shape[0]):
            total = total + parts[j, :, part].astype(jnp.int32)
        tile = base[:, part] + total.astype(jnp.float32) * scale[...]
        combined[:, part] = tile
        terms = terms + jnp.exp(tile - level[...])
        picked = picked + jnp.where(chosen[:, part] > 0.0, tile, 0.0)
    terms = jnp.sum(terms, axis=1, keepdims=True)
    picked = jnp.sum(picked, axis=1, keepdims=True)
    spread = jnp.where(lane == row, terms, 0.0)
    spread = spread + jnp.where(lane == row + flat, picked, 0.0)
    spread = spread + jnp.where(lane == row + 2 * flat, level[...], 0.0)
    stats[...] = jnp.sum(spread, axis=0, keepdims=True)


def last_kernel(sizes):
    def kernel(everyone, combined, logprobs, target, natural):
        texts, positions, piece = logprobs.shape
        flat = texts * positions
        values = everyone[...]
        lane = lanes_of((1, LANES))
        level = jnp.max(values, axis=0, keepdims=True)
        weight = pltpu.roll(jnp.exp(values - level), LANES - 2 * flat, 1)
        total = jnp.sum(values * weight, axis=0, keepdims=True)
        picked = pltpu.roll(jnp.sum(values, axis=0, keepdims=True), LANES - flat, 1)
        level = pltpu.roll(level, LANES - 2 * flat, 1)
        own = lane < flat
        lse = jnp.where(own, level + jnp.log(jnp.where(own, total, 1.0)), 0.0)
        picked = picked - lse
        square = (flat, LANES)
        mine = lanes_of(square) == lax.broadcasted_iota(jnp.int32, square, 0)
        column = jnp.sum(jnp.where(mine, jnp.broadcast_to(lse, square), 0.0), axis=1, keepdims=True)
        tiles = [combined[:, k * LANES : (k + 1) * LANES] - column for k in range(TILES)]
        for k, tile in enumerate(turned_back(tiles, turn_of(sizes, piece), lanes_of(square))):
            natural[:, k * LANES : (k + 1) * LANES] = tile
        shifted = natural[:, :piece]
        for t in range(texts):
            logprobs[t] = shifted[t * positions : (t + 1) * positions]
        for t in range(texts):
            turn = picked if t == 0 else pltpu.roll(picked, LANES - t * positions, 1)
            target[t : t + 1, :] = turn[:, :positions]

    return kernel


def body(private_logits, public_logits, noise, owner, counts, tokens):
    texts, positions, piece = public_logits.shape
    rows = owner.shape[0]
    flat = texts * positions
    sizes = (lax.axis_size("ref_0"), lax.axis_size("ref_1"))
    chips = sizes[0] * sizes[1]
    swap = [(0, 1), (1, 0)]
    scale = float(32767 // (2 * rows * int(clip_bound)))
    square = pltpu.VMEM((flat, LANES), jnp.float32)
    long = pltpu.VMEM((flat, WIDE), jnp.float32)
    owner_there, counts_there, tokens_there, public_there, noise_there, private_there = (
        pltpu.with_memory_space_constraint(x, pltpu.HBM)
        for x in (owner, counts, tokens, public_logits, noise, private_logits)
    )

    partner = lax.ppermute(owner, CORE, swap)
    one, number = pl.pallas_call(
        turn_kernel(sizes),
        out_shape=(long, square),
        in_specs=[VMEM, SMEM],
        out_specs=(VMEM, VMEM),
        scratch_shapes=[pltpu.VMEM((flat, WIDE), jnp.float32)],
        compiler_params=PARAMS,
        name="turn",
    )(public_there, owner_there)
    partner, private_later, one = lax.optimization_barrier((partner, private_logits, one))
    swapped = lax.ppermute(private_later, CORE, swap)
    packed = pl.pallas_call(
        mark_kernel(sizes, piece, positions),
        out_shape=pltpu.VMEM((chips, flat, WIDE), jnp.bfloat16),
        in_specs=[VMEM, VMEM, VMEM],
        out_specs=VMEM,
        compiler_params=PARAMS,
        name="mark",
    )(one, number, partner.reshape(1, rows))
    own = lax.all_to_all(packed, CHIP, split_axis=0, concat_axis=0, tiled=True)
    swapped, own, partner = (
        pltpu.with_memory_space_constraint(x, pltpu.VMEM) for x in (swapped, own, partner)
    )
    lines, beside = sizes
    line_sums = pltpu.VMEM((lines, flat, WIDE), jnp.int16)
    windows = lines * WINDOW
    sums_scratch = pltpu.VMEM((texts + 1, positions, GROUP * WINDOW), jnp.float32)
    strip = pltpu.VMEM((2 * rows, positions, LANES), private_logits.dtype)

    def beyond(x, m):
        return lax.ppermute(x, "ref_1", [(k, k ^ m) for k in range(beside)])

    far, private_here, plan = pl.pallas_call(
        far_kernel(sizes, scale, piece),
        out_shape=(
            line_sums,
            pltpu.VMEM(private_logits.shape, private_logits.dtype),
            jax.ShapeDtypeStruct((4 * rows,), jnp.int32),
        ),
        in_specs=[HBM, VMEM, HBM, HBM, VMEM, VMEM],
        out_specs=(VMEM, VMEM, SMEM),
        scratch_shapes=[
            pltpu.VMEM((texts, positions, windows), jnp.float32),
            pltpu.VMEM((texts + 1, positions, windows), jnp.float32),
            strip,
            pltpu.SMEM((rows,), jnp.int32),
            pltpu.SMEM((rows,), jnp.int32),
            pltpu.SMEM((texts,), jnp.int32),
            pltpu.SMEM((texts,), jnp.int32),
            pltpu.SemaphoreType.DMA((lines,)),
            pltpu.SemaphoreType.DMA((3,)),
        ],
        compiler_params=PARAMS,
        name="far_sums",
    )(owner_there, partner, counts_there, private_there, swapped, own)
    got = [beyond(far, AROUND[0])]
    near = pl.pallas_call(
        near_kernel(sizes, scale, piece),
        out_shape=(line_sums, line_sums),
        in_specs=[SMEM, VMEM, VMEM, VMEM],
        out_specs=(VMEM, VMEM),
        scratch_shapes=[
            pltpu.VMEM((texts, positions, GROUP * WINDOW), jnp.float32),
            sums_scratch,
            strip,
        ],
        compiler_params=PARAMS,
        name="near_sums",
    )(plan, private_here, swapped, own)
    got += [beyond(x, m) for x, m in zip(near, AROUND[1:])]
    near_done, own_later = lax.optimization_barrier((near[0], own))
    line, base, chosen, level, factor = pl.pallas_call(
        own_kernel(sizes, scale, piece),
        out_shape=(line_sums, long, long, square, square),
        in_specs=[VMEM, VMEM, SMEM, SMEM, SMEM, VMEM, VMEM, VMEM],
        out_specs=(VMEM,) * 5,
        scratch_shapes=[
            pltpu.VMEM((texts, positions, windows), jnp.float32),
            sums_scratch,
            strip,
            pltpu.VMEM((2, flat, WIDE), jnp.float32),
        ],
        compiler_params=PARAMS,
        name="own_sums",
    )(public_there, noise_there, counts_there, tokens_there, plan, private_here, swapped, own_later)
    joined = pl.pallas_call(
        join_kernel,
        out_shape=line_sums,
        in_specs=[VMEM] * 4,
        out_specs=VMEM,
        compiler_params=PARAMS,
        name="join",
    )(line, *[pltpu.with_memory_space_constraint(x, pltpu.VMEM) for x in got])
    parts = lax.all_to_all(joined, "ref_0", split_axis=0, concat_axis=0, tiled=True)
    parts = pltpu.with_memory_space_constraint(parts, pltpu.VMEM)
    combined, stats = pl.pallas_call(
        finish_kernel,
        out_shape=(long, pltpu.VMEM((1, LANES), jnp.float32)),
        in_specs=[VMEM] * 5,
        out_specs=(VMEM, VMEM),
        compiler_params=PARAMS,
        name="finish",
    )(parts, base, chosen, level, factor)

    devices = lax.axis_size(REF_VOC)
    everyone = lax.all_to_all(
        jnp.broadcast_to(stats, (devices, 1, LANES)), REF_VOC, split_axis=0, concat_axis=0, tiled=True
    ).reshape(devices, LANES)
    return pl.pallas_call(
        last_kernel(sizes),
        out_shape=(
            jax.ShapeDtypeStruct(public_logits.shape, jnp.float32),
            jax.ShapeDtypeStruct((texts, positions), jnp.float32),
        ),
        in_specs=[VMEM, VMEM],
        out_specs=(VMEM, VMEM),
        scratch_shapes=[pltpu.VMEM((flat, WIDE), jnp.float32)],
        compiler_params=PARAMS,
        name="last",
    )(pltpu.with_memory_space_constraint(everyone, pltpu.VMEM), combined)


def solution(mesh):
    finer = Mesh(
        mesh.devices.reshape(8, 4, 2, mesh.shape["voc"]), ("ref_0", "ref_1", "ref_2", "voc")
    )
    placed = (P(REF, None, "voc"), P(None, None, VOC_REF), P(None, None, VOC_REF), P(REF), P(), P())
    return jax.shard_map(
        body, mesh=finer, in_specs=placed, out_specs=(P(None, None, VOC_REF), P()), check_vma=False
    )
```

```python
import jax
import jax.numpy as jnp
from jax import lax
from jax.experimental import pallas as pl
from jax.experimental.pallas import tpu as pltpu
from jax.sharding import Mesh
from jax.sharding import PartitionSpec as P

REF_VOC = ("ref_0", "ref_1", "ref_2", "voc")
REF = ("ref_0", "ref_1", "ref_2")
CHIP = ("ref_0", "ref_1")
CORE = "ref_2"
VOC_REF = ("voc", "ref_0", "ref_1", "ref_2")

clip_bound = 2.0

LANES = 128
WIDE = 512
TILES = WIDE // LANES
WINDOW = WIDE + LANES
GROUP = 4
AROUND = (2, 1, 3, 0)

PARAMS = pltpu.CompilerParams(vmem_limit_bytes=16 << 20)
SMEM = pl.BlockSpec(memory_space=pltpu.SMEM)
VMEM = pl.BlockSpec(memory_space=pltpu.VMEM)
HBM = pl.BlockSpec(memory_space=pltpu.HBM)


def tile_of(x, k):
    return x[:, k * LANES : (k + 1) * LANES]


def turned(tiles, shift, lane):
    spun = [pltpu.roll(tile, shift, 1) for tile in tiles]
    return [jnp.where(lane >= shift, spun[k], spun[k - 1]) for k in range(TILES)]


def turned_back(tiles, shift, lane):
    back = LANES - shift
    spun = [pltpu.roll(tile, back, 1) for tile in tiles]
    return [jnp.where(lane < back, spun[k], spun[(k + 1) % TILES]) for k in range(TILES)]


def lanes_of(shape):
    return lax.broadcasted_iota(jnp.int32, shape, len(shape) - 1)


def rows_of(array, scratch):
    texts, positions, piece = array.shape
    for t in range(texts):
        part = slice(t * positions, (t + 1) * positions)
        scratch[part, :piece] = array[t].astype(jnp.float32)
    values = scratch[...]
    lane = lanes_of((texts * positions, LANES))
    return [
        jnp.where(lane + k * LANES < piece, tile_of(values, k), 0.0) for k in range(TILES)
    ]


def column_of(lane, k, shift):
    return (lane + k * LANES - shift) & (WIDE - 1)


def place_of(sizes):
    chip = lax.axis_index("ref_0") * sizes[1] + lax.axis_index("ref_1")
    return chip, lax.axis_index("ref_2")


def turn_of(sizes, piece):
    chip, core = place_of(sizes)
    return ((2 * chip + core) * piece) & (LANES - 1)


def inside_text(row, t, positions):
    return (row >= t * positions) & (row < (t + 1) * positions)


def turn_kernel(sizes):
    def kernel(public, near, out, number, scratch):
        texts, positions, piece = public.shape
        square = number.shape
        lane = lanes_of(square)
        row = lax.broadcasted_iota(jnp.int32, square, 0)
        shift = turn_of(sizes, piece)
        for k, tile in enumerate(turned(rows_of(public, scratch), shift, lane)):
            out[:, k * LANES : (k + 1) * LANES] = tile
        many = jnp.zeros(square, jnp.float32)
        for t in range(texts):
            held = jnp.int32(0)
            for r in range(near.shape[0]):
                held += jnp.where(near[r] == t, 1, 0)
            many = jnp.where(inside_text(row, t, positions), held.astype(jnp.float32), many)
        number[...] = many

    return kernel


def mark_kernel(sizes, piece, positions):
    def kernel(one, number, far, out):
        square = number.shape
        row = lax.broadcasted_iota(jnp.int32, square, 0)
        lane = lanes_of(square)
        shift = turn_of(sizes, piece)
        many = number[...]
        for t in range(square[0] // positions):
            held = jnp.sum(jnp.where(far[...] == t, 1.0, 0.0), axis=1, keepdims=True)
            held = jnp.broadcast_to(held, square)
            many = many + jnp.where(inside_text(row, t, positions), held, 0.0)
        for k in range(TILES):
            tile = one[:, k * LANES : (k + 1) * LANES]
            tile = jnp.where(column_of(lane, k, shift) < piece, tile, many)
            tile = tile.astype(out.dtype)
            for j in range(out.shape[0]):
                out[j, :, k * LANES : (k + 1) * LANES] = tile

    return kernel


class Rows:
    def __init__(self, plan, priv, swapped):
        rows, self.positions, self.columns = swapped.shape
        self.entries = []
        for h, held in enumerate((priv, swapped)):
            for r in range(rows):
                at = h * rows + r
                self.entries.append((held, r, plan[at], plan[2 * rows + at], h == 0))


def begins(j, core, piece):
    start = (2 * j + core) * piece
    base = start // LANES * LANES
    return pl.multiple_of(base, LANES), start - base


def widen_into(pub, place, value, positions):
    for t in range(pub.shape[0]):
        part = value[t * positions : (t + 1) * positions]
        pub[t, :, pl.ds(pl.multiple_of(place * WINDOW, LANES), WIDE)] = part
        pub[t, :, pl.ds(pl.multiple_of(place * WINDOW + WIDE, LANES), LANES)] = part[:, :LANES]


def fill_strip(rows, strip, entries):
    last = rows.columns // LANES * LANES
    for e in entries:
        held, r, _, _, packed = rows.entries[e]
        if packed:
            continue
        strip[e] = jnp.zeros(strip.shape[1:], strip.dtype)
        strip[e, :, : rows.columns - last] = held[r, :, last:]


def sum_windows(rows, pub, acc, core, piece, scale, windows, strip=None):
    clear(rows, acc, 0, len(windows))
    add_rows(rows, pub, acc, core, piece, windows, range(len(rows.entries)), 0, strip)
    store_sums(rows, acc, core, piece, scale, windows, 0)


def clear(rows, acc, first, many):
    texts = acc.shape[0] - 1
    acc[:texts, :, first * WINDOW : (first + many) * WINDOW] = jnp.zeros(
        (texts, rows.positions, many * WINDOW), jnp.float32
    )


def add_rows(rows, pub, acc, core, piece, windows, entries, first, strip=None):
    whole = rows.columns // LANES * LANES
    bases = [begins(window[0], core, piece)[0] for window in windows]
    at = [pl.multiple_of(window[1] * WINDOW, LANES) for window in windows]
    packs = [pl.multiple_of(window[3] * WINDOW, LANES) for window in windows]
    if strip is not None:
        fill_strip(rows, strip, entries)
        ends = [base + WINDOW > rows.columns for base in bases]
        edges = [pl.multiple_of(jnp.minimum(base + WIDE, whole - LANES), LANES) for base in bases]
    for e in entries:
        held, r, text, slot, packed = rows.entries[e]
        for g in range(len(windows)):
            size = WINDOW if strip is None or packed else WIDE
            parts = [(0, held[r, :, pl.ds(packs[g] if packed else bases[g], size)])]
            if size == WIDE:
                parts.append((WIDE, jnp.where(ends[g], strip[e], held[r, :, pl.ds(edges[g], LANES)])))
            for offset, value in parts:
                width = value.shape[1]
                beside = pub[text, :, pl.ds(pl.multiple_of(at[g] + offset, LANES), width)]
                value = jnp.clip(value.astype(jnp.float32) - beside, -clip_bound, clip_bound)
                start = (first + g) * WINDOW + offset
                acc[slot, :, start : start + width] = acc[slot, :, start : start + width] + value


def store_sums(rows, acc, core, piece, scale, windows, first):
    texts = acc.shape[0] - 1
    lane = lanes_of((texts * rows.positions, LANES))
    for g, (j, _, store, _) in enumerate(windows):
        shift = begins(j, core, piece)[1]
        tiles = [
            jnp.concatenate(
                [tile_at(acc, t, (first + g) * WINDOW + k * LANES) for t in range(texts)],
                axis=0,
            )
            for k in range(TILES + 1)
        ]
        tiles[0] = jnp.where(lane >= shift, tiles[0], tiles[TILES])
        for k in range(TILES):
            fixed = jnp.round(tiles[k] * scale).astype(jnp.int32).astype(jnp.int16)
            store(slice(k * LANES, (k + 1) * LANES), fixed)


def tile_at(acc, t, start):
    return acc[t, :, start : start + LANES]


def storing(out, index):
    def store(part, value):
        out[index, :, part] = value

    return store


def far_kernel(sizes, scale, piece):
    def kernel(
        owner_there, partner_there, counts_there, source, swapped, own,
        out, priv, plan,
        pub, acc, strip, tail, owner, partner, counts, left, arrived, small,
    ):
        rows, positions, columns = swapped.shape
        texts = pub.shape[0]
        chips, flat, _ = own.shape
        lines, beside = sizes
        chip, core = place_of(sizes)
        mine = lax.axis_index("ref_1")
        lane = lanes_of((flat, LANES))
        row = lax.broadcasted_iota(jnp.int32, (flat, LANES), 0)

        def piece_of(n, i):
            return beside * i + (mine ^ AROUND[n])

        def copy_of(n, i, width=WINDOW):
            start = begins(piece_of(n, i), core, piece)[0]
            place = n * lines + i
            return pltpu.make_async_copy(
                source.at[:, :, pl.ds(start, width)],
                priv.at[:, :, place * WINDOW : place * WINDOW + width],
                arrived.at[place],
            )

        whole = columns // LANES * LANES
        tail_copy = pltpu.make_async_copy(source.at[:, :, whole:], tail, small.at[3])

        def fill_tail(n):
            place = (n + 1) * lines - 1
            ends = begins(piece_of(n, lines - 1), core, piece)[0] + WINDOW > columns
            start = place * WINDOW + WIDE

            @pl.when(ends)
            def _():
                for r in range(rows):
                    priv[r, :, start : start + columns - whole] = tail[r]

        def each_copy(n, i, act):
            if i < lines - 1:
                act(copy_of(n, i))
                return
            ends = begins(piece_of(n, i), core, piece)[0] + WINDOW > columns

            @pl.when(ends)
            def _():
                act(copy_of(n, i, WIDE))

            @pl.when(jnp.logical_not(ends))
            def _():
                act(copy_of(n, i))

        pairs = ((owner_there, owner), (partner_there, partner), (counts_there, counts))
        little = [
            pltpu.make_async_copy(there, here, small.at[i]) for i, (there, here) in enumerate(pairs)
        ]
        for copy in little:
            copy.start()
        tail_copy.start()
        for n in range(beside):
            for i in range(lines):
                each_copy(n, i, lambda copy: copy.start())

        def widen(i, earlier):
            for n in range(beside):
                j = beside * i + (mine ^ AROUND[n])
                value = own[j].astype(jnp.float32)
                if n == 0:
                    widen_into(pub, i, value, positions)
                shift = begins(j, core, piece)[1]
                free = jnp.where(shift == 0, LANES - 1, shift - 1)
                tile = jnp.where(shift == 0, tile_of(value, TILES - 1), tile_of(value, 0))
                free = jnp.where(j < chip, free, LANES)
                earlier = earlier + jnp.where(lane == free, tile, 0.0)
            return earlier

        earlier = lax.fori_loop(0, lines, widen, jnp.zeros((flat, LANES), jnp.float32))
        for copy in little:
            copy.wait()
        for t in range(texts):
            here = jnp.where(row == t * positions, earlier, 0.0)
            left[t] = counts[t] - jnp.sum(here).astype(jnp.int32)

        for c in range(2):
            for r in range(rows):
                text = jnp.where(core == c, owner[r], partner[r])
                still = left[text]
                left[text] = still - 1
                at = jnp.where(core == c, r, rows + r)
                plan[at] = text
                plan[2 * rows + at] = jnp.where(still > 0, text, texts)
        acc[texts] = jnp.zeros(acc.shape[1:], jnp.float32)
        held = Rows(plan, priv, swapped)
        windows = [(piece_of(0, i), i, storing(out, i), i) for i in range(lines)]
        clear(held, acc, 0, lines)

        def add(entries, first):
            batch = windows[first : first + GROUP]
            edge = strip if first + GROUP == lines else None
            add_rows(held, pub, acc, core, piece, batch, entries, first, edge)

        for first in range(0, lines, GROUP):
            add(range(rows, 2 * rows), first)
        for first in range(0, lines, GROUP):
            for i in range(first, first + GROUP):
                each_copy(0, i, lambda copy: copy.wait())
            if first == 0:
                tail_copy.wait()
            if first + GROUP == lines:
                fill_tail(0)
            add(range(rows), first)
            store_sums(held, acc, core, piece, scale, windows[first : first + GROUP], first)
        for n in range(1, beside):
            for i in range(lines):
                each_copy(n, i, lambda copy: copy.wait())
            fill_tail(n)

    return kernel


def near_kernel(sizes, scale, piece):
    def kernel(plan, priv, swapped, own, out_1, out_2, pub, acc, strip):
        texts = pub.shape[0]
        lines, beside = sizes
        chip, core = place_of(sizes)
        mine = lax.axis_index("ref_1")
        held = Rows(plan, priv, swapped)
        acc[texts] = jnp.zeros(acc.shape[1:], jnp.float32)
        step = GROUP // 2

        def some(first, strip=None):
            windows = []
            for k in range(step):
                i = first + k
                for n, out in ((1, out_1), (2, out_2)):
                    j = beside * i + (mine ^ AROUND[n])
                    place = 2 * k + n - 1
                    widen_into(pub, place, own[j].astype(jnp.float32), held.positions)
                    windows.append((j, place, storing(out, i), n * lines + i))
            sum_windows(held, pub, acc, core, piece, scale, windows, strip)

        def looped(b, carry):
            some(b * step)
            return carry

        lax.fori_loop(0, lines // step - 1, looped, 0)
        some(lines - step, strip)

    return kernel


def own_kernel(sizes, scale, piece):
    def kernel(
        public, noise, counts, tokens, plan, priv, swapped, own,
        out, base, chosen, level, factor,
        pub, acc, strip, scratch,
    ):
        texts = pub.shape[0]
        lines, beside = sizes
        chip, core = place_of(sizes)
        mine = lax.axis_index("ref_1")
        held = Rows(plan, priv, swapped)
        for i in range(lines):
            widen_into(pub, i, own[beside * i + mine].astype(jnp.float32), held.positions)
        acc[texts] = jnp.zeros(acc.shape[1:], jnp.float32)
        for first in range(0, lines, GROUP):
            windows = [
                (beside * i + mine, i, storing(out, i), (beside - 1) * lines + i)
                for i in range(first, first + GROUP)
            ]
            last = first + GROUP == lines
            sum_windows(held, pub, acc, core, piece, scale, windows, strip if last else None)
        prepare(sizes, scale / beside, public, noise, counts, tokens, scratch, base, chosen, level, factor)

    return kernel


def join_kernel(a, b, c, d, out):
    for i in range(out.shape[0]):
        total = (a[i].astype(jnp.int32) + b[i].astype(jnp.int32)) + (
            c[i].astype(jnp.int32) + d[i].astype(jnp.int32)
        )
        total = jnp.round(total.astype(jnp.float32) * 0.25)
        out[i] = total.astype(jnp.int32).astype(jnp.int16)


def prepare(sizes, scale_of, public, noise, counts, tokens, scratch, base, chosen, level, factor):
    texts, positions, piece = public.shape
    square = (texts * positions, LANES)
    lane = lanes_of(square)
    row = lax.broadcasted_iota(jnp.int32, square, 0)
    shift = turn_of(sizes, piece)
    chip, core = place_of(sizes)
    chips = sizes[0] * sizes[1]
    first = (lax.axis_index("voc") * 2 * chips + 2 * chip + core) * piece
    number = jnp.ones(square, jnp.float32)
    token = jnp.zeros(square, jnp.int32)
    for t in range(texts):
        number = jnp.where(inside_text(row, t, positions), counts[t].astype(jnp.float32), number)
        for p in range(positions):
            token = jnp.where(row == t * positions + p, tokens[t, p] - first, token)
    factor[...] = (1.0 / scale_of) / (clip_bound * jnp.sqrt(number))
    public_tiles = turned(rows_of(public, scratch.at[0]), shift, lane)
    noise_tiles = turned(rows_of(noise, scratch.at[1]), shift, lane)
    top = jnp.full(square, -jnp.inf, jnp.float32)
    for k in range(TILES):
        column = column_of(lane, k, shift)
        inside = column < piece
        part = slice(k * LANES, (k + 1) * LANES)
        top = jnp.maximum(top, jnp.where(inside, public_tiles[k], -jnp.inf))
        base[:, part] = jnp.where(inside, public_tiles[k] + noise_tiles[k], -jnp.inf)
        chosen[:, part] = jnp.where(inside & (column == token), 1.0, 0.0)
    level[...] = jnp.broadcast_to(jnp.max(top, axis=1, keepdims=True), square)


def finish_kernel(parts, base, chosen, level, scale, combined, stats):
    flat = base.shape[0]
    square = (flat, LANES)
    lane = lanes_of(square)
    row = lax.broadcasted_iota(jnp.int32, square, 0)
    terms = jnp.zeros(square, jnp.float32)
    picked = jnp.zeros(square, jnp.float32)
    for k in range(TILES):
        part = slice(k * LANES, (k + 1) * LANES)
        total = parts[0, :, part].astype(jnp.int32)
        for j in range(1, parts.shape[0]):
            total = total + parts[j, :, part].astype(jnp.int32)
        tile = base[:, part] + total.astype(jnp.float32) * scale[...]
        combined[:, part] = tile
        terms = terms + jnp.exp(tile - level[...])
        picked = picked + jnp.where(chosen[:, part] > 0.0, tile, 0.0)
    terms = jnp.sum(terms, axis=1, keepdims=True)
    picked = jnp.sum(picked, axis=1, keepdims=True)
    spread = jnp.where(lane == row, terms, 0.0)
    spread = spread + jnp.where(lane == row + flat, picked, 0.0)
    spread = spread + jnp.where(lane == row + 2 * flat, level[...], 0.0)
    stats[...] = jnp.sum(spread, axis=0, keepdims=True)


def last_kernel(sizes):
    def kernel(everyone, combined, logprobs, target, natural):
        texts, positions, piece = logprobs.shape
        flat = texts * positions
        values = everyone[...]
        lane = lanes_of((1, LANES))
        level = jnp.max(values, axis=0, keepdims=True)
        weight = pltpu.roll(jnp.exp(values - level), LANES - 2 * flat, 1)
        total = jnp.sum(values * weight, axis=0, keepdims=True)
        picked = pltpu.roll(jnp.sum(values, axis=0, keepdims=True), LANES - flat, 1)
        level = pltpu.roll(level, LANES - 2 * flat, 1)
        own = lane < flat
        lse = jnp.where(own, level + jnp.log(jnp.where(own, total, 1.0)), 0.0)
        picked = picked - lse
        square = (flat, LANES)
        mine = lanes_of(square) == lax.broadcasted_iota(jnp.int32, square, 0)
        column = jnp.sum(jnp.where(mine, jnp.broadcast_to(lse, square), 0.0), axis=1, keepdims=True)
        tiles = [combined[:, k * LANES : (k + 1) * LANES] - column for k in range(TILES)]
        for k, tile in enumerate(turned_back(tiles, turn_of(sizes, piece), lanes_of(square))):
            natural[:, k * LANES : (k + 1) * LANES] = tile
        shifted = natural[:, :piece]
        for t in range(texts):
            logprobs[t] = shifted[t * positions : (t + 1) * positions]
        for t in range(texts):
            turn = picked if t == 0 else pltpu.roll(picked, LANES - t * positions, 1)
            target[t : t + 1, :] = turn[:, :positions]

    return kernel


def body(private_logits, public_logits, noise, owner, counts, tokens):
    texts, positions, piece = public_logits.shape
    rows, _, columns = private_logits.shape
    flat = texts * positions
    sizes = (lax.axis_size("ref_0"), lax.axis_size("ref_1"))
    chips = sizes[0] * sizes[1]
    swap = [(0, 1), (1, 0)]
    scale = float(32767 // (2 * rows * int(clip_bound)))
    square = pltpu.VMEM((flat, LANES), jnp.float32)
    long = pltpu.VMEM((flat, WIDE), jnp.float32)
    owner_there, counts_there, tokens_there, public_there, noise_there, private_there = (
        pltpu.with_memory_space_constraint(x, pltpu.HBM)
        for x in (owner, counts, tokens, public_logits, noise, private_logits)
    )

    partner = lax.ppermute(owner, CORE, swap)
    one, number = pl.pallas_call(
        turn_kernel(sizes),
        out_shape=(long, square),
        in_specs=[VMEM, SMEM],
        out_specs=(VMEM, VMEM),
        scratch_shapes=[pltpu.VMEM((flat, WIDE), jnp.float32)],
        compiler_params=PARAMS,
        name="turn",
    )(public_there, owner_there)
    partner, private_later, one = lax.optimization_barrier((partner, private_logits, one))
    swapped = lax.ppermute(private_later, CORE, swap)
    packed = pl.pallas_call(
        mark_kernel(sizes, piece, positions),
        out_shape=pltpu.VMEM((chips, flat, WIDE), jnp.bfloat16),
        in_specs=[VMEM, VMEM, VMEM],
        out_specs=VMEM,
        compiler_params=PARAMS,
        name="mark",
    )(one, number, partner.reshape(1, rows))
    own = lax.all_to_all(packed, CHIP, split_axis=0, concat_axis=0, tiled=True)
    swapped, own, partner = (
        pltpu.with_memory_space_constraint(x, pltpu.VMEM) for x in (swapped, own, partner)
    )
    lines, beside = sizes
    line_sums = pltpu.VMEM((lines, flat, WIDE), jnp.int16)
    windows = lines * WINDOW
    sums_scratch = pltpu.VMEM((texts + 1, positions, GROUP * WINDOW), jnp.float32)
    strip = pltpu.VMEM((2 * rows, positions, LANES), private_logits.dtype)

    def beyond(x, m):
        return lax.ppermute(x, "ref_1", [(k, k ^ m) for k in range(beside)])

    far, private_here, plan = pl.pallas_call(
        far_kernel(sizes, scale, piece),
        out_shape=(
            line_sums,
            pltpu.VMEM((rows, positions, beside * windows), private_logits.dtype),
            jax.ShapeDtypeStruct((4 * rows,), jnp.int32),
        ),
        in_specs=[HBM, VMEM, HBM, HBM, VMEM, VMEM],
        out_specs=(VMEM, VMEM, SMEM),
        scratch_shapes=[
            pltpu.VMEM((texts, positions, windows), jnp.float32),
            pltpu.VMEM((texts + 1, positions, windows), jnp.float32),
            strip,
            pltpu.VMEM((rows, positions, columns % LANES), private_logits.dtype),
            pltpu.SMEM((rows,), jnp.int32),
            pltpu.SMEM((rows,), jnp.int32),
            pltpu.SMEM((texts,), jnp.int32),
            pltpu.SMEM((texts,), jnp.int32),
            pltpu.SemaphoreType.DMA((chips,)),
            pltpu.SemaphoreType.DMA((4,)),
        ],
        compiler_params=PARAMS,
        name="far_sums",
    )(owner_there, partner, counts_there, private_there, swapped, own)
    got = [beyond(far, AROUND[0])]
    near = pl.pallas_call(
        near_kernel(sizes, scale, piece),
        out_shape=(line_sums, line_sums),
        in_specs=[SMEM, VMEM, VMEM, VMEM],
        out_specs=(VMEM, VMEM),
        scratch_shapes=[
            pltpu.VMEM((texts, positions, GROUP * WINDOW), jnp.float32),
            sums_scratch,
            strip,
        ],
        compiler_params=PARAMS,
        name="near_sums",
    )(plan, private_here, swapped, own)
    got += [beyond(x, m) for x, m in zip(near, AROUND[1:])]
    near_done, own_later = lax.optimization_barrier((near[0], own))
    line, base, chosen, level, factor = pl.pallas_call(
        own_kernel(sizes, scale, piece),
        out_shape=(line_sums, long, long, square, square),
        in_specs=[VMEM, VMEM, SMEM, SMEM, SMEM, VMEM, VMEM, VMEM],
        out_specs=(VMEM,) * 5,
        scratch_shapes=[
            pltpu.VMEM((texts, positions, windows), jnp.float32),
            sums_scratch,
            strip,
            pltpu.VMEM((2, flat, WIDE), jnp.float32),
        ],
        compiler_params=PARAMS,
        name="own_sums",
    )(public_there, noise_there, counts_there, tokens_there, plan, private_here, swapped, own_later)
    joined = pl.pallas_call(
        join_kernel,
        out_shape=line_sums,
        in_specs=[VMEM] * 4,
        out_specs=VMEM,
        compiler_params=PARAMS,
        name="join",
    )(line, *[pltpu.with_memory_space_constraint(x, pltpu.VMEM) for x in got])
    parts = lax.all_to_all(joined, "ref_0", split_axis=0, concat_axis=0, tiled=True)
    parts = pltpu.with_memory_space_constraint(parts, pltpu.VMEM)
    combined, stats = pl.pallas_call(
        finish_kernel,
        out_shape=(long, pltpu.VMEM((1, LANES), jnp.float32)),
        in_specs=[VMEM] * 5,
        out_specs=(VMEM, VMEM),
        compiler_params=PARAMS,
        name="finish",
    )(parts, base, chosen, level, factor)

    devices = lax.axis_size(REF_VOC)
    everyone = lax.all_to_all(
        jnp.broadcast_to(stats, (devices, 1, LANES)), REF_VOC, split_axis=0, concat_axis=0, tiled=True
    ).reshape(devices, LANES)
    return pl.pallas_call(
        last_kernel(sizes),
        out_shape=(
            jax.ShapeDtypeStruct(public_logits.shape, jnp.float32),
            jax.ShapeDtypeStruct((texts, positions), jnp.float32),
        ),
        in_specs=[VMEM, VMEM],
        out_specs=(VMEM, VMEM),
        scratch_shapes=[pltpu.VMEM((flat, WIDE), jnp.float32)],
        compiler_params=PARAMS,
        name="last",
    )(pltpu.with_memory_space_constraint(everyone, pltpu.VMEM), combined)


def solution(mesh):
    finer = Mesh(
        mesh.devices.reshape(8, 4, 2, mesh.shape["voc"]), ("ref_0", "ref_1", "ref_2", "voc")
    )
    placed = (P(REF, None, "voc"), P(None, None, VOC_REF), P(None, None, VOC_REF), P(REF), P(), P())
    return jax.shard_map(
        body, mesh=finer, in_specs=placed, out_specs=(P(None, None, VOC_REF), P()), check_vma=False
    )
```

```python
import jax
import jax.numpy as jnp
from jax import lax
from jax.experimental import pallas as pl
from jax.experimental.pallas import tpu as pltpu
from jax.sharding import Mesh
from jax.sharding import PartitionSpec as P

REF_VOC = ("ref_0", "ref_1", "ref_2", "voc")
REF = ("ref_0", "ref_1", "ref_2")
CHIP = ("ref_0", "ref_1")
CORE = "ref_2"
VOC_REF = ("voc", "ref_0", "ref_1", "ref_2")

clip_bound = 2.0

LANES = 128
WIDE = 512
TILES = WIDE // LANES
WINDOW = WIDE + LANES
GROUP = 4
AROUND = (2, 1, 3, 0)

PARAMS = pltpu.CompilerParams(vmem_limit_bytes=16 << 20)
SMEM = pl.BlockSpec(memory_space=pltpu.SMEM)
VMEM = pl.BlockSpec(memory_space=pltpu.VMEM)
HBM = pl.BlockSpec(memory_space=pltpu.HBM)


def tile_of(x, k):
    return x[:, k * LANES : (k + 1) * LANES]


def turned(tiles, shift, lane):
    spun = [pltpu.roll(tile, shift, 1) for tile in tiles]
    return [jnp.where(lane >= shift, spun[k], spun[k - 1]) for k in range(TILES)]


def turned_back(tiles, shift, lane):
    back = LANES - shift
    spun = [pltpu.roll(tile, back, 1) for tile in tiles]
    return [jnp.where(lane < back, spun[k], spun[(k + 1) % TILES]) for k in range(TILES)]


def lanes_of(shape):
    return lax.broadcasted_iota(jnp.int32, shape, len(shape) - 1)


def rows_of(array, scratch):
    texts, positions, piece = array.shape
    for t in range(texts):
        part = slice(t * positions, (t + 1) * positions)
        scratch[part, :piece] = array[t].astype(jnp.float32)
    values = scratch[...]
    lane = lanes_of((texts * positions, LANES))
    return [
        jnp.where(lane + k * LANES < piece, tile_of(values, k), 0.0) for k in range(TILES)
    ]


def column_of(lane, k, shift):
    return (lane + k * LANES - shift) & (WIDE - 1)


def place_of(sizes):
    chip = lax.axis_index("ref_0") * sizes[1] + lax.axis_index("ref_1")
    return chip, lax.axis_index("ref_2")


def turn_of(sizes, piece):
    chip, core = place_of(sizes)
    return ((2 * chip + core) * piece) & (LANES - 1)


def inside_text(row, t, positions):
    return (row >= t * positions) & (row < (t + 1) * positions)


def turn_kernel(sizes):
    def kernel(public, near, out, number, scratch):
        texts, positions, piece = public.shape
        square = number.shape
        lane = lanes_of(square)
        row = lax.broadcasted_iota(jnp.int32, square, 0)
        shift = turn_of(sizes, piece)
        for k, tile in enumerate(turned(rows_of(public, scratch), shift, lane)):
            out[:, k * LANES : (k + 1) * LANES] = tile
        many = jnp.zeros(square, jnp.float32)
        for t in range(texts):
            held = jnp.int32(0)
            for r in range(near.shape[0]):
                held += jnp.where(near[r] == t, 1, 0)
            many = jnp.where(inside_text(row, t, positions), held.astype(jnp.float32), many)
        number[...] = many

    return kernel


def mark_kernel(sizes, piece, positions):
    def kernel(one, number, far, out):
        square = number.shape
        row = lax.broadcasted_iota(jnp.int32, square, 0)
        lane = lanes_of(square)
        shift = turn_of(sizes, piece)
        many = number[...]
        for t in range(square[0] // positions):
            held = jnp.sum(jnp.where(far[...] == t, 1.0, 0.0), axis=1, keepdims=True)
            held = jnp.broadcast_to(held, square)
            many = many + jnp.where(inside_text(row, t, positions), held, 0.0)
        for k in range(TILES):
            tile = one[:, k * LANES : (k + 1) * LANES]
            tile = jnp.where(column_of(lane, k, shift) < piece, tile, many)
            tile = tile.astype(out.dtype)
            for j in range(out.shape[0]):
                out[j, :, k * LANES : (k + 1) * LANES] = tile

    return kernel


class Rows:
    def __init__(self, plan, priv, swapped, packed=False):
        rows, self.positions, self.columns = swapped.shape
        self.entries = []
        for h, held in enumerate((priv, swapped)):
            for r in range(rows):
                at = h * rows + r
                self.entries.append((held, r, plan[at], plan[2 * rows + at], packed and h == 0))


def begins(j, core, piece):
    start = (2 * j + core) * piece
    base = start // LANES * LANES
    return pl.multiple_of(base, LANES), start - base


def widen_into(pub, place, value, positions):
    for t in range(pub.shape[0]):
        part = value[t * positions : (t + 1) * positions]
        pub[t, :, pl.ds(pl.multiple_of(place * WINDOW, LANES), WIDE)] = part
        pub[t, :, pl.ds(pl.multiple_of(place * WINDOW + WIDE, LANES), LANES)] = part[:, :LANES]


def fill_strip(rows, strip, entries):
    last = rows.columns // LANES * LANES
    for e in entries:
        held, r, _, _, packed = rows.entries[e]
        if packed:
            continue
        strip[e] = jnp.zeros(strip.shape[1:], strip.dtype)
        strip[e, :, : rows.columns - last] = held[r, :, last:]


def sum_windows(rows, pub, acc, core, piece, scale, windows, strip=None):
    clear(rows, acc, 0, len(windows))
    add_rows(rows, pub, acc, core, piece, windows, range(len(rows.entries)), 0, strip)
    store_sums(rows, acc, core, piece, scale, windows, 0)


def clear(rows, acc, first, many):
    texts = acc.shape[0] - 1
    acc[:texts, :, first * WINDOW : (first + many) * WINDOW] = jnp.zeros(
        (texts, rows.positions, many * WINDOW), jnp.float32
    )


def add_rows(rows, pub, acc, core, piece, windows, entries, first, strip=None):
    whole = rows.columns // LANES * LANES
    bases = [begins(window[0], core, piece)[0] for window in windows]
    at = [pl.multiple_of(window[1] * WINDOW, LANES) for window in windows]
    packs = [pl.multiple_of(window[3] * WINDOW, LANES) for window in windows]
    if strip is not None:
        fill_strip(rows, strip, entries)
        ends = [base + WINDOW > rows.columns for base in bases]
        edges = [pl.multiple_of(jnp.minimum(base + WIDE, whole - LANES), LANES) for base in bases]
    for e in entries:
        held, r, text, slot, packed = rows.entries[e]
        for g in range(len(windows)):
            size = WINDOW if strip is None or packed else WIDE
            parts = [(0, held[r, :, pl.ds(packs[g] if packed else bases[g], size)])]
            if size == WIDE:
                parts.append((WIDE, jnp.where(ends[g], strip[e], held[r, :, pl.ds(edges[g], LANES)])))
            for offset, value in parts:
                width = value.shape[1]
                beside = pub[text, :, pl.ds(pl.multiple_of(at[g] + offset, LANES), width)]
                value = jnp.clip(value.astype(jnp.float32) - beside, -clip_bound, clip_bound)
                start = (first + g) * WINDOW + offset
                acc[slot, :, start : start + width] = acc[slot, :, start : start + width] + value


def store_sums(rows, acc, core, piece, scale, windows, first):
    texts = acc.shape[0] - 1
    lane = lanes_of((texts * rows.positions, LANES))
    for g, (j, _, store, _) in enumerate(windows):
        shift = begins(j, core, piece)[1]
        tiles = [
            jnp.concatenate(
                [tile_at(acc, t, (first + g) * WINDOW + k * LANES) for t in range(texts)],
                axis=0,
            )
            for k in range(TILES + 1)
        ]
        tiles[0] = jnp.where(lane >= shift, tiles[0], tiles[TILES])
        for k in range(TILES):
            fixed = jnp.round(tiles[k] * scale).astype(jnp.int32).astype(jnp.int16)
            store(slice(k * LANES, (k + 1) * LANES), fixed)


def tile_at(acc, t, start):
    return acc[t, :, start : start + LANES]


def storing(out, index):
    def store(part, value):
        out[index, :, part] = value

    return store


def far_kernel(sizes, scale, piece):
    def kernel(
        owner_there, partner_there, counts_there, source, swapped, own,
        out, plan,
        priv, pub, acc, strip, tail, owner, partner, counts, left, arrived, small,
    ):
        rows, positions, columns = swapped.shape
        texts = pub.shape[0]
        chips, flat, _ = own.shape
        lines, beside = sizes
        chip, core = place_of(sizes)
        mine = lax.axis_index("ref_1")
        lane = lanes_of((flat, LANES))
        row = lax.broadcasted_iota(jnp.int32, (flat, LANES), 0)

        def piece_of(n, i):
            return beside * i + (mine ^ AROUND[n])

        def copy_of(n, i, width=WINDOW):
            start = begins(piece_of(n, i), core, piece)[0]
            place = n * lines + i
            return pltpu.make_async_copy(
                source.at[:, :, pl.ds(start, width)],
                priv.at[:, :, place * WINDOW : place * WINDOW + width],
                arrived.at[place],
            )

        whole = columns // LANES * LANES
        tail_copy = pltpu.make_async_copy(source.at[:, :, whole:], tail, small.at[3])

        def fill_tail(n):
            place = (n + 1) * lines - 1
            ends = begins(piece_of(n, lines - 1), core, piece)[0] + WINDOW > columns
            start = place * WINDOW + WIDE

            @pl.when(ends)
            def _():
                for r in range(rows):
                    priv[r, :, start : start + columns - whole] = tail[r]

        def each_copy(n, i, act):
            if i < lines - 1:
                act(copy_of(n, i))
                return
            ends = begins(piece_of(n, i), core, piece)[0] + WINDOW > columns

            @pl.when(ends)
            def _():
                act(copy_of(n, i, WIDE))

            @pl.when(jnp.logical_not(ends))
            def _():
                act(copy_of(n, i))

        pairs = ((owner_there, owner), (partner_there, partner), (counts_there, counts))
        little = [
            pltpu.make_async_copy(there, here, small.at[i]) for i, (there, here) in enumerate(pairs)
        ]
        for copy in little:
            copy.start()
        tail_copy.start()
        for i in range(lines):
            each_copy(0, i, lambda copy: copy.start())

        def widen(i, earlier):
            for n in range(beside):
                j = beside * i + (mine ^ AROUND[n])
                value = own[j].astype(jnp.float32)
                if n == 0:
                    widen_into(pub, i, value, positions)
                shift = begins(j, core, piece)[1]
                free = jnp.where(shift == 0, LANES - 1, shift - 1)
                tile = jnp.where(shift == 0, tile_of(value, TILES - 1), tile_of(value, 0))
                free = jnp.where(j < chip, free, LANES)
                earlier = earlier + jnp.where(lane == free, tile, 0.0)
            return earlier

        earlier = lax.fori_loop(0, lines, widen, jnp.zeros((flat, LANES), jnp.float32))
        for copy in little:
            copy.wait()
        for t in range(texts):
            here = jnp.where(row == t * positions, earlier, 0.0)
            left[t] = counts[t] - jnp.sum(here).astype(jnp.int32)

        for c in range(2):
            for r in range(rows):
                text = jnp.where(core == c, owner[r], partner[r])
                still = left[text]
                left[text] = still - 1
                at = jnp.where(core == c, r, rows + r)
                plan[at] = text
                plan[2 * rows + at] = jnp.where(still > 0, text, texts)
        acc[texts] = jnp.zeros(acc.shape[1:], jnp.float32)
        held = Rows(plan, priv, swapped, packed=True)
        windows = [(piece_of(0, i), i, storing(out, i), i) for i in range(lines)]
        clear(held, acc, 0, lines)

        def add(entries, first):
            batch = windows[first : first + GROUP]
            edge = strip if first + GROUP == lines else None
            add_rows(held, pub, acc, core, piece, batch, entries, first, edge)

        for first in range(0, lines, GROUP):
            add(range(rows, 2 * rows), first)
        for first in range(0, lines, GROUP):
            for i in range(first, first + GROUP):
                each_copy(0, i, lambda copy: copy.wait())
            if first == 0:
                tail_copy.wait()
            if first + GROUP == lines:
                fill_tail(0)
            add(range(rows), first)
            store_sums(held, acc, core, piece, scale, windows[first : first + GROUP], first)

    return kernel


def near_kernel(sizes, scale, piece):
    def kernel(plan, priv, swapped, own, out_1, out_2, pub, acc, strip):
        texts = pub.shape[0]
        lines, beside = sizes
        chip, core = place_of(sizes)
        mine = lax.axis_index("ref_1")
        held = Rows(plan, priv, swapped)
        acc[texts] = jnp.zeros(acc.shape[1:], jnp.float32)
        step = GROUP // 2

        def some(first, strip=None):
            windows = []
            for k in range(step):
                i = first + k
                for n, out in ((1, out_1), (2, out_2)):
                    j = beside * i + (mine ^ AROUND[n])
                    place = 2 * k + n - 1
                    widen_into(pub, place, own[j].astype(jnp.float32), held.positions)
                    windows.append((j, place, storing(out, i), 0))
            sum_windows(held, pub, acc, core, piece, scale, windows, strip)

        def looped(b, carry):
            some(b * step)
            return carry

        lax.fori_loop(0, lines // step - 1, looped, 0)
        some(lines - step, strip)

    return kernel


def own_kernel(sizes, scale, piece):
    def kernel(
        public, noise, counts, tokens, plan, priv, swapped, own,
        out, base, chosen, level, factor,
        pub, acc, strip, scratch,
    ):
        texts = pub.shape[0]
        lines, beside = sizes
        chip, core = place_of(sizes)
        mine = lax.axis_index("ref_1")
        held = Rows(plan, priv, swapped)
        for i in range(lines):
            widen_into(pub, i, own[beside * i + mine].astype(jnp.float32), held.positions)
        acc[texts] = jnp.zeros(acc.shape[1:], jnp.float32)
        for first in range(0, lines, GROUP):
            windows = [
                (beside * i + mine, i, storing(out, i), 0)
                for i in range(first, first + GROUP)
            ]
            last = first + GROUP == lines
            sum_windows(held, pub, acc, core, piece, scale, windows, strip if last else None)
        prepare(sizes, scale / beside, public, noise, counts, tokens, scratch, base, chosen, level, factor)

    return kernel


def join_kernel(a, b, c, d, out):
    for i in range(out.shape[0]):
        total = (a[i].astype(jnp.int32) + b[i].astype(jnp.int32)) + (
            c[i].astype(jnp.int32) + d[i].astype(jnp.int32)
        )
        total = jnp.round(total.astype(jnp.float32) * 0.25)
        out[i] = total.astype(jnp.int32).astype(jnp.int16)


def prepare(sizes, scale_of, public, noise, counts, tokens, scratch, base, chosen, level, factor):
    texts, positions, piece = public.shape
    square = (texts * positions, LANES)
    lane = lanes_of(square)
    row = lax.broadcasted_iota(jnp.int32, square, 0)
    shift = turn_of(sizes, piece)
    chip, core = place_of(sizes)
    chips = sizes[0] * sizes[1]
    first = (lax.axis_index("voc") * 2 * chips + 2 * chip + core) * piece
    number = jnp.ones(square, jnp.float32)
    token = jnp.zeros(square, jnp.int32)
    for t in range(texts):
        number = jnp.where(inside_text(row, t, positions), counts[t].astype(jnp.float32), number)
        for p in range(positions):
            token = jnp.where(row == t * positions + p, tokens[t, p] - first, token)
    factor[...] = (1.0 / scale_of) / (clip_bound * jnp.sqrt(number))
    public_tiles = turned(rows_of(public, scratch.at[0]), shift, lane)
    noise_tiles = turned(rows_of(noise, scratch.at[1]), shift, lane)
    top = jnp.full(square, -jnp.inf, jnp.float32)
    for k in range(TILES):
        column = column_of(lane, k, shift)
        inside = column < piece
        part = slice(k * LANES, (k + 1) * LANES)
        top = jnp.maximum(top, jnp.where(inside, public_tiles[k], -jnp.inf))
        base[:, part] = jnp.where(inside, public_tiles[k] + noise_tiles[k], -jnp.inf)
        chosen[:, part] = jnp.where(inside & (column == token), 1.0, 0.0)
    level[...] = jnp.broadcast_to(jnp.max(top, axis=1, keepdims=True), square)


def finish_kernel(parts, base, chosen, level, scale, combined, stats):
    flat = base.shape[0]
    square = (flat, LANES)
    lane = lanes_of(square)
    row = lax.broadcasted_iota(jnp.int32, square, 0)
    terms = jnp.zeros(square, jnp.float32)
    picked = jnp.zeros(square, jnp.float32)
    for k in range(TILES):
        part = slice(k * LANES, (k + 1) * LANES)
        total = parts[0, :, part].astype(jnp.int32)
        for j in range(1, parts.shape[0]):
            total = total + parts[j, :, part].astype(jnp.int32)
        tile = base[:, part] + total.astype(jnp.float32) * scale[...]
        combined[:, part] = tile
        terms = terms + jnp.exp(tile - level[...])
        picked = picked + jnp.where(chosen[:, part] > 0.0, tile, 0.0)
    terms = jnp.sum(terms, axis=1, keepdims=True)
    picked = jnp.sum(picked, axis=1, keepdims=True)
    spread = jnp.where(lane == row, terms, 0.0)
    spread = spread + jnp.where(lane == row + flat, picked, 0.0)
    spread = spread + jnp.where(lane == row + 2 * flat, level[...], 0.0)
    stats[...] = jnp.sum(spread, axis=0, keepdims=True)


def last_kernel(sizes):
    def kernel(everyone, combined, logprobs, target, natural):
        texts, positions, piece = logprobs.shape
        flat = texts * positions
        values = everyone[...]
        lane = lanes_of((1, LANES))
        level = jnp.max(values, axis=0, keepdims=True)
        weight = pltpu.roll(jnp.exp(values - level), LANES - 2 * flat, 1)
        total = jnp.sum(values * weight, axis=0, keepdims=True)
        picked = pltpu.roll(jnp.sum(values, axis=0, keepdims=True), LANES - flat, 1)
        level = pltpu.roll(level, LANES - 2 * flat, 1)
        own = lane < flat
        lse = jnp.where(own, level + jnp.log(jnp.where(own, total, 1.0)), 0.0)
        picked = picked - lse
        square = (flat, LANES)
        mine = lanes_of(square) == lax.broadcasted_iota(jnp.int32, square, 0)
        column = jnp.sum(jnp.where(mine, jnp.broadcast_to(lse, square), 0.0), axis=1, keepdims=True)
        tiles = [combined[:, k * LANES : (k + 1) * LANES] - column for k in range(TILES)]
        for k, tile in enumerate(turned_back(tiles, turn_of(sizes, piece), lanes_of(square))):
            natural[:, k * LANES : (k + 1) * LANES] = tile
        shifted = natural[:, :piece]
        for t in range(texts):
            logprobs[t] = shifted[t * positions : (t + 1) * positions]
        for t in range(texts):
            turn = picked if t == 0 else pltpu.roll(picked, LANES - t * positions, 1)
            target[t : t + 1, :] = turn[:, :positions]

    return kernel


def body(private_logits, public_logits, noise, owner, counts, tokens):
    texts, positions, piece = public_logits.shape
    rows, _, columns = private_logits.shape
    flat = texts * positions
    sizes = (lax.axis_size("ref_0"), lax.axis_size("ref_1"))
    chips = sizes[0] * sizes[1]
    swap = [(0, 1), (1, 0)]
    scale = float(32767 // (2 * rows * int(clip_bound)))
    square = pltpu.VMEM((flat, LANES), jnp.float32)
    long = pltpu.VMEM((flat, WIDE), jnp.float32)
    owner_there, counts_there, tokens_there, public_there, noise_there, private_there = (
        pltpu.with_memory_space_constraint(x, pltpu.HBM)
        for x in (owner, counts, tokens, public_logits, noise, private_logits)
    )

    partner = lax.ppermute(owner, CORE, swap)
    one, number = pl.pallas_call(
        turn_kernel(sizes),
        out_shape=(long, square),
        in_specs=[VMEM, SMEM],
        out_specs=(VMEM, VMEM),
        scratch_shapes=[pltpu.VMEM((flat, WIDE), jnp.float32)],
        compiler_params=PARAMS,
        name="turn",
    )(public_there, owner_there)
    partner, private_later, one = lax.optimization_barrier((partner, private_logits, one))
    swapped = lax.ppermute(private_later, CORE, swap)
    packed = pl.pallas_call(
        mark_kernel(sizes, piece, positions),
        out_shape=pltpu.VMEM((chips, flat, WIDE), jnp.bfloat16),
        in_specs=[VMEM, VMEM, VMEM],
        out_specs=VMEM,
        compiler_params=PARAMS,
        name="mark",
    )(one, number, partner.reshape(1, rows))
    own = lax.all_to_all(packed, CHIP, split_axis=0, concat_axis=0, tiled=True)
    swapped, own, partner = (
        pltpu.with_memory_space_constraint(x, pltpu.VMEM) for x in (swapped, own, partner)
    )
    lines, beside = sizes
    line_sums = pltpu.VMEM((lines, flat, WIDE), jnp.int16)
    windows = lines * WINDOW
    sums_scratch = pltpu.VMEM((texts + 1, positions, GROUP * WINDOW), jnp.float32)
    strip = pltpu.VMEM((2 * rows, positions, LANES), private_logits.dtype)

    def beyond(x, m):
        return lax.ppermute(x, "ref_1", [(k, k ^ m) for k in range(beside)])

    private_here = pltpu.with_memory_space_constraint(private_logits, pltpu.VMEM)
    far, plan = pl.pallas_call(
        far_kernel(sizes, scale, piece),
        out_shape=(
            line_sums,
            jax.ShapeDtypeStruct((4 * rows,), jnp.int32),
        ),
        in_specs=[HBM, VMEM, HBM, HBM, VMEM, VMEM],
        out_specs=(VMEM, SMEM),
        scratch_shapes=[
            pltpu.VMEM((rows, positions, windows), private_logits.dtype),
            pltpu.VMEM((texts, positions, windows), jnp.float32),
            pltpu.VMEM((texts + 1, positions, windows), jnp.float32),
            strip,
            pltpu.VMEM((rows, positions, columns % LANES), private_logits.dtype),
            pltpu.SMEM((rows,), jnp.int32),
            pltpu.SMEM((rows,), jnp.int32),
            pltpu.SMEM((texts,), jnp.int32),
            pltpu.SMEM((texts,), jnp.int32),
            pltpu.SemaphoreType.DMA((lines,)),
            pltpu.SemaphoreType.DMA((4,)),
        ],
        compiler_params=PARAMS,
        name="far_sums",
    )(owner_there, partner, counts_there, private_there, swapped, own)
    got = [beyond(far, AROUND[0])]
    near = pl.pallas_call(
        near_kernel(sizes, scale, piece),
        out_shape=(line_sums, line_sums),
        in_specs=[SMEM, VMEM, VMEM, VMEM],
        out_specs=(VMEM, VMEM),
        scratch_shapes=[
            pltpu.VMEM((texts, positions, GROUP * WINDOW), jnp.float32),
            sums_scratch,
            strip,
        ],
        compiler_params=PARAMS,
        name="near_sums",
    )(plan, private_here, swapped, own)
    got += [beyond(x, m) for x, m in zip(near, AROUND[1:])]
    near_done, own_later = lax.optimization_barrier((near[0], own))
    line, base, chosen, level, factor = pl.pallas_call(
        own_kernel(sizes, scale, piece),
        out_shape=(line_sums, long, long, square, square),
        in_specs=[VMEM, VMEM, SMEM, SMEM, SMEM, VMEM, VMEM, VMEM],
        out_specs=(VMEM,) * 5,
        scratch_shapes=[
            pltpu.VMEM((texts, positions, windows), jnp.float32),
            sums_scratch,
            strip,
            pltpu.VMEM((2, flat, WIDE), jnp.float32),
        ],
        compiler_params=PARAMS,
        name="own_sums",
    )(public_there, noise_there, counts_there, tokens_there, plan, private_here, swapped, own_later)
    joined = pl.pallas_call(
        join_kernel,
        out_shape=line_sums,
        in_specs=[VMEM] * 4,
        out_specs=VMEM,
        compiler_params=PARAMS,
        name="join",
    )(line, *[pltpu.with_memory_space_constraint(x, pltpu.VMEM) for x in got])
    parts = lax.all_to_all(joined, "ref_0", split_axis=0, concat_axis=0, tiled=True)
    parts = pltpu.with_memory_space_constraint(parts, pltpu.VMEM)
    combined, stats = pl.pallas_call(
        finish_kernel,
        out_shape=(long, pltpu.VMEM((1, LANES), jnp.float32)),
        in_specs=[VMEM] * 5,
        out_specs=(VMEM, VMEM),
        compiler_params=PARAMS,
        name="finish",
    )(parts, base, chosen, level, factor)

    devices = lax.axis_size(REF_VOC)
    everyone = lax.all_to_all(
        jnp.broadcast_to(stats, (devices, 1, LANES)), REF_VOC, split_axis=0, concat_axis=0, tiled=True
    ).reshape(devices, LANES)
    return pl.pallas_call(
        last_kernel(sizes),
        out_shape=(
            jax.ShapeDtypeStruct(public_logits.shape, jnp.float32),
            jax.ShapeDtypeStruct((texts, positions), jnp.float32),
        ),
        in_specs=[VMEM, VMEM],
        out_specs=(VMEM, VMEM),
        scratch_shapes=[pltpu.VMEM((flat, WIDE), jnp.float32)],
        compiler_params=PARAMS,
        name="last",
    )(pltpu.with_memory_space_constraint(everyone, pltpu.VMEM), combined)


def solution(mesh):
    finer = Mesh(
        mesh.devices.reshape(8, 4, 2, mesh.shape["voc"]), ("ref_0", "ref_1", "ref_2", "voc")
    )
    placed = (P(REF, None, "voc"), P(None, None, VOC_REF), P(None, None, VOC_REF), P(REF), P(), P())
    return jax.shard_map(
        body, mesh=finer, in_specs=placed, out_specs=(P(None, None, VOC_REF), P()), check_vma=False
    )
```

```python
import jax
import jax.numpy as jnp
from jax import lax
from jax.experimental import pallas as pl
from jax.experimental.pallas import tpu as pltpu
from jax.sharding import Mesh
from jax.sharding import PartitionSpec as P

REF_VOC = ("ref_0", "ref_1", "ref_2", "voc")
REF = ("ref_0", "ref_1", "ref_2")
CHIP = ("ref_0", "ref_1")
CORE = "ref_2"
VOC_REF = ("voc", "ref_0", "ref_1", "ref_2")

clip_bound = 2.0

LANES = 128
WIDE = 512
TILES = WIDE // LANES
WINDOW = WIDE + LANES
GROUP = 4
AROUND = (2, 1, 3, 0)

PARAMS = pltpu.CompilerParams(vmem_limit_bytes=16 << 20)
SMEM = pl.BlockSpec(memory_space=pltpu.SMEM)
VMEM = pl.BlockSpec(memory_space=pltpu.VMEM)
HBM = pl.BlockSpec(memory_space=pltpu.HBM)


def tile_of(x, k):
    return x[:, k * LANES : (k + 1) * LANES]


def turned(tiles, shift, lane):
    spun = [pltpu.roll(tile, shift, 1) for tile in tiles]
    return [jnp.where(lane >= shift, spun[k], spun[k - 1]) for k in range(TILES)]


def turned_back(tiles, shift, lane):
    back = LANES - shift
    spun = [pltpu.roll(tile, back, 1) for tile in tiles]
    return [jnp.where(lane < back, spun[k], spun[(k + 1) % TILES]) for k in range(TILES)]


def lanes_of(shape):
    return lax.broadcasted_iota(jnp.int32, shape, len(shape) - 1)


def rows_of(array, scratch):
    texts, positions, piece = array.shape
    for t in range(texts):
        part = slice(t * positions, (t + 1) * positions)
        scratch[part, :piece] = array[t].astype(jnp.float32)
    values = scratch[...]
    lane = lanes_of((texts * positions, LANES))
    return [
        jnp.where(lane + k * LANES < piece, tile_of(values, k), 0.0) for k in range(TILES)
    ]


def column_of(lane, k, shift):
    return (lane + k * LANES - shift) & (WIDE - 1)


def place_of(sizes):
    chip = lax.axis_index("ref_0") * sizes[1] + lax.axis_index("ref_1")
    return chip, lax.axis_index("ref_2")


def turn_of(sizes, piece):
    chip, core = place_of(sizes)
    return ((2 * chip + core) * piece) & (LANES - 1)


def inside_text(row, t, positions):
    return (row >= t * positions) & (row < (t + 1) * positions)


def turn_kernel(sizes):
    def kernel(public, near, out, number, scratch):
        texts, positions, piece = public.shape
        square = number.shape
        lane = lanes_of(square)
        row = lax.broadcasted_iota(jnp.int32, square, 0)
        shift = turn_of(sizes, piece)
        for k, tile in enumerate(turned(rows_of(public, scratch), shift, lane)):
            out[:, k * LANES : (k + 1) * LANES] = tile
        many = jnp.zeros(square, jnp.float32)
        for t in range(texts):
            held = jnp.int32(0)
            for r in range(near.shape[0]):
                held += jnp.where(near[r] == t, 1, 0)
            many = jnp.where(inside_text(row, t, positions), held.astype(jnp.float32), many)
        number[...] = many

    return kernel


def mark_kernel(sizes, piece, positions):
    def kernel(one, number, far, out):
        square = number.shape
        row = lax.broadcasted_iota(jnp.int32, square, 0)
        lane = lanes_of(square)
        shift = turn_of(sizes, piece)
        many = number[...]
        for t in range(square[0] // positions):
            held = jnp.sum(jnp.where(far[...] == t, 1.0, 0.0), axis=1, keepdims=True)
            held = jnp.broadcast_to(held, square)
            many = many + jnp.where(inside_text(row, t, positions), held, 0.0)
        for k in range(TILES):
            tile = one[:, k * LANES : (k + 1) * LANES]
            tile = jnp.where(column_of(lane, k, shift) < piece, tile, many)
            tile = tile.astype(out.dtype)
            for j in range(out.shape[0]):
                out[j, :, k * LANES : (k + 1) * LANES] = tile

    return kernel


class Rows:
    def __init__(self, plan, priv, swapped, packed=False):
        rows, self.positions, self.columns = swapped.shape
        self.entries = []
        for h, held in enumerate((priv, swapped)):
            for r in range(rows):
                at = h * rows + r
                self.entries.append((held, r, plan[at], plan[2 * rows + at], packed and h == 0))


def begins(j, core, piece):
    start = (2 * j + core) * piece
    base = start // LANES * LANES
    return pl.multiple_of(base, LANES), start - base


def widen_into(pub, place, value, positions):
    for t in range(pub.shape[0]):
        part = value[t * positions : (t + 1) * positions]
        pub[t, :, pl.ds(pl.multiple_of(place * WINDOW, LANES), WIDE)] = part
        pub[t, :, pl.ds(pl.multiple_of(place * WINDOW + WIDE, LANES), LANES)] = part[:, :LANES]


def fill_strip(rows, strip, entries):
    last = rows.columns // LANES * LANES
    for e in entries:
        held, r, _, _, packed = rows.entries[e]
        if packed:
            continue
        strip[e] = jnp.zeros(strip.shape[1:], strip.dtype)
        strip[e, :, : rows.columns - last] = held[r, :, last:]


def sum_windows(rows, pub, acc, core, piece, scale, windows, strip=None):
    clear(rows, acc, 0, len(windows))
    add_rows(rows, pub, acc, core, piece, windows, range(len(rows.entries)), 0, strip)
    store_sums(rows, acc, core, piece, scale, windows, 0)


def clear(rows, acc, first, many):
    texts = acc.shape[0] - 1
    acc[:texts, :, first * WINDOW : (first + many) * WINDOW] = jnp.zeros(
        (texts, rows.positions, many * WINDOW), jnp.float32
    )


def add_rows(rows, pub, acc, core, piece, windows, entries, first, strip=None):
    whole = rows.columns // LANES * LANES
    bases = [begins(window[0], core, piece)[0] for window in windows]
    at = [pl.multiple_of(window[1] * WINDOW, LANES) for window in windows]
    packs = [pl.multiple_of(window[3] * WINDOW, LANES) for window in windows]
    if strip is not None:
        fill_strip(rows, strip, entries)
        ends = [base + WINDOW > rows.columns for base in bases]
        edges = [pl.multiple_of(jnp.minimum(base + WIDE, whole - LANES), LANES) for base in bases]
    for e in entries:
        held, r, text, slot, packed = rows.entries[e]
        for g in range(len(windows)):
            size = WINDOW if strip is None or packed else WIDE
            parts = [(0, held[r, :, pl.ds(packs[g] if packed else bases[g], size)])]
            if size == WIDE:
                parts.append((WIDE, jnp.where(ends[g], strip[e], held[r, :, pl.ds(edges[g], LANES)])))
            for offset, value in parts:
                width = value.shape[1]
                beside = pub[text, :, pl.ds(pl.multiple_of(at[g] + offset, LANES), width)]
                value = jnp.clip(value.astype(jnp.float32) - beside, -clip_bound, clip_bound)
                start = (first + g) * WINDOW + offset
                acc[slot, :, start : start + width] = acc[slot, :, start : start + width] + value


def store_sums(rows, acc, core, piece, scale, windows, first):
    texts = acc.shape[0] - 1
    lane = lanes_of((texts * rows.positions, LANES))
    for g, (j, _, store, _) in enumerate(windows):
        shift = begins(j, core, piece)[1]
        tiles = [
            jnp.concatenate(
                [tile_at(acc, t, (first + g) * WINDOW + k * LANES) for t in range(texts)],
                axis=0,
            )
            for k in range(TILES + 1)
        ]
        tiles[0] = jnp.where(lane >= shift, tiles[0], tiles[TILES])
        for k in range(TILES):
            fixed = jnp.round(tiles[k] * scale).astype(jnp.int32).astype(jnp.int16)
            store(slice(k * LANES, (k + 1) * LANES), fixed)


def tile_at(acc, t, start):
    return acc[t, :, start : start + LANES]


def storing(out, index):
    def store(part, value):
        out[index, :, part] = value

    return store


def far_kernel(sizes, scale, piece):
    def kernel(
        owner_there, partner_there, counts_there, source, swapped, own,
        out, plan,
        priv, pub, acc, strip, tail, owner, partner, counts, left, arrived, small,
    ):
        rows, positions, columns = swapped.shape
        texts = pub.shape[0]
        chips, flat, _ = own.shape
        lines, beside = sizes
        chip, core = place_of(sizes)
        mine = lax.axis_index("ref_1")
        lane = lanes_of((flat, LANES))
        row = lax.broadcasted_iota(jnp.int32, (flat, LANES), 0)

        def piece_of(n, i):
            return beside * i + (mine ^ AROUND[n])

        def copy_of(n, i, width=WINDOW):
            start = begins(piece_of(n, i), core, piece)[0]
            place = n * lines + i
            return pltpu.make_async_copy(
                source.at[:, :, pl.ds(start, width)],
                priv.at[:, :, place * WINDOW : place * WINDOW + width],
                arrived.at[place],
            )

        whole = columns // LANES * LANES
        tail_copy = pltpu.make_async_copy(source.at[:, :, whole:], tail, small.at[3])

        def fill_tail(n):
            place = (n + 1) * lines - 1
            ends = begins(piece_of(n, lines - 1), core, piece)[0] + WINDOW > columns
            start = place * WINDOW + WIDE

            @pl.when(ends)
            def _():
                for r in range(rows):
                    priv[r, :, start : start + columns - whole] = tail[r]

        def each_copy(n, i, act):
            if i < lines - 1:
                act(copy_of(n, i))
                return
            ends = begins(piece_of(n, i), core, piece)[0] + WINDOW > columns

            @pl.when(ends)
            def _():
                act(copy_of(n, i, WIDE))

            @pl.when(jnp.logical_not(ends))
            def _():
                act(copy_of(n, i))

        pairs = ((owner_there, owner), (partner_there, partner), (counts_there, counts))
        little = [
            pltpu.make_async_copy(there, here, small.at[i]) for i, (there, here) in enumerate(pairs)
        ]
        for copy in little:
            copy.start()
        tail_copy.start()
        for i in range(lines):
            each_copy(0, i, lambda copy: copy.start())

        def widen(i, earlier):
            for n in range(beside):
                j = beside * i + (mine ^ AROUND[n])
                value = own[j].astype(jnp.float32)
                if n == 0:
                    widen_into(pub, i, value, positions)
                shift = begins(j, core, piece)[1]
                free = jnp.where(shift == 0, LANES - 1, shift - 1)
                tile = jnp.where(shift == 0, tile_of(value, TILES - 1), tile_of(value, 0))
                free = jnp.where(j < chip, free, LANES)
                earlier = earlier + jnp.where(lane == free, tile, 0.0)
            return earlier

        earlier = lax.fori_loop(0, lines, widen, jnp.zeros((flat, LANES), jnp.float32))
        for copy in little:
            copy.wait()
        for t in range(texts):
            here = jnp.where(row == t * positions, earlier, 0.0)
            left[t] = counts[t] - jnp.sum(here).astype(jnp.int32)

        for c in range(2):
            for r in range(rows):
                text = jnp.where(core == c, owner[r], partner[r])
                still = left[text]
                left[text] = still - 1
                at = jnp.where(core == c, r, rows + r)
                plan[at] = text
                plan[2 * rows + at] = jnp.where(still > 0, text, texts)
        acc[texts] = jnp.zeros(acc.shape[1:], jnp.float32)
        held = Rows(plan, priv, swapped, packed=True)
        windows = [(piece_of(0, i), i, storing(out, i), i) for i in range(lines)]
        clear(held, acc, 0, lines)

        def add(entries, first):
            batch = windows[first : first + GROUP]
            edge = strip if first + GROUP == lines else None
            add_rows(held, pub, acc, core, piece, batch, entries, first, edge)

        for first in range(0, lines, GROUP):
            add(range(rows, 2 * rows), first)
        for first in range(0, lines, GROUP):
            for i in range(first, first + GROUP):
                each_copy(0, i, lambda copy: copy.wait())
            if first == 0:
                tail_copy.wait()
            if first + GROUP == lines:
                fill_tail(0)
            add(range(rows), first)
            store_sums(held, acc, core, piece, scale, windows[first : first + GROUP], first)

    return kernel


def near_kernel(sizes, scale, piece):
    def kernel(plan, priv, swapped, own, out_1, out_2, pub, acc, strip):
        texts = pub.shape[0]
        lines, beside = sizes
        chip, core = place_of(sizes)
        mine = lax.axis_index("ref_1")
        held = Rows(plan, priv, swapped)
        acc[texts] = jnp.zeros(acc.shape[1:], jnp.float32)
        step = GROUP // 2

        def some(first, strip=None):
            windows = []
            for k in range(step):
                i = first + k
                for n, out in ((1, out_1), (2, out_2)):
                    j = beside * i + (mine ^ AROUND[n])
                    place = 2 * k + n - 1
                    widen_into(pub, place, own[j].astype(jnp.float32), held.positions)
                    windows.append((j, place, storing(out, i), 0))
            sum_windows(held, pub, acc, core, piece, scale, windows, strip)

        def looped(b, carry):
            some(b * step)
            return carry

        lax.fori_loop(0, lines // step - 1, looped, 0)
        some(lines - step, strip)

    return kernel


def own_kernel(sizes, scale, piece):
    def kernel(
        public, noise, counts, tokens, plan, priv, swapped, own,
        out, base, chosen, level, factor,
        pub, acc, strip, scratch,
    ):
        texts = pub.shape[0]
        lines, beside = sizes
        chip, core = place_of(sizes)
        mine = lax.axis_index("ref_1")
        held = Rows(plan, priv, swapped)
        for i in range(lines):
            widen_into(pub, i, own[beside * i + mine].astype(jnp.float32), held.positions)
        acc[texts] = jnp.zeros(acc.shape[1:], jnp.float32)
        for first in range(0, lines, GROUP):
            windows = [
                (beside * i + mine, i, storing(out, i), 0)
                for i in range(first, first + GROUP)
            ]
            last = first + GROUP == lines
            sum_windows(held, pub, acc, core, piece, scale, windows, strip if last else None)
        prepare(sizes, scale / beside, public, noise, counts, tokens, scratch, base, chosen, level, factor)

    return kernel


def join_kernel(a, b, c, d, out):
    for i in range(out.shape[0]):
        total = (a[i].astype(jnp.int32) + b[i].astype(jnp.int32)) + (
            c[i].astype(jnp.int32) + d[i].astype(jnp.int32)
        )
        total = jnp.round(total.astype(jnp.float32) * 0.25)
        out[i] = total.astype(jnp.int32).astype(jnp.int16)


def prepare(sizes, scale_of, public, noise, counts, tokens, scratch, base, chosen, level, factor):
    texts, positions, piece = public.shape
    square = (texts * positions, LANES)
    lane = lanes_of(square)
    row = lax.broadcasted_iota(jnp.int32, square, 0)
    shift = turn_of(sizes, piece)
    chip, core = place_of(sizes)
    chips = sizes[0] * sizes[1]
    first = (lax.axis_index("voc") * 2 * chips + 2 * chip + core) * piece
    number = jnp.ones(square, jnp.float32)
    token = jnp.zeros(square, jnp.int32)
    for t in range(texts):
        number = jnp.where(inside_text(row, t, positions), counts[t].astype(jnp.float32), number)
        for p in range(positions):
            token = jnp.where(row == t * positions + p, tokens[t, p] - first, token)
    factor[...] = (1.0 / scale_of) / (clip_bound * jnp.sqrt(number))
    public_tiles = turned(rows_of(public, scratch.at[0]), shift, lane)
    noise_tiles = turned(rows_of(noise, scratch.at[1]), shift, lane)
    top = jnp.full(square, -jnp.inf, jnp.float32)
    for k in range(TILES):
        column = column_of(lane, k, shift)
        inside = column < piece
        part = slice(k * LANES, (k + 1) * LANES)
        top = jnp.maximum(top, jnp.where(inside, public_tiles[k], -jnp.inf))
        base[:, part] = jnp.where(inside, public_tiles[k] + noise_tiles[k], -jnp.inf)
        chosen[:, part] = jnp.where(inside & (column == token), 1.0, 0.0)
    level[...] = jnp.broadcast_to(jnp.max(top, axis=1, keepdims=True), square)


def finish_kernel(parts, base, chosen, level, scale, combined, stats):
    flat = base.shape[0]
    square = (flat, LANES)
    lane = lanes_of(square)
    row = lax.broadcasted_iota(jnp.int32, square, 0)
    terms = jnp.zeros(square, jnp.float32)
    picked = jnp.zeros(square, jnp.float32)
    for k in range(TILES):
        part = slice(k * LANES, (k + 1) * LANES)
        total = parts[0, :, part].astype(jnp.int32)
        for j in range(1, parts.shape[0]):
            total = total + parts[j, :, part].astype(jnp.int32)
        tile = base[:, part] + total.astype(jnp.float32) * scale[...]
        combined[:, part] = tile
        terms = terms + jnp.exp(tile - level[...])
        picked = picked + jnp.where(chosen[:, part] > 0.0, tile, 0.0)
    terms = jnp.sum(terms, axis=1, keepdims=True)
    picked = jnp.sum(picked, axis=1, keepdims=True)
    spread = jnp.where(lane == row, terms, 0.0)
    spread = spread + jnp.where(lane == row + flat, picked, 0.0)
    spread = spread + jnp.where(lane == row + 2 * flat, level[...], 0.0)
    stats[...] = jnp.sum(spread, axis=0, keepdims=True)


def last_kernel(sizes):
    def kernel(everyone, combined, logprobs, target, natural):
        texts, positions, piece = logprobs.shape
        flat = texts * positions
        values = everyone[...]
        lane = lanes_of((1, LANES))
        level = jnp.max(values, axis=0, keepdims=True)
        weight = pltpu.roll(jnp.exp(values - level), LANES - 2 * flat, 1)
        total = jnp.sum(values * weight, axis=0, keepdims=True)
        picked = pltpu.roll(jnp.sum(values, axis=0, keepdims=True), LANES - flat, 1)
        level = pltpu.roll(level, LANES - 2 * flat, 1)
        own = lane < flat
        lse = jnp.where(own, level + jnp.log(jnp.where(own, total, 1.0)), 0.0)
        picked = picked - lse
        square = (flat, LANES)
        mine = lanes_of(square) == lax.broadcasted_iota(jnp.int32, square, 0)
        column = jnp.sum(jnp.where(mine, jnp.broadcast_to(lse, square), 0.0), axis=1, keepdims=True)
        tiles = [combined[:, k * LANES : (k + 1) * LANES] - column for k in range(TILES)]
        for k, tile in enumerate(turned_back(tiles, turn_of(sizes, piece), lanes_of(square))):
            natural[:, k * LANES : (k + 1) * LANES] = tile
        shifted = natural[:, :piece]
        for t in range(texts):
            logprobs[t] = shifted[t * positions : (t + 1) * positions]
        for t in range(texts):
            turn = picked if t == 0 else pltpu.roll(picked, LANES - t * positions, 1)
            target[t : t + 1, :] = turn[:, :positions]

    return kernel


def body(private_logits, public_logits, noise, owner, counts, tokens):
    texts, positions, piece = public_logits.shape
    rows, _, columns = private_logits.shape
    flat = texts * positions
    sizes = (lax.axis_size("ref_0"), lax.axis_size("ref_1"))
    chips = sizes[0] * sizes[1]
    swap = [(0, 1), (1, 0)]
    scale = float(32767 // (2 * rows * int(clip_bound)))
    square = pltpu.VMEM((flat, LANES), jnp.float32)
    long = pltpu.VMEM((flat, WIDE), jnp.float32)
    owner_there, counts_there, tokens_there, public_there, noise_there, private_there = (
        pltpu.with_memory_space_constraint(x, pltpu.HBM)
        for x in (owner, counts, tokens, public_logits, noise, private_logits)
    )

    partner = lax.ppermute(owner, CORE, swap)
    one, number = pl.pallas_call(
        turn_kernel(sizes),
        out_shape=(long, square),
        in_specs=[VMEM, SMEM],
        out_specs=(VMEM, VMEM),
        scratch_shapes=[pltpu.VMEM((flat, WIDE), jnp.float32)],
        compiler_params=PARAMS,
        name="turn",
    )(public_there, owner_there)
    partner, private_later, one = lax.optimization_barrier((partner, private_logits, one))
    swapped = lax.ppermute(private_later, CORE, swap)
    packed = pl.pallas_call(
        mark_kernel(sizes, piece, positions),
        out_shape=pltpu.VMEM((chips, flat, WIDE), jnp.bfloat16),
        in_specs=[VMEM, VMEM, VMEM],
        out_specs=VMEM,
        compiler_params=PARAMS,
        name="mark",
    )(one, number, partner.reshape(1, rows))
    own = lax.all_to_all(packed, CHIP, split_axis=0, concat_axis=0, tiled=True)
    swapped, own, partner = (
        pltpu.with_memory_space_constraint(x, pltpu.VMEM) for x in (swapped, own, partner)
    )
    lines, beside = sizes
    line_sums = pltpu.VMEM((lines, flat, WIDE), jnp.int16)
    windows = lines * WINDOW
    sums_scratch = pltpu.VMEM((texts + 1, positions, GROUP * WINDOW), jnp.float32)
    strip = pltpu.VMEM((2 * rows, positions, LANES), private_logits.dtype)

    def beyond(x, m):
        return lax.ppermute(x, "ref_1", [(k, k ^ m) for k in range(beside)])

    private_here = pltpu.with_memory_space_constraint(private_logits, pltpu.VMEM)
    far, plan = pl.pallas_call(
        far_kernel(sizes, scale, piece),
        out_shape=(
            line_sums,
            jax.ShapeDtypeStruct((4 * rows,), jnp.int32),
        ),
        in_specs=[HBM, VMEM, HBM, HBM, VMEM, VMEM],
        out_specs=(VMEM, SMEM),
        scratch_shapes=[
            pltpu.VMEM((rows, positions, windows), private_logits.dtype),
            pltpu.VMEM((texts, positions, windows), jnp.float32),
            pltpu.VMEM((texts + 1, positions, windows), jnp.float32),
            strip,
            pltpu.VMEM((rows, positions, columns % LANES), private_logits.dtype),
            pltpu.SMEM((rows,), jnp.int32),
            pltpu.SMEM((rows,), jnp.int32),
            pltpu.SMEM((texts,), jnp.int32),
            pltpu.SMEM((texts,), jnp.int32),
            pltpu.SemaphoreType.DMA((lines,)),
            pltpu.SemaphoreType.DMA((4,)),
        ],
        compiler_params=PARAMS,
        name="far_sums",
    )(owner_there, partner, counts_there, private_there, swapped, own)
    near = pl.pallas_call(
        near_kernel(sizes, scale, piece),
        out_shape=(line_sums, line_sums),
        in_specs=[SMEM, VMEM, VMEM, VMEM],
        out_specs=(VMEM, VMEM),
        scratch_shapes=[
            pltpu.VMEM((texts, positions, GROUP * WINDOW), jnp.float32),
            sums_scratch,
            strip,
        ],
        compiler_params=PARAMS,
        name="near_sums",
    )(plan, private_here, swapped, own)
    away = lax.optimization_barrier((far, *near))
    got = [beyond(x, m) for x, m in zip(away, AROUND)]
    near_done, own_later = lax.optimization_barrier((near[0], own))
    line, base, chosen, level, factor = pl.pallas_call(
        own_kernel(sizes, scale, piece),
        out_shape=(line_sums, long, long, square, square),
        in_specs=[VMEM, VMEM, SMEM, SMEM, SMEM, VMEM, VMEM, VMEM],
        out_specs=(VMEM,) * 5,
        scratch_shapes=[
            pltpu.VMEM((texts, positions, windows), jnp.float32),
            sums_scratch,
            strip,
            pltpu.VMEM((2, flat, WIDE), jnp.float32),
        ],
        compiler_params=PARAMS,
        name="own_sums",
    )(public_there, noise_there, counts_there, tokens_there, plan, private_here, swapped, own_later)
    joined = pl.pallas_call(
        join_kernel,
        out_shape=line_sums,
        in_specs=[VMEM] * 4,
        out_specs=VMEM,
        compiler_params=PARAMS,
        name="join",
    )(line, *[pltpu.with_memory_space_constraint(x, pltpu.VMEM) for x in got])
    parts = lax.all_to_all(joined, "ref_0", split_axis=0, concat_axis=0, tiled=True)
    parts = pltpu.with_memory_space_constraint(parts, pltpu.VMEM)
    combined, stats = pl.pallas_call(
        finish_kernel,
        out_shape=(long, pltpu.VMEM((1, LANES), jnp.float32)),
        in_specs=[VMEM] * 5,
        out_specs=(VMEM, VMEM),
        compiler_params=PARAMS,
        name="finish",
    )(parts, base, chosen, level, factor)

    devices = lax.axis_size(REF_VOC)
    everyone = lax.all_to_all(
        jnp.broadcast_to(stats, (devices, 1, LANES)), REF_VOC, split_axis=0, concat_axis=0, tiled=True
    ).reshape(devices, LANES)
    return pl.pallas_call(
        last_kernel(sizes),
        out_shape=(
            jax.ShapeDtypeStruct(public_logits.shape, jnp.float32),
            jax.ShapeDtypeStruct((texts, positions), jnp.float32),
        ),
        in_specs=[VMEM, VMEM],
        out_specs=(VMEM, VMEM),
        scratch_shapes=[pltpu.VMEM((flat, WIDE), jnp.float32)],
        compiler_params=PARAMS,
        name="last",
    )(pltpu.with_memory_space_constraint(everyone, pltpu.VMEM), combined)


def solution(mesh):
    finer = Mesh(
        mesh.devices.reshape(8, 4, 2, mesh.shape["voc"]), ("ref_0", "ref_1", "ref_2", "voc")
    )
    placed = (P(REF, None, "voc"), P(None, None, VOC_REF), P(None, None, VOC_REF), P(REF), P(), P())
    return jax.shard_map(
        body, mesh=finer, in_specs=placed, out_specs=(P(None, None, VOC_REF), P()), check_vma=False
    )
```

```python
import jax
import jax.numpy as jnp
from jax import lax
from jax.experimental import pallas as pl
from jax.experimental.pallas import tpu as pltpu
from jax.sharding import Mesh
from jax.sharding import PartitionSpec as P

REF_VOC = ("ref_0", "ref_1", "ref_2", "voc")
REF = ("ref_0", "ref_1", "ref_2")
CHIP = ("ref_0", "ref_1")
CORE = "ref_2"
VOC_REF = ("voc", "ref_0", "ref_1", "ref_2")

clip_bound = 2.0

LANES = 128
WIDE = 512
TILES = WIDE // LANES
WINDOW = WIDE + LANES
GROUP = 4
AROUND = (2, 1, 3, 0)

PARAMS = pltpu.CompilerParams(vmem_limit_bytes=16 << 20)
SMEM = pl.BlockSpec(memory_space=pltpu.SMEM)
VMEM = pl.BlockSpec(memory_space=pltpu.VMEM)
HBM = pl.BlockSpec(memory_space=pltpu.HBM)


def tile_of(x, k):
    return x[:, k * LANES : (k + 1) * LANES]


def turned(tiles, shift, lane):
    spun = [pltpu.roll(tile, shift, 1) for tile in tiles]
    return [jnp.where(lane >= shift, spun[k], spun[k - 1]) for k in range(TILES)]


def turned_back(tiles, shift, lane):
    back = LANES - shift
    spun = [pltpu.roll(tile, back, 1) for tile in tiles]
    return [jnp.where(lane < back, spun[k], spun[(k + 1) % TILES]) for k in range(TILES)]


def lanes_of(shape):
    return lax.broadcasted_iota(jnp.int32, shape, len(shape) - 1)


def rows_of(array, scratch):
    texts, positions, piece = array.shape
    for t in range(texts):
        part = slice(t * positions, (t + 1) * positions)
        scratch[part, :piece] = array[t].astype(jnp.float32)
    values = scratch[...]
    lane = lanes_of((texts * positions, LANES))
    return [
        jnp.where(lane + k * LANES < piece, tile_of(values, k), 0.0) for k in range(TILES)
    ]


def column_of(lane, k, shift):
    return (lane + k * LANES - shift) & (WIDE - 1)


def place_of(sizes):
    chip = lax.axis_index("ref_0") * sizes[1] + lax.axis_index("ref_1")
    return chip, lax.axis_index("ref_2")


def turn_of(sizes, piece):
    chip, core = place_of(sizes)
    return ((2 * chip + core) * piece) & (LANES - 1)


def inside_text(row, t, positions):
    return (row >= t * positions) & (row < (t + 1) * positions)


def turn_kernel(sizes):
    def kernel(public, near, out, number, scratch):
        texts, positions, piece = public.shape
        square = number.shape
        lane = lanes_of(square)
        row = lax.broadcasted_iota(jnp.int32, square, 0)
        shift = turn_of(sizes, piece)
        for k, tile in enumerate(turned(rows_of(public, scratch), shift, lane)):
            out[:, k * LANES : (k + 1) * LANES] = tile
        many = jnp.zeros(square, jnp.float32)
        for t in range(texts):
            held = jnp.int32(0)
            for r in range(near.shape[0]):
                held += jnp.where(near[r] == t, 1, 0)
            many = jnp.where(inside_text(row, t, positions), held.astype(jnp.float32), many)
        number[...] = many

    return kernel


def mark_kernel(sizes, piece, positions):
    def kernel(one, number, far, out):
        square = number.shape
        row = lax.broadcasted_iota(jnp.int32, square, 0)
        lane = lanes_of(square)
        shift = turn_of(sizes, piece)
        many = number[...]
        for t in range(square[0] // positions):
            held = jnp.sum(jnp.where(far[...] == t, 1.0, 0.0), axis=1, keepdims=True)
            held = jnp.broadcast_to(held, square)
            many = many + jnp.where(inside_text(row, t, positions), held, 0.0)
        for k in range(TILES):
            tile = one[:, k * LANES : (k + 1) * LANES]
            tile = jnp.where(column_of(lane, k, shift) < piece, tile, many)
            tile = tile.astype(out.dtype)
            for j in range(out.shape[0]):
                out[j, :, k * LANES : (k + 1) * LANES] = tile

    return kernel


class Rows:
    def __init__(self, plan, priv, swapped, packed=False):
        rows, self.positions, self.columns = swapped.shape
        self.entries = []
        for h, held in enumerate((priv, swapped)):
            for r in range(rows):
                at = h * rows + r
                self.entries.append((held, r, plan[at], plan[2 * rows + at], packed and h == 0))


def begins(j, core, piece):
    start = (2 * j + core) * piece
    base = start // LANES * LANES
    return pl.multiple_of(base, LANES), start - base


def widen_into(pub, place, value, positions):
    for t in range(pub.shape[0]):
        part = value[t * positions : (t + 1) * positions]
        pub[t, :, pl.ds(pl.multiple_of(place * WINDOW, LANES), WIDE)] = part
        pub[t, :, pl.ds(pl.multiple_of(place * WINDOW + WIDE, LANES), LANES)] = part[:, :LANES]


def fill_strip(rows, strip, entries):
    last = rows.columns // LANES * LANES
    for e in entries:
        held, r, _, _, packed = rows.entries[e]
        if packed:
            continue
        strip[e] = jnp.zeros(strip.shape[1:], strip.dtype)
        strip[e, :, : rows.columns - last] = held[r, :, last:]


def sum_windows(rows, pub, acc, core, piece, scale, windows, strip=None):
    clear(rows, acc, 0, len(windows))
    add_rows(rows, pub, acc, core, piece, windows, range(len(rows.entries)), 0, strip)
    store_sums(rows, acc, core, piece, scale, windows, 0)


def clear(rows, acc, first, many):
    texts = acc.shape[0] - 1
    acc[:texts, :, first * WINDOW : (first + many) * WINDOW] = jnp.zeros(
        (texts, rows.positions, many * WINDOW), jnp.float32
    )


def add_rows(rows, pub, acc, core, piece, windows, entries, first, strip=None):
    whole = rows.columns // LANES * LANES
    bases = [begins(window[0], core, piece)[0] for window in windows]
    at = [pl.multiple_of(window[1] * WINDOW, LANES) for window in windows]
    packs = [pl.multiple_of(window[3] * WINDOW, LANES) for window in windows]
    if strip is not None:
        fill_strip(rows, strip, entries)
        ends = [base + WINDOW > rows.columns for base in bases]
        edges = [pl.multiple_of(jnp.minimum(base + WIDE, whole - LANES), LANES) for base in bases]
    for e in entries:
        held, r, text, slot, packed = rows.entries[e]
        for g in range(len(windows)):
            size = WINDOW if strip is None or packed else WIDE
            parts = [(0, held[r, :, pl.ds(packs[g] if packed else bases[g], size)])]
            if size == WIDE:
                parts.append((WIDE, jnp.where(ends[g], strip[e], held[r, :, pl.ds(edges[g], LANES)])))
            for offset, value in parts:
                width = value.shape[1]
                beside = pub[text, :, pl.ds(pl.multiple_of(at[g] + offset, LANES), width)]
                value = jnp.clip(value.astype(jnp.float32) - beside, -clip_bound, clip_bound)
                start = (first + g) * WINDOW + offset
                acc[slot, :, start : start + width] = acc[slot, :, start : start + width] + value


def store_sums(rows, acc, core, piece, scale, windows, first):
    texts = acc.shape[0] - 1
    lane = lanes_of((texts * rows.positions, LANES))
    for g, (j, _, store, _) in enumerate(windows):
        shift = begins(j, core, piece)[1]
        tiles = [
            jnp.concatenate(
                [tile_at(acc, t, (first + g) * WINDOW + k * LANES) for t in range(texts)],
                axis=0,
            )
            for k in range(TILES + 1)
        ]
        tiles[0] = jnp.where(lane >= shift, tiles[0], tiles[TILES])
        for k in range(TILES):
            fixed = jnp.round(tiles[k] * scale).astype(jnp.int32).astype(jnp.int16)
            store(slice(k * LANES, (k + 1) * LANES), fixed)


def tile_at(acc, t, start):
    return acc[t, :, start : start + LANES]


def storing(out, index):
    def store(part, value):
        out[index, :, part] = value

    return store


def far_kernel(sizes, scale, piece):
    def kernel(
        owner_there, partner_there, counts_there, source, swapped, own,
        out, plan,
        priv, pub, acc, strip, tail, owner, partner, counts, left, arrived, small,
    ):
        rows, positions, columns = swapped.shape
        texts = pub.shape[0]
        chips, flat, _ = own.shape
        lines, beside = sizes
        chip, core = place_of(sizes)
        mine = lax.axis_index("ref_1")
        lane = lanes_of((flat, LANES))
        row = lax.broadcasted_iota(jnp.int32, (flat, LANES), 0)

        def piece_of(n, i):
            return beside * i + (mine ^ AROUND[n])

        def copy_of(n, i, width=WINDOW):
            start = begins(piece_of(n, i), core, piece)[0]
            place = n * lines + i
            return pltpu.make_async_copy(
                source.at[:, :, pl.ds(start, width)],
                priv.at[:, :, place * WINDOW : place * WINDOW + width],
                arrived.at[place],
            )

        whole = columns // LANES * LANES
        tail_copy = pltpu.make_async_copy(source.at[:, :, whole:], tail, small.at[3])

        def fill_tail(n):
            place = (n + 1) * lines - 1
            ends = begins(piece_of(n, lines - 1), core, piece)[0] + WINDOW > columns
            start = place * WINDOW + WIDE

            @pl.when(ends)
            def _():
                for r in range(rows):
                    priv[r, :, start : start + columns - whole] = tail[r]

        def each_copy(n, i, act):
            if i < lines - 1:
                act(copy_of(n, i))
                return
            ends = begins(piece_of(n, i), core, piece)[0] + WINDOW > columns

            @pl.when(ends)
            def _():
                act(copy_of(n, i, WIDE))

            @pl.when(jnp.logical_not(ends))
            def _():
                act(copy_of(n, i))

        pairs = ((owner_there, owner), (partner_there, partner), (counts_there, counts))
        little = [
            pltpu.make_async_copy(there, here, small.at[i]) for i, (there, here) in enumerate(pairs)
        ]
        for copy in little:
            copy.start()
        tail_copy.start()
        for i in range(lines):
            each_copy(0, i, lambda copy: copy.start())

        def widen(i, earlier):
            for n in range(beside):
                j = beside * i + (mine ^ AROUND[n])
                value = own[j].astype(jnp.float32)
                if n == 0:
                    widen_into(pub, i, value, positions)
                shift = begins(j, core, piece)[1]
                free = jnp.where(shift == 0, LANES - 1, shift - 1)
                tile = jnp.where(shift == 0, tile_of(value, TILES - 1), tile_of(value, 0))
                free = jnp.where(j < chip, free, LANES)
                earlier = earlier + jnp.where(lane == free, tile, 0.0)
            return earlier

        earlier = lax.fori_loop(
            0, lines, widen, jnp.zeros((flat, LANES), jnp.float32), unroll=True
        )
        for copy in little:
            copy.wait()
        for t in range(texts):
            here = jnp.where(row == t * positions, earlier, 0.0)
            left[t] = counts[t] - jnp.sum(here).astype(jnp.int32)

        for c in range(2):
            for r in range(rows):
                text = jnp.where(core == c, owner[r], partner[r])
                still = left[text]
                left[text] = still - 1
                at = jnp.where(core == c, r, rows + r)
                plan[at] = text
                plan[2 * rows + at] = jnp.where(still > 0, text, texts)
        acc[texts] = jnp.zeros(acc.shape[1:], jnp.float32)
        held = Rows(plan, priv, swapped, packed=True)
        windows = [(piece_of(0, i), i, storing(out, i), i) for i in range(lines)]
        clear(held, acc, 0, lines)

        def add(entries, first):
            batch = windows[first : first + GROUP]
            edge = strip if first + GROUP == lines else None
            add_rows(held, pub, acc, core, piece, batch, entries, first, edge)

        for first in range(0, lines, GROUP):
            add(range(rows, 2 * rows), first)
        for first in range(0, lines, GROUP):
            for i in range(first, first + GROUP):
                each_copy(0, i, lambda copy: copy.wait())
            if first == 0:
                tail_copy.wait()
            if first + GROUP == lines:
                fill_tail(0)
            add(range(rows), first)
            store_sums(held, acc, core, piece, scale, windows[first : first + GROUP], first)

    return kernel


def near_kernel(sizes, scale, piece):
    def kernel(plan, priv, swapped, own, out_1, out_2, pub, acc, strip):
        texts = pub.shape[0]
        lines, beside = sizes
        chip, core = place_of(sizes)
        mine = lax.axis_index("ref_1")
        held = Rows(plan, priv, swapped)
        acc[texts] = jnp.zeros(acc.shape[1:], jnp.float32)
        step = GROUP // 2

        def some(first, strip=None):
            windows = []
            for k in range(step):
                i = first + k
                for n, out in ((1, out_1), (2, out_2)):
                    j = beside * i + (mine ^ AROUND[n])
                    place = 2 * k + n - 1
                    widen_into(pub, place, own[j].astype(jnp.float32), held.positions)
                    windows.append((j, place, storing(out, i), 0))
            sum_windows(held, pub, acc, core, piece, scale, windows, strip)

        def looped(b, carry):
            some(b * step)
            return carry

        lax.fori_loop(0, lines // step - 1, looped, 0)
        some(lines - step, strip)

    return kernel


def own_kernel(sizes, scale, piece):
    def kernel(
        public, noise, counts, tokens, plan, priv, swapped, own,
        out, base, chosen, level, factor,
        pub, acc, strip, scratch,
    ):
        texts = pub.shape[0]
        lines, beside = sizes
        chip, core = place_of(sizes)
        mine = lax.axis_index("ref_1")
        held = Rows(plan, priv, swapped)
        for i in range(lines):
            widen_into(pub, i, own[beside * i + mine].astype(jnp.float32), held.positions)
        acc[texts] = jnp.zeros(acc.shape[1:], jnp.float32)
        for first in range(0, lines, GROUP):
            windows = [
                (beside * i + mine, i, storing(out, i), 0)
                for i in range(first, first + GROUP)
            ]
            last = first + GROUP == lines
            sum_windows(held, pub, acc, core, piece, scale, windows, strip if last else None)
        prepare(sizes, scale / beside, public, noise, counts, tokens, scratch, base, chosen, level, factor)

    return kernel


def join_kernel(a, b, c, d, out):
    for i in range(out.shape[0]):
        total = (a[i].astype(jnp.int32) + b[i].astype(jnp.int32)) + (
            c[i].astype(jnp.int32) + d[i].astype(jnp.int32)
        )
        total = jnp.round(total.astype(jnp.float32) * 0.25)
        out[i] = total.astype(jnp.int32).astype(jnp.int16)


def prepare(sizes, scale_of, public, noise, counts, tokens, scratch, base, chosen, level, factor):
    texts, positions, piece = public.shape
    square = (texts * positions, LANES)
    lane = lanes_of(square)
    row = lax.broadcasted_iota(jnp.int32, square, 0)
    shift = turn_of(sizes, piece)
    chip, core = place_of(sizes)
    chips = sizes[0] * sizes[1]
    first = (lax.axis_index("voc") * 2 * chips + 2 * chip + core) * piece
    number = jnp.ones(square, jnp.float32)
    token = jnp.zeros(square, jnp.int32)
    for t in range(texts):
        number = jnp.where(inside_text(row, t, positions), counts[t].astype(jnp.float32), number)
        for p in range(positions):
            token = jnp.where(row == t * positions + p, tokens[t, p] - first, token)
    factor[...] = (1.0 / scale_of) / (clip_bound * jnp.sqrt(number))
    public_tiles = turned(rows_of(public, scratch.at[0]), shift, lane)
    noise_tiles = turned(rows_of(noise, scratch.at[1]), shift, lane)
    top = jnp.full(square, -jnp.inf, jnp.float32)
    for k in range(TILES):
        column = column_of(lane, k, shift)
        inside = column < piece
        part = slice(k * LANES, (k + 1) * LANES)
        top = jnp.maximum(top, jnp.where(inside, public_tiles[k], -jnp.inf))
        base[:, part] = jnp.where(inside, public_tiles[k] + noise_tiles[k], -jnp.inf)
        chosen[:, part] = jnp.where(inside & (column == token), 1.0, 0.0)
    level[...] = jnp.broadcast_to(jnp.max(top, axis=1, keepdims=True), square)


def finish_kernel(parts, base, chosen, level, scale, combined, stats):
    flat = base.shape[0]
    square = (flat, LANES)
    lane = lanes_of(square)
    row = lax.broadcasted_iota(jnp.int32, square, 0)
    terms = jnp.zeros(square, jnp.float32)
    picked = jnp.zeros(square, jnp.float32)
    for k in range(TILES):
        part = slice(k * LANES, (k + 1) * LANES)
        total = parts[0, :, part].astype(jnp.int32)
        for j in range(1, parts.shape[0]):
            total = total + parts[j, :, part].astype(jnp.int32)
        tile = base[:, part] + total.astype(jnp.float32) * scale[...]
        combined[:, part] = tile
        terms = terms + jnp.exp(tile - level[...])
        picked = picked + jnp.where(chosen[:, part] > 0.0, tile, 0.0)
    terms = jnp.sum(terms, axis=1, keepdims=True)
    picked = jnp.sum(picked, axis=1, keepdims=True)
    spread = jnp.where(lane == row, terms, 0.0)
    spread = spread + jnp.where(lane == row + flat, picked, 0.0)
    spread = spread + jnp.where(lane == row + 2 * flat, level[...], 0.0)
    stats[...] = jnp.sum(spread, axis=0, keepdims=True)


def last_kernel(sizes):
    def kernel(everyone, combined, logprobs, target, natural):
        texts, positions, piece = logprobs.shape
        flat = texts * positions
        values = everyone[...]
        lane = lanes_of((1, LANES))
        level = jnp.max(values, axis=0, keepdims=True)
        weight = pltpu.roll(jnp.exp(values - level), LANES - 2 * flat, 1)
        total = jnp.sum(values * weight, axis=0, keepdims=True)
        picked = pltpu.roll(jnp.sum(values, axis=0, keepdims=True), LANES - flat, 1)
        level = pltpu.roll(level, LANES - 2 * flat, 1)
        own = lane < flat
        lse = jnp.where(own, level + jnp.log(jnp.where(own, total, 1.0)), 0.0)
        picked = picked - lse
        square = (flat, LANES)
        mine = lanes_of(square) == lax.broadcasted_iota(jnp.int32, square, 0)
        column = jnp.sum(jnp.where(mine, jnp.broadcast_to(lse, square), 0.0), axis=1, keepdims=True)
        tiles = [combined[:, k * LANES : (k + 1) * LANES] - column for k in range(TILES)]
        for k, tile in enumerate(turned_back(tiles, turn_of(sizes, piece), lanes_of(square))):
            natural[:, k * LANES : (k + 1) * LANES] = tile
        shifted = natural[:, :piece]
        for t in range(texts):
            logprobs[t] = shifted[t * positions : (t + 1) * positions]
        for t in range(texts):
            turn = picked if t == 0 else pltpu.roll(picked, LANES - t * positions, 1)
            target[t : t + 1, :] = turn[:, :positions]

    return kernel


def body(private_logits, public_logits, noise, owner, counts, tokens):
    texts, positions, piece = public_logits.shape
    rows, _, columns = private_logits.shape
    flat = texts * positions
    sizes = (lax.axis_size("ref_0"), lax.axis_size("ref_1"))
    chips = sizes[0] * sizes[1]
    swap = [(0, 1), (1, 0)]
    scale = float(32767 // (2 * rows * int(clip_bound)))
    square = pltpu.VMEM((flat, LANES), jnp.float32)
    long = pltpu.VMEM((flat, WIDE), jnp.float32)
    owner_there, counts_there, tokens_there, public_there, noise_there, private_there = (
        pltpu.with_memory_space_constraint(x, pltpu.HBM)
        for x in (owner, counts, tokens, public_logits, noise, private_logits)
    )

    partner = lax.ppermute(owner, CORE, swap)
    one, number = pl.pallas_call(
        turn_kernel(sizes),
        out_shape=(long, square),
        in_specs=[VMEM, SMEM],
        out_specs=(VMEM, VMEM),
        scratch_shapes=[pltpu.VMEM((flat, WIDE), jnp.float32)],
        compiler_params=PARAMS,
        name="turn",
    )(public_there, owner_there)
    partner, private_later, one = lax.optimization_barrier((partner, private_logits, one))
    swapped = lax.ppermute(private_later, CORE, swap)
    packed = pl.pallas_call(
        mark_kernel(sizes, piece, positions),
        out_shape=pltpu.VMEM((chips, flat, WIDE), jnp.bfloat16),
        in_specs=[VMEM, VMEM, VMEM],
        out_specs=VMEM,
        compiler_params=PARAMS,
        name="mark",
    )(one, number, partner.reshape(1, rows))
    own = lax.all_to_all(packed, CHIP, split_axis=0, concat_axis=0, tiled=True)
    swapped, own, partner = (
        pltpu.with_memory_space_constraint(x, pltpu.VMEM) for x in (swapped, own, partner)
    )
    lines, beside = sizes
    line_sums = pltpu.VMEM((lines, flat, WIDE), jnp.int16)
    windows = lines * WINDOW
    sums_scratch = pltpu.VMEM((texts + 1, positions, GROUP * WINDOW), jnp.float32)
    strip = pltpu.VMEM((2 * rows, positions, LANES), private_logits.dtype)

    def beyond(x, m):
        return lax.ppermute(x, "ref_1", [(k, k ^ m) for k in range(beside)])

    private_here = pltpu.with_memory_space_constraint(private_logits, pltpu.VMEM)
    far, plan = pl.pallas_call(
        far_kernel(sizes, scale, piece),
        out_shape=(
            line_sums,
            jax.ShapeDtypeStruct((4 * rows,), jnp.int32),
        ),
        in_specs=[HBM, VMEM, HBM, HBM, VMEM, VMEM],
        out_specs=(VMEM, SMEM),
        scratch_shapes=[
            pltpu.VMEM((rows, positions, windows), private_logits.dtype),
            pltpu.VMEM((texts, positions, windows), jnp.float32),
            pltpu.VMEM((texts + 1, positions, windows), jnp.float32),
            strip,
            pltpu.VMEM((rows, positions, columns % LANES), private_logits.dtype),
            pltpu.SMEM((rows,), jnp.int32),
            pltpu.SMEM((rows,), jnp.int32),
            pltpu.SMEM((texts,), jnp.int32),
            pltpu.SMEM((texts,), jnp.int32),
            pltpu.SemaphoreType.DMA((lines,)),
            pltpu.SemaphoreType.DMA((4,)),
        ],
        compiler_params=PARAMS,
        name="far_sums",
    )(owner_there, partner, counts_there, private_there, swapped, own)
    got = [beyond(far, AROUND[0])]
    near = pl.pallas_call(
        near_kernel(sizes, scale, piece),
        out_shape=(line_sums, line_sums),
        in_specs=[SMEM, VMEM, VMEM, VMEM],
        out_specs=(VMEM, VMEM),
        scratch_shapes=[
            pltpu.VMEM((texts, positions, GROUP * WINDOW), jnp.float32),
            sums_scratch,
            strip,
        ],
        compiler_params=PARAMS,
        name="near_sums",
    )(plan, private_here, swapped, own)
    got += [beyond(x, m) for x, m in zip(near, AROUND[1:])]
    near_done, own_later = lax.optimization_barrier((near[0], own))
    line, base, chosen, level, factor = pl.pallas_call(
        own_kernel(sizes, scale, piece),
        out_shape=(line_sums, long, long, square, square),
        in_specs=[VMEM, VMEM, SMEM, SMEM, SMEM, VMEM, VMEM, VMEM],
        out_specs=(VMEM,) * 5,
        scratch_shapes=[
            pltpu.VMEM((texts, positions, windows), jnp.float32),
            sums_scratch,
            strip,
            pltpu.VMEM((2, flat, WIDE), jnp.float32),
        ],
        compiler_params=PARAMS,
        name="own_sums",
    )(public_there, noise_there, counts_there, tokens_there, plan, private_here, swapped, own_later)
    joined = pl.pallas_call(
        join_kernel,
        out_shape=line_sums,
        in_specs=[VMEM] * 4,
        out_specs=VMEM,
        compiler_params=PARAMS,
        name="join",
    )(line, *[pltpu.with_memory_space_constraint(x, pltpu.VMEM) for x in got])
    parts = lax.all_to_all(joined, "ref_0", split_axis=0, concat_axis=0, tiled=True)
    parts = pltpu.with_memory_space_constraint(parts, pltpu.VMEM)
    combined, stats = pl.pallas_call(
        finish_kernel,
        out_shape=(long, pltpu.VMEM((1, LANES), jnp.float32)),
        in_specs=[VMEM] * 5,
        out_specs=(VMEM, VMEM),
        compiler_params=PARAMS,
        name="finish",
    )(parts, base, chosen, level, factor)

    devices = lax.axis_size(REF_VOC)
    everyone = lax.all_to_all(
        jnp.broadcast_to(stats, (devices, 1, LANES)), REF_VOC, split_axis=0, concat_axis=0, tiled=True
    ).reshape(devices, LANES)
    return pl.pallas_call(
        last_kernel(sizes),
        out_shape=(
            jax.ShapeDtypeStruct(public_logits.shape, jnp.float32),
            jax.ShapeDtypeStruct((texts, positions), jnp.float32),
        ),
        in_specs=[VMEM, VMEM],
        out_specs=(VMEM, VMEM),
        scratch_shapes=[pltpu.VMEM((flat, WIDE), jnp.float32)],
        compiler_params=PARAMS,
        name="last",
    )(pltpu.with_memory_space_constraint(everyone, pltpu.VMEM), combined)


def solution(mesh):
    finer = Mesh(
        mesh.devices.reshape(8, 4, 2, mesh.shape["voc"]), ("ref_0", "ref_1", "ref_2", "voc")
    )
    placed = (P(REF, None, "voc"), P(None, None, VOC_REF), P(None, None, VOC_REF), P(REF), P(), P())
    return jax.shard_map(
        body, mesh=finer, in_specs=placed, out_specs=(P(None, None, VOC_REF), P()), check_vma=False
    )
```

```python
import jax
import jax.numpy as jnp
from jax import lax
from jax.experimental import pallas as pl
from jax.experimental.pallas import tpu as pltpu
from jax.sharding import Mesh
from jax.sharding import PartitionSpec as P

REF_VOC = ("ref_0", "ref_1", "ref_2", "voc")
REF = ("ref_0", "ref_1", "ref_2")
CHIP = ("ref_0", "ref_1")
CORE = "ref_2"
VOC_REF = ("voc", "ref_0", "ref_1", "ref_2")

clip_bound = 2.0

LANES = 128
WIDE = 512
TILES = WIDE // LANES
WINDOW = WIDE + LANES
GROUP = 4
AROUND = (2, 1, 3, 0)

PARAMS = pltpu.CompilerParams(vmem_limit_bytes=16 << 20)
SMEM = pl.BlockSpec(memory_space=pltpu.SMEM)
VMEM = pl.BlockSpec(memory_space=pltpu.VMEM)
HBM = pl.BlockSpec(memory_space=pltpu.HBM)


def tile_of(x, k):
    return x[:, k * LANES : (k + 1) * LANES]


def turned(tiles, shift, lane):
    spun = [pltpu.roll(tile, shift, 1) for tile in tiles]
    return [jnp.where(lane >= shift, spun[k], spun[k - 1]) for k in range(TILES)]


def turned_back(tiles, shift, lane):
    back = LANES - shift
    spun = [pltpu.roll(tile, back, 1) for tile in tiles]
    return [jnp.where(lane < back, spun[k], spun[(k + 1) % TILES]) for k in range(TILES)]


def lanes_of(shape):
    return lax.broadcasted_iota(jnp.int32, shape, len(shape) - 1)


def rows_of(array, scratch):
    texts, positions, piece = array.shape
    for t in range(texts):
        part = slice(t * positions, (t + 1) * positions)
        scratch[part, :piece] = array[t].astype(jnp.float32)
    values = scratch[...]
    lane = lanes_of((texts * positions, LANES))
    return [
        jnp.where(lane + k * LANES < piece, tile_of(values, k), 0.0) for k in range(TILES)
    ]


def column_of(lane, k, shift):
    return (lane + k * LANES - shift) & (WIDE - 1)


def place_of(sizes):
    chip = lax.axis_index("ref_0") * sizes[1] + lax.axis_index("ref_1")
    return chip, lax.axis_index("ref_2")


def turn_of(sizes, piece):
    chip, core = place_of(sizes)
    return ((2 * chip + core) * piece) & (LANES - 1)


def inside_text(row, t, positions):
    return (row >= t * positions) & (row < (t + 1) * positions)


def turn_kernel(sizes):
    def kernel(public, near, out, number, scratch):
        texts, positions, piece = public.shape
        square = number.shape
        lane = lanes_of(square)
        row = lax.broadcasted_iota(jnp.int32, square, 0)
        shift = turn_of(sizes, piece)
        for k, tile in enumerate(turned(rows_of(public, scratch), shift, lane)):
            out[:, k * LANES : (k + 1) * LANES] = tile
        many = jnp.zeros(square, jnp.float32)
        for t in range(texts):
            held = jnp.int32(0)
            for r in range(near.shape[0]):
                held += jnp.where(near[r] == t, 1, 0)
            many = jnp.where(inside_text(row, t, positions), held.astype(jnp.float32), many)
        number[...] = many

    return kernel


def mark_kernel(sizes, piece, positions):
    def kernel(one, number, far, out):
        square = number.shape
        row = lax.broadcasted_iota(jnp.int32, square, 0)
        lane = lanes_of(square)
        shift = turn_of(sizes, piece)
        many = number[...]
        for t in range(square[0] // positions):
            held = jnp.sum(jnp.where(far[...] == t, 1.0, 0.0), axis=1, keepdims=True)
            held = jnp.broadcast_to(held, square)
            many = many + jnp.where(inside_text(row, t, positions), held, 0.0)
        for k in range(TILES):
            tile = one[:, k * LANES : (k + 1) * LANES]
            tile = jnp.where(column_of(lane, k, shift) < piece, tile, many)
            tile = tile.astype(out.dtype)
            for j in range(out.shape[0]):
                out[j, :, k * LANES : (k + 1) * LANES] = tile

    return kernel


class Rows:
    def __init__(self, plan, priv, swapped, packed=False):
        rows, self.positions, self.columns = swapped.shape
        self.entries = []
        for h, held in enumerate((priv, swapped)):
            for r in range(rows):
                at = h * rows + r
                self.entries.append((held, r, plan[at], plan[2 * rows + at], packed and h == 0))


def begins(j, core, piece):
    start = (2 * j + core) * piece
    base = start // LANES * LANES
    return pl.multiple_of(base, LANES), start - base


def widen_into(pub, place, value, positions):
    for t in range(pub.shape[0]):
        part = value[t * positions : (t + 1) * positions]
        pub[t, :, pl.ds(pl.multiple_of(place * WINDOW, LANES), WIDE)] = part
        pub[t, :, pl.ds(pl.multiple_of(place * WINDOW + WIDE, LANES), LANES)] = part[:, :LANES]


def fill_strip(rows, strip, entries):
    last = rows.columns // LANES * LANES
    for e in entries:
        held, r, _, _, packed = rows.entries[e]
        if packed:
            continue
        strip[e] = jnp.zeros(strip.shape[1:], strip.dtype)
        strip[e, :, : rows.columns - last] = held[r, :, last:]


def sum_windows(rows, pub, acc, core, piece, scale, windows, strip=None):
    clear(rows, acc, 0, len(windows))
    add_rows(rows, pub, acc, core, piece, windows, range(len(rows.entries)), 0, strip)
    store_sums(rows, acc, core, piece, scale, windows, 0)


def clear(rows, acc, first, many):
    texts = acc.shape[0] - 1
    acc[:texts, :, first * WINDOW : (first + many) * WINDOW] = jnp.zeros(
        (texts, rows.positions, many * WINDOW), jnp.float32
    )


def add_rows(rows, pub, acc, core, piece, windows, entries, first, strip=None):
    whole = rows.columns // LANES * LANES
    bases = [begins(window[0], core, piece)[0] for window in windows]
    at = [pl.multiple_of(window[1] * WINDOW, LANES) for window in windows]
    packs = [pl.multiple_of(window[3] * WINDOW, LANES) for window in windows]
    if strip is not None:
        fill_strip(rows, strip, entries)
        ends = [base + WINDOW > rows.columns for base in bases]
        edges = [pl.multiple_of(jnp.minimum(base + WIDE, whole - LANES), LANES) for base in bases]
    for e in entries:
        held, r, text, slot, packed = rows.entries[e]
        for g in range(len(windows)):
            size = WINDOW if strip is None or packed else WIDE
            parts = [(0, held[r, :, pl.ds(packs[g] if packed else bases[g], size)])]
            if size == WIDE:
                parts.append((WIDE, jnp.where(ends[g], strip[e], held[r, :, pl.ds(edges[g], LANES)])))
            for offset, value in parts:
                width = value.shape[1]
                beside = pub[text, :, pl.ds(pl.multiple_of(at[g] + offset, LANES), width)]
                value = jnp.clip(value.astype(jnp.float32) - beside, -clip_bound, clip_bound)
                start = (first + g) * WINDOW + offset
                acc[slot, :, start : start + width] = acc[slot, :, start : start + width] + value


def store_sums(rows, acc, core, piece, scale, windows, first):
    texts = acc.shape[0] - 1
    lane = lanes_of((texts * rows.positions, LANES))
    for g, (j, _, store, _) in enumerate(windows):
        shift = begins(j, core, piece)[1]
        tiles = [
            jnp.concatenate(
                [tile_at(acc, t, (first + g) * WINDOW + k * LANES) for t in range(texts)],
                axis=0,
            )
            for k in range(TILES + 1)
        ]
        tiles[0] = jnp.where(lane >= shift, tiles[0], tiles[TILES])
        for k in range(TILES):
            fixed = jnp.round(tiles[k] * scale).astype(jnp.int32).astype(jnp.int16)
            store(slice(k * LANES, (k + 1) * LANES), fixed)


def tile_at(acc, t, start):
    return acc[t, :, start : start + LANES]


def storing(out, index):
    def store(part, value):
        out[index, :, part] = value

    return store


def far_kernel(sizes, scale, piece):
    def kernel(
        owner_there, partner_there, counts_there, source, swapped, own,
        out, plan,
        priv, pub, acc, strip, tail, owner, partner, counts, left, arrived, small,
    ):
        rows, positions, columns = swapped.shape
        texts = pub.shape[0]
        chips, flat, _ = own.shape
        lines, beside = sizes
        chip, core = place_of(sizes)
        mine = lax.axis_index("ref_1")
        lane = lanes_of((flat, LANES))
        row = lax.broadcasted_iota(jnp.int32, (flat, LANES), 0)

        def piece_of(n, i):
            return beside * i + (mine ^ AROUND[n])

        def copy_of(n, i, width=WINDOW):
            start = begins(piece_of(n, i), core, piece)[0]
            place = n * lines + i
            return pltpu.make_async_copy(
                source.at[:, :, pl.ds(start, width)],
                priv.at[:, :, place * WINDOW : place * WINDOW + width],
                arrived.at[place],
            )

        whole = columns // LANES * LANES
        tail_copy = pltpu.make_async_copy(source.at[:, :, whole:], tail, small.at[3])

        def fill_tail(n):
            place = (n + 1) * lines - 1
            ends = begins(piece_of(n, lines - 1), core, piece)[0] + WINDOW > columns
            start = place * WINDOW + WIDE

            @pl.when(ends)
            def _():
                for r in range(rows):
                    priv[r, :, start : start + columns - whole] = tail[r]

        def each_copy(n, i, act):
            if i < lines - 1:
                act(copy_of(n, i))
                return
            ends = begins(piece_of(n, i), core, piece)[0] + WINDOW > columns

            @pl.when(ends)
            def _():
                act(copy_of(n, i, WIDE))

            @pl.when(jnp.logical_not(ends))
            def _():
                act(copy_of(n, i))

        pairs = ((owner_there, owner), (partner_there, partner), (counts_there, counts))
        little = [
            pltpu.make_async_copy(there, here, small.at[i]) for i, (there, here) in enumerate(pairs)
        ]
        for copy in little:
            copy.start()
        tail_copy.start()
        for i in range(lines):
            each_copy(0, i, lambda copy: copy.start())

        def widen(i, earlier):
            for n in range(beside):
                j = beside * i + (mine ^ AROUND[n])
                value = own[j].astype(jnp.float32)
                if n == 0:
                    widen_into(pub, i, value, positions)
                shift = begins(j, core, piece)[1]
                free = jnp.where(shift == 0, LANES - 1, shift - 1)
                tile = jnp.where(shift == 0, tile_of(value, TILES - 1), tile_of(value, 0))
                free = jnp.where(j < chip, free, LANES)
                earlier = earlier + jnp.where(lane == free, tile, 0.0)
            return earlier

        earlier = lax.fori_loop(
            0, lines, widen, jnp.zeros((flat, LANES), jnp.float32), unroll=True
        )
        for copy in little:
            copy.wait()
        for t in range(texts):
            here = jnp.where(row == t * positions, earlier, 0.0)
            left[t] = counts[t] - jnp.sum(here).astype(jnp.int32)

        for c in range(2):
            for r in range(rows):
                text = jnp.where(core == c, owner[r], partner[r])
                still = left[text]
                left[text] = still - 1
                at = jnp.where(core == c, r, rows + r)
                plan[at] = text
                plan[2 * rows + at] = jnp.where(still > 0, text, texts)
        acc[texts] = jnp.zeros(acc.shape[1:], jnp.float32)
        held = Rows(plan, priv, swapped, packed=True)
        windows = [(piece_of(0, i), i, storing(out, i), i) for i in range(lines)]
        clear(held, acc, 0, lines)

        def add(entries, first):
            batch = windows[first : first + GROUP]
            edge = strip if first + GROUP == lines else None
            add_rows(held, pub, acc, core, piece, batch, entries, first, edge)

        for first in range(0, lines, GROUP):
            add(range(rows, 2 * rows), first)
        for first in range(0, lines, GROUP):
            for i in range(first, first + GROUP):
                each_copy(0, i, lambda copy: copy.wait())
            if first == 0:
                tail_copy.wait()
            if first + GROUP == lines:
                fill_tail(0)
            add(range(rows), first)
            store_sums(held, acc, core, piece, scale, windows[first : first + GROUP], first)

    return kernel


def near_kernel(sizes, scale, piece):
    def kernel(plan, priv, swapped, own, out_1, out_2, pub, acc, strip):
        texts = pub.shape[0]
        lines, beside = sizes
        chip, core = place_of(sizes)
        mine = lax.axis_index("ref_1")
        held = Rows(plan, priv, swapped)
        acc[texts] = jnp.zeros(acc.shape[1:], jnp.float32)
        step = GROUP // 2

        def some(first, strip=None):
            windows = []
            for k in range(step):
                i = first + k
                for n, out in ((1, out_1), (2, out_2)):
                    j = beside * i + (mine ^ AROUND[n])
                    place = 2 * k + n - 1
                    widen_into(pub, place, own[j].astype(jnp.float32), held.positions)
                    windows.append((j, place, storing(out, i), 0))
            sum_windows(held, pub, acc, core, piece, scale, windows, strip)

        def looped(b, carry):
            some(b * step)
            return carry

        lax.fori_loop(0, lines // step - 1, looped, 0, unroll=True)
        some(lines - step, strip)

    return kernel


def own_kernel(sizes, scale, piece):
    def kernel(
        public, noise, counts, tokens, plan, priv, swapped, own,
        out, base, chosen, level, factor,
        pub, acc, strip, scratch,
    ):
        texts = pub.shape[0]
        lines, beside = sizes
        chip, core = place_of(sizes)
        mine = lax.axis_index("ref_1")
        held = Rows(plan, priv, swapped)
        for i in range(lines):
            widen_into(pub, i, own[beside * i + mine].astype(jnp.float32), held.positions)
        acc[texts] = jnp.zeros(acc.shape[1:], jnp.float32)
        for first in range(0, lines, GROUP):
            windows = [
                (beside * i + mine, i, storing(out, i), 0)
                for i in range(first, first + GROUP)
            ]
            last = first + GROUP == lines
            sum_windows(held, pub, acc, core, piece, scale, windows, strip if last else None)
        prepare(sizes, scale / beside, public, noise, counts, tokens, scratch, base, chosen, level, factor)

    return kernel


def join_kernel(a, b, c, d, out):
    for i in range(out.shape[0]):
        total = (a[i].astype(jnp.int32) + b[i].astype(jnp.int32)) + (
            c[i].astype(jnp.int32) + d[i].astype(jnp.int32)
        )
        total = jnp.round(total.astype(jnp.float32) * 0.25)
        out[i] = total.astype(jnp.int32).astype(jnp.int16)


def prepare(sizes, scale_of, public, noise, counts, tokens, scratch, base, chosen, level, factor):
    texts, positions, piece = public.shape
    square = (texts * positions, LANES)
    lane = lanes_of(square)
    row = lax.broadcasted_iota(jnp.int32, square, 0)
    shift = turn_of(sizes, piece)
    chip, core = place_of(sizes)
    chips = sizes[0] * sizes[1]
    first = (lax.axis_index("voc") * 2 * chips + 2 * chip + core) * piece
    number = jnp.ones(square, jnp.float32)
    token = jnp.zeros(square, jnp.int32)
    for t in range(texts):
        number = jnp.where(inside_text(row, t, positions), counts[t].astype(jnp.float32), number)
        for p in range(positions):
            token = jnp.where(row == t * positions + p, tokens[t, p] - first, token)
    factor[...] = (1.0 / scale_of) / (clip_bound * jnp.sqrt(number))
    public_tiles = turned(rows_of(public, scratch.at[0]), shift, lane)
    noise_tiles = turned(rows_of(noise, scratch.at[1]), shift, lane)
    top = jnp.full(square, -jnp.inf, jnp.float32)
    for k in range(TILES):
        column = column_of(lane, k, shift)
        inside = column < piece
        part = slice(k * LANES, (k + 1) * LANES)
        top = jnp.maximum(top, jnp.where(inside, public_tiles[k], -jnp.inf))
        base[:, part] = jnp.where(inside, public_tiles[k] + noise_tiles[k], -jnp.inf)
        chosen[:, part] = jnp.where(inside & (column == token), 1.0, 0.0)
    level[...] = jnp.broadcast_to(jnp.max(top, axis=1, keepdims=True), square)


def finish_kernel(parts, base, chosen, level, scale, combined, stats):
    flat = base.shape[0]
    square = (flat, LANES)
    lane = lanes_of(square)
    row = lax.broadcasted_iota(jnp.int32, square, 0)
    terms = jnp.zeros(square, jnp.float32)
    picked = jnp.zeros(square, jnp.float32)
    for k in range(TILES):
        part = slice(k * LANES, (k + 1) * LANES)
        total = parts[0, :, part].astype(jnp.int32)
        for j in range(1, parts.shape[0]):
            total = total + parts[j, :, part].astype(jnp.int32)
        tile = base[:, part] + total.astype(jnp.float32) * scale[...]
        combined[:, part] = tile
        terms = terms + jnp.exp(tile - level[...])
        picked = picked + jnp.where(chosen[:, part] > 0.0, tile, 0.0)
    terms = jnp.sum(terms, axis=1, keepdims=True)
    picked = jnp.sum(picked, axis=1, keepdims=True)
    spread = jnp.where(lane == row, terms, 0.0)
    spread = spread + jnp.where(lane == row + flat, picked, 0.0)
    spread = spread + jnp.where(lane == row + 2 * flat, level[...], 0.0)
    stats[...] = jnp.sum(spread, axis=0, keepdims=True)


def last_kernel(sizes):
    def kernel(everyone, combined, logprobs, target, natural):
        texts, positions, piece = logprobs.shape
        flat = texts * positions
        values = everyone[...]
        lane = lanes_of((1, LANES))
        level = jnp.max(values, axis=0, keepdims=True)
        weight = pltpu.roll(jnp.exp(values - level), LANES - 2 * flat, 1)
        total = jnp.sum(values * weight, axis=0, keepdims=True)
        picked = pltpu.roll(jnp.sum(values, axis=0, keepdims=True), LANES - flat, 1)
        level = pltpu.roll(level, LANES - 2 * flat, 1)
        own = lane < flat
        lse = jnp.where(own, level + jnp.log(jnp.where(own, total, 1.0)), 0.0)
        picked = picked - lse
        square = (flat, LANES)
        mine = lanes_of(square) == lax.broadcasted_iota(jnp.int32, square, 0)
        column = jnp.sum(jnp.where(mine, jnp.broadcast_to(lse, square), 0.0), axis=1, keepdims=True)
        tiles = [combined[:, k * LANES : (k + 1) * LANES] - column for k in range(TILES)]
        for k, tile in enumerate(turned_back(tiles, turn_of(sizes, piece), lanes_of(square))):
            natural[:, k * LANES : (k + 1) * LANES] = tile
        shifted = natural[:, :piece]
        for t in range(texts):
            logprobs[t] = shifted[t * positions : (t + 1) * positions]
        for t in range(texts):
            turn = picked if t == 0 else pltpu.roll(picked, LANES - t * positions, 1)
            target[t : t + 1, :] = turn[:, :positions]

    return kernel


def body(private_logits, public_logits, noise, owner, counts, tokens):
    texts, positions, piece = public_logits.shape
    rows, _, columns = private_logits.shape
    flat = texts * positions
    sizes = (lax.axis_size("ref_0"), lax.axis_size("ref_1"))
    chips = sizes[0] * sizes[1]
    swap = [(0, 1), (1, 0)]
    scale = float(32767 // (2 * rows * int(clip_bound)))
    square = pltpu.VMEM((flat, LANES), jnp.float32)
    long = pltpu.VMEM((flat, WIDE), jnp.float32)
    owner_there, counts_there, tokens_there, public_there, noise_there, private_there = (
        pltpu.with_memory_space_constraint(x, pltpu.HBM)
        for x in (owner, counts, tokens, public_logits, noise, private_logits)
    )

    partner = lax.ppermute(owner, CORE, swap)
    one, number = pl.pallas_call(
        turn_kernel(sizes),
        out_shape=(long, square),
        in_specs=[VMEM, SMEM],
        out_specs=(VMEM, VMEM),
        scratch_shapes=[pltpu.VMEM((flat, WIDE), jnp.float32)],
        compiler_params=PARAMS,
        name="turn",
    )(public_there, owner_there)
    partner, private_later, one = lax.optimization_barrier((partner, private_logits, one))
    swapped = lax.ppermute(private_later, CORE, swap)
    packed = pl.pallas_call(
        mark_kernel(sizes, piece, positions),
        out_shape=pltpu.VMEM((chips, flat, WIDE), jnp.bfloat16),
        in_specs=[VMEM, VMEM, VMEM],
        out_specs=VMEM,
        compiler_params=PARAMS,
        name="mark",
    )(one, number, partner.reshape(1, rows))
    own = lax.all_to_all(packed, CHIP, split_axis=0, concat_axis=0, tiled=True)
    swapped, own, partner = (
        pltpu.with_memory_space_constraint(x, pltpu.VMEM) for x in (swapped, own, partner)
    )
    lines, beside = sizes
    line_sums = pltpu.VMEM((lines, flat, WIDE), jnp.int16)
    windows = lines * WINDOW
    sums_scratch = pltpu.VMEM((texts + 1, positions, GROUP * WINDOW), jnp.float32)
    strip = pltpu.VMEM((2 * rows, positions, LANES), private_logits.dtype)

    def beyond(x, m):
        return lax.ppermute(x, "ref_1", [(k, k ^ m) for k in range(beside)])

    private_here = pltpu.with_memory_space_constraint(private_logits, pltpu.VMEM)
    far, plan = pl.pallas_call(
        far_kernel(sizes, scale, piece),
        out_shape=(
            line_sums,
            jax.ShapeDtypeStruct((4 * rows,), jnp.int32),
        ),
        in_specs=[HBM, VMEM, HBM, HBM, VMEM, VMEM],
        out_specs=(VMEM, SMEM),
        scratch_shapes=[
            pltpu.VMEM((rows, positions, windows), private_logits.dtype),
            pltpu.VMEM((texts, positions, windows), jnp.float32),
            pltpu.VMEM((texts + 1, positions, windows), jnp.float32),
            strip,
            pltpu.VMEM((rows, positions, columns % LANES), private_logits.dtype),
            pltpu.SMEM((rows,), jnp.int32),
            pltpu.SMEM((rows,), jnp.int32),
            pltpu.SMEM((texts,), jnp.int32),
            pltpu.SMEM((texts,), jnp.int32),
            pltpu.SemaphoreType.DMA((lines,)),
            pltpu.SemaphoreType.DMA((4,)),
        ],
        compiler_params=PARAMS,
        name="far_sums",
    )(owner_there, partner, counts_there, private_there, swapped, own)
    got = [beyond(far, AROUND[0])]
    near = pl.pallas_call(
        near_kernel(sizes, scale, piece),
        out_shape=(line_sums, line_sums),
        in_specs=[SMEM, VMEM, VMEM, VMEM],
        out_specs=(VMEM, VMEM),
        scratch_shapes=[
            pltpu.VMEM((texts, positions, GROUP * WINDOW), jnp.float32),
            sums_scratch,
            strip,
        ],
        compiler_params=PARAMS,
        name="near_sums",
    )(plan, private_here, swapped, own)
    got += [beyond(x, m) for x, m in zip(near, AROUND[1:])]
    near_done, own_later = lax.optimization_barrier((near[0], own))
    line, base, chosen, level, factor = pl.pallas_call(
        own_kernel(sizes, scale, piece),
        out_shape=(line_sums, long, long, square, square),
        in_specs=[VMEM, VMEM, SMEM, SMEM, SMEM, VMEM, VMEM, VMEM],
        out_specs=(VMEM,) * 5,
        scratch_shapes=[
            pltpu.VMEM((texts, positions, windows), jnp.float32),
            sums_scratch,
            strip,
            pltpu.VMEM((2, flat, WIDE), jnp.float32),
        ],
        compiler_params=PARAMS,
        name="own_sums",
    )(public_there, noise_there, counts_there, tokens_there, plan, private_here, swapped, own_later)
    joined = pl.pallas_call(
        join_kernel,
        out_shape=line_sums,
        in_specs=[VMEM] * 4,
        out_specs=VMEM,
        compiler_params=PARAMS,
        name="join",
    )(line, *[pltpu.with_memory_space_constraint(x, pltpu.VMEM) for x in got])
    parts = lax.all_to_all(joined, "ref_0", split_axis=0, concat_axis=0, tiled=True)
    parts = pltpu.with_memory_space_constraint(parts, pltpu.VMEM)
    combined, stats = pl.pallas_call(
        finish_kernel,
        out_shape=(long, pltpu.VMEM((1, LANES), jnp.float32)),
        in_specs=[VMEM] * 5,
        out_specs=(VMEM, VMEM),
        compiler_params=PARAMS,
        name="finish",
    )(parts, base, chosen, level, factor)

    devices = lax.axis_size(REF_VOC)
    everyone = lax.all_to_all(
        jnp.broadcast_to(stats, (devices, 1, LANES)), REF_VOC, split_axis=0, concat_axis=0, tiled=True
    ).reshape(devices, LANES)
    return pl.pallas_call(
        last_kernel(sizes),
        out_shape=(
            jax.ShapeDtypeStruct(public_logits.shape, jnp.float32),
            jax.ShapeDtypeStruct((texts, positions), jnp.float32),
        ),
        in_specs=[VMEM, VMEM],
        out_specs=(VMEM, VMEM),
        scratch_shapes=[pltpu.VMEM((flat, WIDE), jnp.float32)],
        compiler_params=PARAMS,
        name="last",
    )(pltpu.with_memory_space_constraint(everyone, pltpu.VMEM), combined)


def solution(mesh):
    finer = Mesh(
        mesh.devices.reshape(8, 4, 2, mesh.shape["voc"]), ("ref_0", "ref_1", "ref_2", "voc")
    )
    placed = (P(REF, None, "voc"), P(None, None, VOC_REF), P(None, None, VOC_REF), P(REF), P(), P())
    return jax.shard_map(
        body, mesh=finer, in_specs=placed, out_specs=(P(None, None, VOC_REF), P()), check_vma=False
    )
```
